256 devices in a mesh: grp: 2 (over core), fsdp: 16 (over y, z_lo), tp: 8 (over x, z_hi).
Axes of the slice: x: 4, y: 4, z: 8 (z_hi: 2, z_lo: 4; z = z_hi * 4 + z_lo), core: 2. Of those that a mesh axis runs over, the one named last changes fastest.
Arguments:
- frames: bfloat16 [2, 4096, 8192], P('grp', 'fsdp'), may hold values from -6 to 6
- rewards: bfloat16 [4096], P('fsdp'), may hold values from -5 to 5
- actions: int32 [2, 4096], P('grp', 'fsdp'), may hold values from 0 to 17
- fractions: int32 [2, 4096, 32], P('grp', 'fsdp'), may hold values from 0 to 63
- episode_shard: int32 [4096, 1], P('fsdp'), may hold values from 0 to 15, as said below
- table: float32 [64], replicated, may hold values from 0.02 to 0.98
- norm_gain: float32 [8192], replicated, may hold values from 0.1 to 1.9
- torso_weight: bfloat16 [8192, 4096], P(('grp', 'fsdp'), 'tp'), may hold values from -0.0625 to 0.0625
- embed_weight: bfloat16 [64, 4096], P(None, 'tp'), may hold values from -0.75 to 0.75
- value_weight: bfloat16 [18, 4096], P(None, 'tp'), may hold values from -0.59765625 to 0.59765625
Outputs:
- torso_grad: float32 [8192, 4096], P(('grp', 'fsdp'), 'tp')
- refreshed_weight: bfloat16 [8192, 4096], P(('grp', 'fsdp', 'tp'))
The draws below stay inside these ranges and needn't reach their ends.
Inputs may be any that keep to these rules, and one draw needn't show every extreme that they name: `episode_shard`: of the rows of one index of fsdp, at most 24 belong to one learner shard, and in every such block some learner shard gets exactly 24; every learner shard gets at least one row from every block.
All inputs are finite; a program needn't handle non-finite values.
Results may differ from the reference program's by a relative error of at most 0.0075.
Values may be sent and summed in bfloat16 or wider, within the bound.
No kernel may reach another device: no remote copies, remote signals or barrier semaphores. Data moves between devices by JAX's collectives and lax.ppermute only.
A program may use at most 64 MiB of HBM per device.

```python
import jax
import jax.numpy as jnp
from jax import lax

D = 8192
H = 4096
ACTIONS = 18
COSINES = 64
FRACS = 64
SAMPLES = 32
ROWS_DEV = 256
ROWS = 4096
N_FSDP = 16


def draw_episode_shard(key, part):
    mean_rows = ROWS_DEV // N_FSDP
    half_rows = mean_rows // 2
    pair_count = N_FSDP // 2
    shard_ids = jnp.arange(N_FSDP, dtype=jnp.int32)
    inner = jnp.minimum(shard_ids, N_FSDP - 1 - shard_ids)
    spread = half_rows * (pair_count - inner) // pair_count
    profile = jnp.where(shard_ids < pair_count, mean_rows - spread, mean_rows + spread).astype(jnp.int32)

    def one_block(block_id):
        order_key = jax.random.fold_in(key, 7 * block_id + 1)
        shuffle_key = jax.random.fold_in(key, 7 * block_id + 2)
        perm = jax.random.permutation(order_key, N_FSDP)
        counts = profile[perm]
        bounds = jnp.cumsum(counts).astype(jnp.int32)
        places = jnp.arange(ROWS_DEV, dtype=jnp.int32)
        owner = jnp.sum((places[:, None] >= bounds[None, :]).astype(jnp.int32), axis=1).astype(jnp.int32)
        shuffle = jax.random.permutation(shuffle_key, ROWS_DEV)
        return owner[shuffle]
    blocks = jax.vmap(one_block)(jnp.arange(N_FSDP, dtype=jnp.int32))
    return blocks.reshape(ROWS, 1).astype(jnp.int32)


def touch_ends(array, rng, smallest, top_value):
    shape = array.shape
    spot = [jax.random.randint(jax.random.fold_in(rng, axis), (), 0, shape[axis]) for axis in range(len(shape))]
    array = array.at[tuple(spot)].set(smallest)
    longest = shape.index(max(shape))
    spot[longest] = (spot[longest] + 1) % shape[longest]
    return array.at[tuple(spot)].set(top_value)


def level_of(key, extent, shards, smallest, largest):
    factor_of, own = 1.0, jax.random.fold_in(key, 6)
    for position, parts in shards:
        heights = jnp.exp(jax.random.uniform(jax.random.fold_in(own, position), (parts,), jnp.float32, smallest / len(shards), largest / len(shards)))
        factor_of = factor_of * jnp.repeat(heights, extent[position] // parts).reshape([-1 if axis == position else 1 for axis in range(len(extent))])
    return factor_of


def bell_draw(stream_key, dims, width, limit, pieces=(), kind=jnp.bfloat16):
    drawn = jax.random.normal(stream_key, dims, jnp.float32) * width
    if len(pieces) > 0:
        drawn = level_of(stream_key, dims, pieces, -0.22, 0.18) * drawn
    return jnp.clip(drawn, min=-limit, max=limit).astype(kind)


def setup_inputs(seed: int = 0) -> dict:
    keys = jax.random.split(jax.random.key(seed), 11)
    frames = bell_draw(keys[0], (2, ROWS, D), 1.0, 6.0, ((0, 2), (1, 16)))
    rewards = bell_draw(keys[1], (ROWS,), 1.0, 5.0, ((0, 16),))
    actions = touch_ends(jax.random.randint(keys[2], (2, ROWS), 0, ACTIONS), jax.random.fold_in(keys[2], 1), 0, ACTIONS - 1).astype(jnp.int32)
    fractions = touch_ends(jax.random.randint(keys[3], (2, ROWS, SAMPLES), 0, FRACS), jax.random.fold_in(keys[3], 1), 0, FRACS - 1).astype(jnp.int32)
    episode_shard = draw_episode_shard(jax.random.fold_in(keys[10], 71), 0)
    table = jnp.clip(jax.random.uniform(keys[5], (FRACS,), jnp.float32, 0.02, 0.98), 0.02, 0.98)
    norm_gain = jnp.clip(1.0 + 0.18 * jax.random.normal(keys[6], (D,), jnp.float32), 0.1, 1.9)
    torso_weight = bell_draw(keys[7], (D, H), D ** -0.5, 0.0625, ((0, 32), (1, 8)))
    embed_weight = bell_draw(keys[8], (COSINES, H), COSINES ** -0.5, 0.75, ((1, 8),))
    value_weight = bell_draw(keys[9], (ACTIONS, H), 0.1, 0.59765625, ((1, 8),))
    return {"frames": frames, "rewards": rewards, "actions": actions, "fractions": fractions, "episode_shard": episode_shard, "table": table, "norm_gain": norm_gain, "torso_weight": torso_weight, "embed_weight": embed_weight, "value_weight": value_weight}


def forward_part(frames_part, action_part, fraction_part, norm_gain, torso_weight, value_weight, embedding):
    values = frames_part.astype(jnp.float32)
    mean_square = lax.optimization_barrier(jnp.mean(values * values, axis=-1, keepdims=True))
    normed = (values * lax.rsqrt(mean_square + 1e-05) * norm_gain).astype(jnp.bfloat16)
    preact = jnp.dot(normed, torso_weight, preferred_element_type=jnp.float32)
    choose_mask = (action_part[:, None] == jnp.arange(ACTIONS, dtype=jnp.int32)[None, :]).astype(jnp.bfloat16)
    picked = jnp.dot(choose_mask, value_weight, preferred_element_type=jnp.float32)
    weighted = (jax.nn.silu(preact) * picked).astype(jnp.bfloat16)
    table_values = jnp.dot(weighted, embedding.T, preferred_element_type=jnp.float32)
    selector = (fraction_part[:, :, None] == jnp.arange(FRACS, dtype=jnp.int32)[None, None, :]).astype(jnp.float32)
    quant = jnp.einsum('mj,mtj->mt', table_values, selector, precision=lax.Precision.HIGHEST)
    return (normed, preact, picked, selector, quant)

def reference(frames, rewards, actions, fractions, episode_shard, table, norm_gain, torso_weight, embed_weight, value_weight):
    destination = episode_shard[:, 0]
    onehot = (destination[:, None] == jnp.arange(N_FSDP, dtype=jnp.int32)[None, :]).astype(jnp.float32)
    counts = lax.optimization_barrier(jnp.sum(onehot, axis=0))
    row_weight = jnp.dot(onehot, float(ROWS_DEV) / counts, precision=lax.Precision.HIGHEST)
    cosine = jnp.cos(jnp.pi * jnp.arange(COSINES, dtype=jnp.float32)[None, :] * table[:, None]).astype(jnp.bfloat16)
    embedding = jax.nn.relu(jnp.dot(cosine, embed_weight, preferred_element_type=jnp.float32)).astype(jnp.bfloat16)
    target_out = forward_part(frames[0], actions[0], fractions[0], norm_gain, torso_weight, value_weight, embedding)
    normed, preact, picked, selector, online_quant = forward_part(frames[1], actions[1], fractions[1], norm_gain, torso_weight, value_weight, embedding)
    target_quant = target_out[4]
    levels = jnp.einsum('mtj,j->mt', selector, table, precision=lax.Precision.HIGHEST)
    target_value = rewards.astype(jnp.float32)[:, None] + 0.99 * target_quant
    errors = target_value[:, None, :] - online_quant[:, :, None]
    weight = jnp.abs(levels[:, :, None] - (errors < 0).astype(jnp.float32))
    grad_quant = -row_weight[:, None] * lax.optimization_barrier(jnp.sum(weight * jnp.clip(errors, -1.0, 1.0), axis=-1))
    grad_table = jnp.einsum('mi,mij->mj', grad_quant, selector, precision=lax.Precision.HIGHEST)
    grad_feature = jnp.dot(grad_table, embedding.astype(jnp.float32), precision=lax.Precision.HIGHEST)
    gate_value = jax.nn.sigmoid(preact)
    grad_preact = (grad_feature * picked * gate_value * (1.0 + preact * (1.0 - gate_value))).astype(jnp.bfloat16)
    torso_grad = jnp.dot(normed.T, grad_preact, preferred_element_type=jnp.float32)
    refreshed_weight = (torso_weight.astype(jnp.float32) - 0.01 * torso_grad).astype(jnp.bfloat16)
    return (torso_grad, refreshed_weight)
```

```python
import jax
import jax.numpy as jnp
from jax import lax
from jax.sharding import PartitionSpec as P

ACTIONS = 18
COSINES = 64
FRACS = 64
Z = 4
Y = 4

SWAP = [(0, 1), (1, 0)]


def z_from(step):
    return [(f, (f // Z) * Z + (f % Z - step) % Z) for f in range(Y * Z)]


def y_from(step):
    return [(f, (f - step * Z) % (Y * Z)) for f in range(Y * Z)]


def roll_from(array, start, axis):
    size = array.shape[axis]
    return lax.dynamic_slice_in_dim(jnp.concatenate([array, array], axis), start, size, axis)


def shards(
    frames,
    rewards,
    actions,
    fractions,
    episode_shard,
    table,
    norm_gain,
    torso_weight,
    embed_weight,
    value_weight,
):
    group = lax.axis_index("grp")
    place = lax.axis_index("fsdp")
    shard_total = lax.axis_size("fsdp")
    whole = lax.all_gather(torso_weight, ("grp", "fsdp"), axis=0, tiled=True)
    rows_block = frames.shape[1]
    width = frames.shape[2]
    half = rows_block // 2
    own_rows = group * half
    other_rows = (1 - group) * half

    def swap(array):
        kept = lax.dynamic_slice_in_dim(array, own_rows, half, 0)
        sent = lax.dynamic_slice_in_dim(array, other_rows, half, 0)
        got = lax.ppermute(sent, "grp", SWAP)
        return jnp.where(group == 0, kept, got), jnp.where(group == 0, got, kept)

    with jax.named_scope("rows_swap"):
        target_rows, online_rows = swap(frames[0])
        ints = jnp.concatenate([fractions[0].T, actions[0][None, :]], 0)
        target_ints, online_ints = swap(ints.T)
        ints_all = jnp.concatenate([target_ints, online_ints], 0).T
        fraction_rows = ints_all[:-1]
        action_rows = ints_all[-1]

    def norm(rows):
        values = rows.astype(jnp.float32)
        mean_square = jnp.mean(values * values, axis=-1, keepdims=True)
        return (values * lax.rsqrt(mean_square + 1e-05) * norm_gain).astype(jnp.bfloat16)

    normed_target = norm(target_rows)
    normed_online = norm(online_rows)
    normed = jnp.concatenate([normed_target, normed_online], 0)

    with jax.named_scope("columns_exchange"):
        block = width // (2 * shard_total)
        own_cols = lax.dynamic_slice_in_dim(normed_online, group * (width // 2), width // 2, 1)
        other_cols = lax.dynamic_slice_in_dim(
            normed_online, (1 - group) * (width // 2), width // 2, 1
        )
        pieces = jnp.stack(
            [
                own_cols.reshape(half, shard_total, block),
                other_cols.reshape(half, shard_total, block),
            ],
            2,
        )
        pieces = jnp.transpose(pieces, (1, 0, 2, 3)).reshape(shard_total, half, 2 * block)
        columns = lax.all_to_all(pieces, "fsdp", 0, 0, tiled=True)
        columns = columns.reshape(Y, Z, half, 2 * block)
        columns = roll_from(roll_from(columns, place // Z, 0), place % Z, 1)

    with jax.named_scope("counts"):
        lanes = jnp.arange(shard_total, dtype=jnp.int32)
        onehot = episode_shard[:, :1] == lanes[None, :]
        local_counts = jnp.sum(onehot.astype(jnp.float32), axis=0)
        counts = jnp.sum(
            lax.all_to_all(
                jnp.broadcast_to(local_counts[None, :], (shard_total, shard_total)),
                "fsdp",
                0,
                0,
                tiled=True,
            ),
            axis=0,
        )
        inverse = float(rows_block) / counts
        row_weight = jnp.sum(jnp.where(onehot, inverse[None, :], 0.0), axis=1)
        row_weight = lax.dynamic_slice_in_dim(row_weight, own_rows, half, 0)

    choose_mask = (action_rows[:, None] == jnp.arange(ACTIONS, dtype=jnp.int32)[None, :]).astype(
        jnp.bfloat16
    )
    picked = jnp.dot(choose_mask, value_weight, preferred_element_type=jnp.float32)
    cosine = jnp.cos(
        jnp.pi * jnp.arange(COSINES, dtype=jnp.float32)[None, :] * table[:, None]
    ).astype(jnp.bfloat16)
    embedding = jax.nn.relu(
        jnp.dot(cosine, embed_weight, preferred_element_type=jnp.float32)
    ).astype(jnp.bfloat16)
    ids = jnp.arange(FRACS, dtype=jnp.int32)
    online_fractions = fraction_rows[:, half:]
    online_select = online_fractions[:, None, :] == ids[None, :, None]
    levels = jnp.sum(jnp.where(online_select, table[None, :, None], 0.0), axis=1)
    reward_rows = lax.dynamic_slice_in_dim(rewards, own_rows, half, 0).astype(jnp.float32)

    preact = jnp.dot(normed, whole, preferred_element_type=jnp.float32)
    weighted = (jax.nn.silu(preact) * picked).astype(jnp.bfloat16)
    table_values = lax.dot_general(
        embedding, weighted, (((1,), (1,)), ((), ())), preferred_element_type=jnp.float32
    )
    partial_quant = jnp.sum(
        jnp.where(
            fraction_rows[:, None, :] == ids[None, :, None], table_values[None, :, :], 0.0
        ),
        axis=1,
    )
    with jax.named_scope("quant_sum"):
        tp_total = lax.axis_size("tp")
        quant = jnp.sum(
            lax.all_to_all(
                jnp.broadcast_to(partial_quant[None], (tp_total,) + partial_quant.shape),
                "tp",
                0,
                0,
                tiled=True,
            ),
            axis=0,
        )
    target_quant = quant[:, :half]
    online_quant = quant[:, half:]
    target_value = reward_rows[None, :] + 0.99 * target_quant
    errors = target_value[None, :, :] - online_quant[:, None, :]
    weight = jnp.abs(levels[:, None, :] - (errors < 0).astype(jnp.float32))
    grad_quant = -row_weight[None, :] * jnp.sum(weight * jnp.clip(errors, -1.0, 1.0), axis=1)
    grad_table = jnp.sum(jnp.where(online_select, grad_quant[:, None, :], 0.0), axis=0)
    grad_feature = lax.dot_general(
        grad_table,
        embedding.astype(jnp.float32),
        (((0,), (0,)), ((), ())),
        precision=lax.Precision.HIGHEST,
    )
    online_preact = preact[half:]
    gate_value = jax.nn.sigmoid(online_preact)
    grad_preact = (
        grad_feature
        * picked[half:]
        * gate_value
        * (1.0 + online_preact * (1.0 - gate_value))
    ).astype(jnp.bfloat16)

    with jax.named_scope("grad_gather"):
        quad = jnp.stack(
            [grad_preact] + [lax.ppermute(grad_preact, "fsdp", z_from(k)) for k in range(1, Z)]
        )
        below = lax.ppermute(quad, "fsdp", y_from(1))
        above = lax.ppermute(quad, "fsdp", y_from(3))
        far_low = lax.ppermute(above[: Z // 2], "fsdp", y_from(3))
        far_high = lax.ppermute(below[Z // 2 :], "fsdp", y_from(1))

    def product(cols, grads):
        return lax.dot_general(
            cols.reshape(-1, cols.shape[-1]),
            grads.reshape(-1, grads.shape[-1]),
            (((0,), (0,)), ((), ())),
            preferred_element_type=jnp.float32,
        )

    part = (
        product(columns[0], quad)
        + product(columns[1], below)
        + product(columns[3], above)
        + product(columns[2, : Z // 2], far_low)
        + product(columns[2, Z // 2 :], far_high)
    )
    torso_grad = part[:block] + lax.ppermute(part[block:], "grp", SWAP)
    updated = (torso_weight.astype(jnp.float32) - 0.01 * torso_grad).astype(jnp.bfloat16)
    refreshed_weight = lax.all_to_all(updated, "tp", split_axis=0, concat_axis=1, tiled=True)
    return (torso_grad, refreshed_weight)


def solution(mesh):
    placed = (
        P("grp", "fsdp", None),
        P("fsdp"),
        P("grp", "fsdp"),
        P("grp", "fsdp", None),
        P("fsdp", None),
        P(),
        P(),
        P(("grp", "fsdp"), "tp"),
        P(None, "tp"),
        P(None, "tp"),
    )
    return jax.shard_map(
        shards,
        mesh=mesh,
        in_specs=placed,
        out_specs=(P(("grp", "fsdp"), "tp"), P(("grp", "fsdp", "tp"), None)),
        check_vma=False,
    )
```

```python
import jax
import jax.numpy as jnp
from jax import lax
from jax.sharding import PartitionSpec as P

ACTIONS = 18
COSINES = 64
FRACS = 64
X = 4
Y = 4
Z = 4

SWAP = [(0, 1), (1, 0)]


def z_from(step):
    return [(f, (f // Z) * Z + (f % Z - step) % Z) for f in range(Y * Z)]


def y_from(step):
    return [(f, (f - step * Z) % (Y * Z)) for f in range(Y * Z)]


def x_from(step):
    return [(t, (t - step * 2) % (X * 2)) for t in range(X * 2)]


def roll_from(array, start, axis):
    size = array.shape[axis]
    return lax.dynamic_slice_in_dim(jnp.concatenate([array, array], axis), start, size, axis)


def shards(
    frames,
    rewards,
    actions,
    fractions,
    episode_shard,
    table,
    norm_gain,
    torso_weight,
    embed_weight,
    value_weight,
):
    group = lax.axis_index("grp")
    place = lax.axis_index("fsdp")
    shard_total = lax.axis_size("fsdp")
    whole = lax.all_gather(torso_weight, ("grp", "fsdp"), axis=0, tiled=True)
    rows_block = frames.shape[1]
    width = frames.shape[2]
    half = rows_block // 2
    own_rows = group * half
    other_rows = (1 - group) * half

    def swap(array):
        kept = lax.dynamic_slice_in_dim(array, own_rows, half, 0)
        sent = lax.dynamic_slice_in_dim(array, other_rows, half, 0)
        got = lax.ppermute(sent, "grp", SWAP)
        return jnp.where(group == 0, kept, got), jnp.where(group == 0, got, kept)

    with jax.named_scope("rows_swap"):
        target_rows, online_rows = swap(frames[0])
        ints = jnp.concatenate([fractions[0].T, actions[0][None, :]], 0)
        target_ints, online_ints = swap(ints.T)
        ints_all = jnp.concatenate([target_ints, online_ints], 0).T
        fraction_rows = ints_all[:-1]
        action_rows = ints_all[-1]

    def norm(rows):
        values = rows.astype(jnp.float32)
        mean_square = jnp.mean(values * values, axis=-1, keepdims=True)
        return (values * lax.rsqrt(mean_square + 1e-05) * norm_gain).astype(jnp.bfloat16)

    normed_target = norm(target_rows)
    normed_online = norm(online_rows)
    normed = jnp.concatenate([normed_target, normed_online], 0)

    with jax.named_scope("columns_exchange"):
        block = width // (2 * shard_total)
        strip = half // X
        x_place = lax.axis_index("tp") // 2
        mine = lax.dynamic_slice_in_dim(normed_online, x_place * strip, strip, 0)
        own_cols = lax.dynamic_slice_in_dim(mine, group * (width // 2), width // 2, 1)
        other_cols = lax.dynamic_slice_in_dim(mine, (1 - group) * (width // 2), width // 2, 1)
        pieces = jnp.stack(
            [
                own_cols.reshape(strip, shard_total, block),
                other_cols.reshape(strip, shard_total, block),
            ],
            2,
        )
        pieces = jnp.transpose(pieces, (1, 0, 2, 3)).reshape(shard_total, strip, 2 * block)
        columns = lax.all_to_all(pieces, "fsdp", 0, 0, tiled=True)
        after = lax.ppermute(columns, "tp", x_from(1))
        before = lax.ppermute(columns, "tp", x_from(3))
        far = jnp.concatenate(
            [
                lax.ppermute(after[: shard_total // 2], "tp", x_from(1)),
                lax.ppermute(before[shard_total // 2 :], "tp", x_from(3)),
            ],
            0,
        )
        columns = jnp.stack([columns, after, far, before])
        columns = roll_from(columns, (X - x_place) % X, 0)
        columns = columns.reshape(X, Y, Z, strip, 2 * block)
        columns = roll_from(roll_from(columns, place // Z, 1), place % Z, 2)
        columns = jnp.transpose(columns, (1, 2, 0, 3, 4)).reshape(Y, Z, half, 2 * block)

    with jax.named_scope("counts"):
        lanes = jnp.arange(shard_total, dtype=jnp.int32)
        onehot = episode_shard[:, :1] == lanes[None, :]
        local_counts = jnp.sum(onehot.astype(jnp.float32), axis=0)
        counts = jnp.sum(
            lax.all_to_all(
                jnp.broadcast_to(local_counts[None, :], (shard_total, shard_total)),
                "fsdp",
                0,
                0,
                tiled=True,
            ),
            axis=0,
        )
        inverse = float(rows_block) / counts
        row_weight = jnp.sum(jnp.where(onehot, inverse[None, :], 0.0), axis=1)
        row_weight = lax.dynamic_slice_in_dim(row_weight, own_rows, half, 0)

    choose_mask = (action_rows[:, None] == jnp.arange(ACTIONS, dtype=jnp.int32)[None, :]).astype(
        jnp.bfloat16
    )
    picked = jnp.dot(choose_mask, value_weight, preferred_element_type=jnp.float32)
    cosine = jnp.cos(
        jnp.pi * jnp.arange(COSINES, dtype=jnp.float32)[None, :] * table[:, None]
    ).astype(jnp.bfloat16)
    embedding = jax.nn.relu(
        jnp.dot(cosine, embed_weight, preferred_element_type=jnp.float32)
    ).astype(jnp.bfloat16)
    ids = jnp.arange(FRACS, dtype=jnp.int32)
    online_fractions = fraction_rows[:, half:]
    online_select = online_fractions[:, None, :] == ids[None, :, None]
    levels = jnp.sum(jnp.where(online_select, table[None, :, None], 0.0), axis=1)
    reward_rows = lax.dynamic_slice_in_dim(rewards, own_rows, half, 0).astype(jnp.float32)

    preact = jnp.dot(normed, whole, preferred_element_type=jnp.float32)
    weighted = (jax.nn.silu(preact) * picked).astype(jnp.bfloat16)
    table_values = lax.dot_general(
        embedding, weighted, (((1,), (1,)), ((), ())), preferred_element_type=jnp.float32
    )
    partial_quant = jnp.sum(
        jnp.where(
            fraction_rows[:, None, :] == ids[None, :, None], table_values[None, :, :], 0.0
        ),
        axis=1,
    )
    with jax.named_scope("quant_sum"):
        tp_total = lax.axis_size("tp")
        quant = jnp.sum(
            lax.all_to_all(
                jnp.broadcast_to(partial_quant[None], (tp_total,) + partial_quant.shape),
                "tp",
                0,
                0,
                tiled=True,
            ),
            axis=0,
        )
    target_quant = quant[:, :half]
    online_quant = quant[:, half:]
    target_value = reward_rows[None, :] + 0.99 * target_quant
    errors = target_value[None, :, :] - online_quant[:, None, :]
    weight = jnp.abs(levels[:, None, :] - (errors < 0).astype(jnp.float32))
    grad_quant = -row_weight[None, :] * jnp.sum(weight * jnp.clip(errors, -1.0, 1.0), axis=1)
    grad_table = jnp.sum(jnp.where(online_select, grad_quant[:, None, :], 0.0), axis=0)
    grad_feature = lax.dot_general(
        grad_table,
        embedding.astype(jnp.float32),
        (((0,), (0,)), ((), ())),
        precision=lax.Precision.HIGHEST,
    )
    online_preact = preact[half:]
    gate_value = jax.nn.sigmoid(online_preact)
    grad_preact = (
        grad_feature
        * picked[half:]
        * gate_value
        * (1.0 + online_preact * (1.0 - gate_value))
    ).astype(jnp.bfloat16)

    with jax.named_scope("grad_gather"):
        quad = jnp.stack(
            [grad_preact] + [lax.ppermute(grad_preact, "fsdp", z_from(k)) for k in range(1, Z)]
        )
        below = lax.ppermute(quad, "fsdp", y_from(1))
        above = lax.ppermute(quad, "fsdp", y_from(3))
        far_low = lax.ppermute(above[: Z // 2], "fsdp", y_from(3))
        far_high = lax.ppermute(below[Z // 2 :], "fsdp", y_from(1))

    def product(cols, grads):
        return lax.dot_general(
            cols.reshape(-1, cols.shape[-1]),
            grads.reshape(-1, grads.shape[-1]),
            (((0,), (0,)), ((), ())),
            preferred_element_type=jnp.float32,
        )

    part = (
        product(columns[0], quad)
        + product(columns[1], below)
        + product(columns[3], above)
        + product(columns[2, : Z // 2], far_low)
        + product(columns[2, Z // 2 :], far_high)
    )
    torso_grad = part[:block] + lax.ppermute(part[block:], "grp", SWAP)
    updated = (torso_weight.astype(jnp.float32) - 0.01 * torso_grad).astype(jnp.bfloat16)
    refreshed_weight = lax.all_to_all(updated, "tp", split_axis=0, concat_axis=1, tiled=True)
    return (torso_grad, refreshed_weight)


def solution(mesh):
    placed = (
        P("grp", "fsdp", None),
        P("fsdp"),
        P("grp", "fsdp"),
        P("grp", "fsdp", None),
        P("fsdp", None),
        P(),
        P(),
        P(("grp", "fsdp"), "tp"),
        P(None, "tp"),
        P(None, "tp"),
    )
    return jax.shard_map(
        shards,
        mesh=mesh,
        in_specs=placed,
        out_specs=(P(("grp", "fsdp"), "tp"), P(("grp", "fsdp", "tp"), None)),
        check_vma=False,
    )
```

```python
import jax
import jax.numpy as jnp
from jax import lax
from jax.experimental import pallas as pl
from jax.experimental.pallas import tpu as pltpu
from jax.sharding import PartitionSpec as P

ACTIONS = 18
COSINES = 64
FRACS = 64
X = 4
Y = 4
Z = 4

SWAP = [(0, 1), (1, 0)]


def z_from(step):
    return [(f, (f // Z) * Z + (f % Z - step) % Z) for f in range(Y * Z)]


def y_from(step):
    return [(f, (f - step * Z) % (Y * Z)) for f in range(Y * Z)]


def x_from(step):
    return [(t, (t - step * 2) % (X * 2)) for t in range(X * 2)]


def round_y(block):
    half = block.shape[0] // 2
    below = lax.ppermute(block, "fsdp", y_from(1))
    above = lax.ppermute(block, "fsdp", y_from(3))
    low = lax.ppermute(above[:half], "fsdp", y_from(3))
    high = lax.ppermute(below[half:], "fsdp", y_from(1))
    return below, above, low, high


def preact_kernel(where_ref, own_ref, got_ref, *refs):
    weights = refs[: 5 * Z]
    keep_ref, send_ref, total = refs[5 * Z :]
    group, y, z = where_ref[0], where_ref[1], where_ref[2]
    rows = own_ref.shape[0]
    block = weights[0].shape[0]
    total[...] = jnp.zeros_like(total)
    for step_y in range(Y):
        for step_z in range(Z):
            place = lax.rem(y + step_y, Y) * Z + lax.rem(z + step_z, Z)
            cols = pl.ds(pl.multiple_of(place * block, block), block)
            if step_y == 0:
                weight = weights[step_z][...]
            elif step_y == 2:
                weight = jnp.concatenate(
                    [weights[3 * Z + step_z][...], weights[4 * Z + step_z][...]], 0
                )
            else:
                weight = weights[(1 if step_y == 1 else 2) * Z + step_z][...]
            total[:rows] += jnp.dot(own_ref[:, cols], weight, preferred_element_type=jnp.float32)
            total[rows:] += jnp.dot(got_ref[:, cols], weight, preferred_element_type=jnp.float32)
    half = rows // 2
    other = 1 - group
    for mine, part in ((True, group), (False, other)):
        base = 0 if mine else rows
        out = pl.ds(pl.multiple_of(part * half, half), half)
        keep_ref[out, :] = total[pl.ds(pl.multiple_of(base + group * half, half), half), :]
        send_ref[out, :] = total[pl.ds(pl.multiple_of(base + other * half, half), half), :]


def norm_kernel(where_ref, rows_ref, gain_ref, own_ref, send_ref):
    side = own_ref.shape[1]
    wide = rows_ref[...].astype(jnp.float32)
    scale = lax.rsqrt(jnp.mean(wide * wide, axis=-1, keepdims=True) + 1e-05)
    for part, out_ref in ((where_ref[0], own_ref), (1 - where_ref[0], send_ref)):
        cols = pl.ds(pl.multiple_of(part * side, side), side)
        values = rows_ref[:, cols].astype(jnp.float32)
        out_ref[...] = (values * scale * gain_ref[:, cols]).astype(jnp.bfloat16)


def pieces_kernel(where_ref, own_ref, got_ref, out_ref, held, sems):
    places, strip, block = out_ref.shape[1:]
    half = own_ref.shape[0] // 2

    def fetch(source):
        copies = []
        for k in range(2):
            row = pl.multiple_of(k * half + where_ref[3] * strip, strip)
            copies.append(
                pltpu.make_async_copy(source.at[pl.ds(row, strip), :], held.at[k], sems.at[k])
            )
            copies[-1].start()
        for copy in copies:
            copy.wait()

    @pl.when(where_ref[0] == 1)
    def _():
        fetch(own_ref)

    @pl.when(where_ref[0] == 0)
    def _():
        fetch(got_ref)

    for k in range(2):
        for place in range(places):
            out_ref[k, place] = held[k, :, place * block : (place + 1) * block]


def columns_kernel(where_ref, own_ref, after_ref, before_ref, far_a_ref, far_b_ref, out_ref, held):
    group, y, z, x = where_ref[0], where_ref[1], where_ref[2], where_ref[3]
    other = 1 - group
    strip, block = own_ref.shape[2], own_ref.shape[3]
    span = strip * X

    def body(step, carry):
        place = lax.rem(y + step // Z, Y) * Z + lax.rem(z + lax.rem(step, Z), Z)
        for shift, ref in ((0, own_ref), (1, after_ref), (3, before_ref)):
            rows = pl.ds(pl.multiple_of(lax.rem(x + shift, X) * strip, strip), strip)
            held[rows, :block] = ref[group, place]
            held[rows, block:] = ref[other, place]
        rows = pl.ds(pl.multiple_of(lax.rem(x + 2, X) * strip, strip), strip)
        held[rows, pl.ds(pl.multiple_of(group * block, block), block)] = far_a_ref[place]
        held[rows, pl.ds(pl.multiple_of(other * block, block), block)] = far_b_ref[place]
        out_ref[:, pl.ds(pl.multiple_of(step * span, span), span)] = held[...].T
        return carry

    lax.fori_loop(0, Y * Z, body, 0)


def near_kernel(cols_ref, own_ref, line_ref, b0_ref, b1_ref, a0_ref, a1_ref, out_ref):
    half = own_ref.shape[0]
    span = Z * half
    total = None
    for base, first, rest in (
        (0, own_ref, line_ref),
        (span, b0_ref, b1_ref),
        (3 * span, a0_ref, a1_ref),
    ):
        grads = jnp.concatenate([first[...], rest[...]], 0)
        term = jnp.dot(
            cols_ref[:, base : base + span], grads, preferred_element_type=jnp.float32
        )
        total = term if total is None else total + term
    out_ref[...] = total


def far_kernel(cols_ref, near_ref, l0_ref, h0_ref, l1_ref, h1_ref, own_ref, other_ref):
    grads = jnp.concatenate([l0_ref[...], h0_ref[...], l1_ref[...], h1_ref[...]], 0)
    span = grads.shape[0]
    block = own_ref.shape[0]
    cols = cols_ref[:, 2 * span : 3 * span]
    total = near_ref[...] + jnp.dot(cols, grads, preferred_element_type=jnp.float32)
    own_ref[...] = total[:block]
    other_ref[...] = total[block:]


def shards(
    frames,
    rewards,
    actions,
    fractions,
    episode_shard,
    table,
    norm_gain,
    torso_weight,
    embed_weight,
    value_weight,
):
    group = lax.axis_index("grp")
    place = lax.axis_index("fsdp")
    x_place = lax.axis_index("tp") // 2
    shard_total = lax.axis_size("fsdp")
    where = jnp.stack([group, place // Z, place % Z, x_place]).astype(jnp.int32)
    rows_block = frames.shape[1]
    width = frames.shape[2]
    features = torso_weight.shape[1]
    half = rows_block // 2
    side = width // 2
    block = side // shard_total
    strip = half // X
    own_rows = group * half
    other_rows = (1 - group) * half
    smem = pl.BlockSpec(memory_space=pltpu.SMEM)
    vmem = pl.BlockSpec(memory_space=pltpu.VMEM)

    with jax.named_scope("rows_swap"):
        values = frames[0]
        tile = 32
        normed_own, normed_send = pl.pallas_call(
            norm_kernel,
            grid=(rows_block // tile,),
            out_shape=(jax.ShapeDtypeStruct((rows_block, side), jnp.bfloat16),) * 2,
            in_specs=[
                smem,
                pl.BlockSpec((tile, width), lambda i: (i, 0)),
                pl.BlockSpec((1, width), lambda i: (0, 0)),
            ],
            out_specs=(pl.BlockSpec((tile, side), lambda i: (i, 0)),) * 2,
            compiler_params=pltpu.CompilerParams(vmem_limit_bytes=12 << 20),
            cost_estimate=pl.CostEstimate(
                flops=6 * rows_block * width,
                transcendentals=0,
                bytes_accessed=4 * rows_block * width,
            ),
            name="norm",
        )(where, values, norm_gain[None, :])
    with jax.named_scope("weight_gather"):
        own_weight, normed_send = lax.optimization_barrier((torso_weight, normed_send))
        lines = [own_weight] + [lax.ppermute(own_weight, "fsdp", z_from(k)) for k in range(1, Z)]
        rounds = [round_y(line) for line in lines]
        chunks = lines + [r[k] for k in range(4) for r in rounds]

    with jax.named_scope("rows_swap"):
        normed_got = lax.ppermute(normed_send, "grp", SWAP)
        ints = jnp.concatenate([fractions[0].T, actions[0][None, :]], 0)
        kept = lax.dynamic_slice_in_dim(ints, own_rows, half, 1)
        got = lax.ppermute(lax.dynamic_slice_in_dim(ints, other_rows, half, 1), "grp", SWAP)
        target_ints = jnp.where(group == 0, kept, got)
        online_ints = jnp.where(group == 0, got, kept)
        ints_all = jnp.concatenate([target_ints, online_ints], 1)
        fraction_rows = ints_all[:-1]
        action_rows = ints_all[-1]

    with jax.named_scope("columns_exchange"):

        pieces = pl.pallas_call(
            pieces_kernel,
            out_shape=jax.ShapeDtypeStruct((2, shard_total, strip, block), jnp.bfloat16),
            in_specs=[smem] + [pl.BlockSpec(memory_space=pl.ANY)] * 2,
            out_specs=vmem,
            scratch_shapes=[
                pltpu.VMEM((2, strip, side), jnp.bfloat16),
                pltpu.SemaphoreType.DMA((2,)),
            ],
            compiler_params=pltpu.CompilerParams(vmem_limit_bytes=4 << 20),
            cost_estimate=pl.CostEstimate(
                flops=0, transcendentals=0, bytes_accessed=8 * strip * side
            ),
            name="pieces",
        )(where, normed_own, normed_got)
        pieces = lax.all_to_all(
            pieces.reshape(2 * shard_total, strip, block), ("grp", "fsdp"), 0, 0, tiled=True
        ).reshape(2, shard_total, strip, block)
        after = lax.ppermute(pieces, "tp", x_from(1))
        before = lax.ppermute(pieces, "tp", x_from(3))
        far_a = lax.ppermute(after[0], "tp", x_from(1))
        far_b = lax.ppermute(before[1], "tp", x_from(3))
        columns = pl.pallas_call(
            columns_kernel,
            out_shape=jax.ShapeDtypeStruct((2 * block, shard_total * half), jnp.bfloat16),
            in_specs=[smem] + [vmem] * 5,
            out_specs=vmem,
            scratch_shapes=[pltpu.VMEM((half, 2 * block), jnp.bfloat16)],
            compiler_params=pltpu.CompilerParams(vmem_limit_bytes=8 << 20),
            cost_estimate=pl.CostEstimate(
                flops=0, transcendentals=0, bytes_accessed=8 * shard_total * half * block
            ),
            name="columns",
        )(where, pieces, after, before, far_a, far_b)

    with jax.named_scope("counts"):
        lanes = jnp.arange(shard_total, dtype=jnp.int32)
        onehot = episode_shard[:, :1] == lanes[None, :]
        local_counts = jnp.sum(onehot.astype(jnp.float32), axis=0)
        counts = jnp.sum(
            lax.all_to_all(
                jnp.broadcast_to(local_counts[None, :], (shard_total, shard_total)),
                "fsdp",
                0,
                0,
                tiled=True,
            ),
            axis=0,
        )
        inverse = float(rows_block) / counts
        row_weight = jnp.sum(jnp.where(onehot, inverse[None, :], 0.0), axis=1)
        row_weight = lax.dynamic_slice_in_dim(row_weight, own_rows, half, 0)

    choose_mask = (action_rows[:, None] == jnp.arange(ACTIONS, dtype=jnp.int32)[None, :]).astype(
        jnp.bfloat16
    )
    picked = jnp.dot(choose_mask, value_weight, preferred_element_type=jnp.float32)
    cosine = jnp.cos(
        jnp.pi * jnp.arange(COSINES, dtype=jnp.float32)[None, :] * table[:, None]
    ).astype(jnp.bfloat16)
    embedding = jax.nn.relu(
        jnp.dot(cosine, embed_weight, preferred_element_type=jnp.float32)
    ).astype(jnp.bfloat16)
    ids = jnp.arange(FRACS, dtype=jnp.int32)
    online_fractions = fraction_rows[:, half:]
    online_select = online_fractions[:, None, :] == ids[None, :, None]
    levels = jnp.sum(jnp.where(online_select, table[None, :, None], 0.0), axis=1)
    reward_rows = lax.dynamic_slice_in_dim(rewards, own_rows, half, 0).astype(jnp.float32)

    normed_own, _ = lax.optimization_barrier((normed_own, pieces))
    part_shape = jax.ShapeDtypeStruct((rows_block, features), jnp.float32)
    keep, send = pl.pallas_call(
        preact_kernel,
        out_shape=(part_shape, part_shape),
        in_specs=[smem] + [vmem] * (2 + 5 * Z),
        out_specs=(vmem, vmem),
        scratch_shapes=[pltpu.VMEM((2 * rows_block, features), jnp.float32)],
        compiler_params=pltpu.CompilerParams(vmem_limit_bytes=16 << 20),
        cost_estimate=pl.CostEstimate(
            flops=4 * rows_block * side * features,
            transcendentals=0,
            bytes_accessed=2 * side * features + 4 * side * rows_block + 8 * rows_block * features,
        ),
        name="preact",
    )(where, normed_own, normed_got, *chunks)
    preact = keep + lax.ppermute(send, "grp", SWAP)
    weighted = (jax.nn.silu(preact) * picked).astype(jnp.bfloat16)
    table_values = lax.dot_general(
        embedding, weighted, (((1,), (1,)), ((), ())), preferred_element_type=jnp.float32
    )
    partial_quant = jnp.sum(
        jnp.where(
            fraction_rows[:, None, :] == ids[None, :, None], table_values[None, :, :], 0.0
        ),
        axis=1,
    )
    with jax.named_scope("quant_sum"):
        tp_total = lax.axis_size("tp")
        quant = jnp.sum(
            lax.all_to_all(
                jnp.broadcast_to(partial_quant[None], (tp_total,) + partial_quant.shape),
                "tp",
                0,
                0,
                tiled=True,
            ),
            axis=0,
        )
    quant, _ = lax.optimization_barrier((quant, (after, before)))
    target_quant = quant[:, :half]
    online_quant = quant[:, half:]
    target_value = reward_rows[None, :] + 0.99 * target_quant
    errors = target_value[None, :, :] - online_quant[:, None, :]
    weight = jnp.abs(levels[:, None, :] - (errors < 0).astype(jnp.float32))
    grad_quant = -row_weight[None, :] * jnp.sum(weight * jnp.clip(errors, -1.0, 1.0), axis=1)
    grad_table = jnp.sum(jnp.where(online_select, grad_quant[:, None, :], 0.0), axis=0)
    grad_feature = lax.dot_general(
        grad_table,
        embedding.astype(jnp.float32),
        (((0,), (0,)), ((), ())),
        precision=lax.Precision.HIGHEST,
    )
    online_preact = preact[half:]
    gate_value = jax.nn.sigmoid(online_preact)
    grad_preact = (
        grad_feature
        * picked[half:]
        * gate_value
        * (1.0 + online_preact * (1.0 - gate_value))
    ).astype(jnp.bfloat16)

    with jax.named_scope("grad_gather"):
        first = round_y(grad_preact)
        pieces_z = tuple(lax.ppermute(grad_preact, "fsdp", z_from(k)) for k in range(1, Z))
        pieces_z, _ = lax.optimization_barrier((pieces_z, (first[0], first[1], far_a, far_b)))
        line = jnp.concatenate(pieces_z, 0)
        rest = round_y(line)

    near = pl.pallas_call(
        near_kernel,
        out_shape=jax.ShapeDtypeStruct((2 * block, features), jnp.float32),
        in_specs=[vmem] * 7,
        out_specs=vmem,
        compiler_params=pltpu.CompilerParams(vmem_limit_bytes=12 << 20),
        cost_estimate=pl.CostEstimate(
            flops=12 * Z * half * 2 * block * features // 2,
            transcendentals=0,
            bytes_accessed=6 * Z * half * (2 * block + features),
        ),
        name="near",
    )(columns, grad_preact, line, first[0], rest[0], first[1], rest[1])
    final_shape = jax.ShapeDtypeStruct((block, features), jnp.float32)
    mine, theirs = pl.pallas_call(
        far_kernel,
        out_shape=(final_shape, final_shape),
        in_specs=[vmem] * 6,
        out_specs=(vmem, vmem),
        compiler_params=pltpu.CompilerParams(vmem_limit_bytes=12 << 20),
        cost_estimate=pl.CostEstimate(
            flops=4 * Z * half * block * features,
            transcendentals=0,
            bytes_accessed=2 * Z * half * (2 * block + features) + 16 * block * features,
        ),
        name="far",
    )(columns, near, first[2], first[3], rest[2], rest[3])
    torso_grad = mine + lax.ppermute(theirs, "grp", SWAP)
    updated = (torso_weight.astype(jnp.float32) - 0.01 * torso_grad).astype(jnp.bfloat16)
    refreshed_weight = lax.all_to_all(updated, "tp", split_axis=0, concat_axis=1, tiled=True)
    return (torso_grad, refreshed_weight)


def solution(mesh):
    placed = (
        P("grp", "fsdp", None),
        P("fsdp"),
        P("grp", "fsdp"),
        P("grp", "fsdp", None),
        P("fsdp", None),
        P(),
        P(),
        P(("grp", "fsdp"), "tp"),
        P(None, "tp"),
        P(None, "tp"),
    )
    return jax.shard_map(
        shards,
        mesh=mesh,
        in_specs=placed,
        out_specs=(P(("grp", "fsdp"), "tp"), P(("grp", "fsdp", "tp"), None)),
        check_vma=False,
    )
```

```python
import jax
import jax.numpy as jnp
from jax import lax
from jax.experimental import pallas as pl
from jax.experimental.pallas import tpu as pltpu
from jax.sharding import PartitionSpec as P

ACTIONS = 18
COSINES = 64
FRACS = 64
X = 4
Y = 4
Z = 4


SWAP = [(0, 1), (1, 0)]


def z_from(step):
    return [(f, (f // Z) * Z + (f % Z - step) % Z) for f in range(Y * Z)]


def y_from(step):
    return [(f, (f - step * Z) % (Y * Z)) for f in range(Y * Z)]


def x_from(step):
    return [(t, (t - step * 2) % (X * 2)) for t in range(X * 2)]


def round_y(block, upward):
    below = lax.ppermute(block, "fsdp", y_from(1))
    above = lax.ppermute(block, "fsdp", y_from(3))
    if upward:
        return below, above, lax.ppermute(above, "fsdp", y_from(3))
    return below, above, lax.ppermute(below, "fsdp", y_from(1))


def preact_kernel(where_ref, own_ref, got_ref, *refs):
    weights = refs[: Y * Z]
    keep_ref, send_ref, total, rows_held, held, sems = refs[Y * Z :]
    group, y, z = where_ref[0], where_ref[1], where_ref[2]
    rows = own_ref.shape[0]
    block = weights[0].shape[0]
    order = [(0, k) for k in range(Z)] + [(j, k) for k in range(Z) for j in (1, 3)]
    order += [(2, k) for k in range(Z)]
    copies = []
    for step, (step_y, step_z) in enumerate(order):
        place = lax.rem(y + step_y, Y) * Z + lax.rem(z + step_z, Z)
        cols = pl.ds(pl.multiple_of(place * block, block), block)
        source = weights[step_y * Z + step_z]
        copies.append(
            (
                pltpu.make_async_copy(
                    own_ref.at[:, cols], rows_held.at[step, pl.ds(0, rows)], sems.at[0, step]
                ),
                pltpu.make_async_copy(
                    got_ref.at[:, cols], rows_held.at[step, pl.ds(rows, rows)], sems.at[1, step]
                ),
                pltpu.make_async_copy(source, held.at[step], sems.at[2, step]),
            )
        )
        for copy in copies[-1]:
            copy.start()
    for step in range(len(order)):
        for copy in copies[step]:
            copy.wait()
        term = jnp.dot(rows_held[step], held[step], preferred_element_type=jnp.float32)
        if step == 0:
            total[...] = term
        else:
            total[...] += term
    half = rows // 2
    other = 1 - group
    for base, part in ((0, group), (rows, other)):
        out = pl.ds(pl.multiple_of(part * half, half), half)
        keep_ref[out, :] = total[pl.ds(pl.multiple_of(base + group * half, half), half), :]
        send_ref[out, :] = total[pl.ds(pl.multiple_of(base + other * half, half), half), :]


def norm_kernel(where_ref, rows_ref, gain_ref, own_ref, send_ref):
    side = own_ref.shape[1]
    wide = rows_ref[...].astype(jnp.float32)
    scale = lax.rsqrt(jnp.mean(wide * wide, axis=-1, keepdims=True) + 1e-05)
    for part, out_ref in ((where_ref[0], own_ref), (1 - where_ref[0], send_ref)):
        cols = pl.ds(pl.multiple_of(part * side, side), side)
        values = rows_ref[:, cols].astype(jnp.float32)
        out_ref[...] = (values * scale * gain_ref[:, cols]).astype(jnp.bfloat16)


def pieces_kernel(where_ref, own_ref, got_ref, count_ref, out_ref, held, sems):
    places, _, block = out_ref.shape[1:]
    strip = held.shape[1]
    half = own_ref.shape[0] // 2

    def fetch(source):
        copies = []
        for k in range(2):
            row = pl.multiple_of(k * half + where_ref[3] * strip, strip)
            copies.append(
                pltpu.make_async_copy(source.at[pl.ds(row, strip), :], held.at[k], sems.at[k])
            )
            copies[-1].start()
        for copy in copies:
            copy.wait()

    @pl.when(where_ref[0] == 1)
    def _():
        fetch(own_ref)

    @pl.when(where_ref[0] == 0)
    def _():
        fetch(got_ref)

    for k in range(2):
        for place in range(places):
            out_ref[k, place, :strip] = held[k, :, place * block : (place + 1) * block]
            out_ref[k, place, strip:] = count_ref[...]


def columns_kernel(where_ref, own_ref, after_ref, before_ref, far_a_ref, far_b_ref, out_ref, held):
    group, y, z, x = where_ref[0], where_ref[1], where_ref[2], where_ref[3]
    other = 1 - group
    strip, block = own_ref.shape[2], own_ref.shape[3]
    span = strip * X

    def body(step, carry):
        place = lax.rem(y + step // Z, Y) * Z + lax.rem(z + lax.rem(step, Z), Z)
        for shift, ref in ((0, own_ref), (1, after_ref), (3, before_ref)):
            rows = pl.ds(pl.multiple_of(lax.rem(x + shift, X) * strip, strip), strip)
            held[rows, :block] = ref[group, place]
            held[rows, block:] = ref[other, place]
        rows = pl.ds(pl.multiple_of(lax.rem(x + 2, X) * strip, strip), strip)
        held[rows, pl.ds(pl.multiple_of(group * block, block), block)] = far_a_ref[place]
        held[rows, pl.ds(pl.multiple_of(other * block, block), block)] = far_b_ref[place]
        out_ref[:, pl.ds(pl.multiple_of(step * span, span), span)] = held[...].T
        return carry

    lax.fori_loop(0, Y * Z, body, 0)


def near_kernel(cols_ref, own_ref, line_ref, b0_ref, b1_ref, a0_ref, a1_ref, out_ref):
    half = own_ref.shape[0]
    span = Z * half
    total = None
    for base, first, rest in (
        (0, own_ref, line_ref),
        (span, b0_ref, b1_ref),
        (3 * span, a0_ref, a1_ref),
    ):
        grads = jnp.concatenate([first[...], rest[...]], 0)
        term = jnp.dot(
            cols_ref[:, base : base + span], grads, preferred_element_type=jnp.float32
        )
        total = term if total is None else total + term
    out_ref[...] = total


def far_kernel(cols_ref, near_ref, f0_ref, f1_ref, f2_ref, own_ref, other_ref):
    grads = jnp.concatenate([f0_ref[...], f1_ref[...], f2_ref[...]], 0)
    span = grads.shape[0]
    block = own_ref.shape[0]
    cols = cols_ref[:, 2 * span : 3 * span]
    total = near_ref[...] + jnp.dot(cols, grads, preferred_element_type=jnp.float32)
    own_ref[...] = total[:block]
    other_ref[...] = total[block:]


def shards(
    frames,
    rewards,
    actions,
    fractions,
    episode_shard,
    table,
    norm_gain,
    torso_weight,
    embed_weight,
    value_weight,
):
    group = lax.axis_index("grp")
    place = lax.axis_index("fsdp")
    x_place = lax.axis_index("tp") // 2
    shard_total = lax.axis_size("fsdp")
    where = jnp.stack([group, place // Z, place % Z, x_place]).astype(jnp.int32)
    rows_block = frames.shape[1]
    width = frames.shape[2]
    features = torso_weight.shape[1]
    half = rows_block // 2
    side = width // 2
    block = side // shard_total
    strip = half // X
    own_rows = group * half
    other_rows = (1 - group) * half
    smem = pl.BlockSpec(memory_space=pltpu.SMEM)
    vmem = pl.BlockSpec(memory_space=pltpu.VMEM)

    with jax.named_scope("rows_swap"):
        values = frames[0]
        tile = 32
        normed_own, normed_send = pl.pallas_call(
            norm_kernel,
            grid=(rows_block // tile,),
            out_shape=(jax.ShapeDtypeStruct((rows_block, side), jnp.bfloat16),) * 2,
            in_specs=[
                smem,
                pl.BlockSpec((tile, width), lambda i: (i, 0)),
                pl.BlockSpec((1, width), lambda i: (0, 0)),
            ],
            out_specs=(pl.BlockSpec((tile, side), lambda i: (i, 0)),) * 2,
            compiler_params=pltpu.CompilerParams(vmem_limit_bytes=12 << 20),
            cost_estimate=pl.CostEstimate(
                flops=6 * rows_block * width,
                transcendentals=0,
                bytes_accessed=4 * rows_block * width,
            ),
            name="norm",
        )(where, values, norm_gain[None, :])
    with jax.named_scope("weight_gather"):
        lines = [torso_weight] + [
            lax.ppermute(torso_weight, "fsdp", z_from(k)) for k in range(1, Z)
        ]
        rounds = [round_y(line, k < 2) for k, line in enumerate(lines)]
        chunks = lines + [rounds[k][j] for j in (0, 2, 1) for k in range(Z)]

    with jax.named_scope("rows_swap"):
        normed_got = lax.ppermute(normed_send, "grp", SWAP)
        ints = jnp.concatenate([fractions[0].T, actions[0][None, :]], 0)
        kept = lax.dynamic_slice_in_dim(ints, own_rows, half, 1)
        got = lax.ppermute(lax.dynamic_slice_in_dim(ints, other_rows, half, 1), "grp", SWAP)
        target_ints = jnp.where(group == 0, kept, got)
        online_ints = jnp.where(group == 0, got, kept)
        ints_all = jnp.concatenate([target_ints, online_ints], 1)
        fraction_rows = ints_all[:-1]
        action_rows = ints_all[-1]

    with jax.named_scope("columns_exchange"):

        lanes = jnp.arange(shard_total, dtype=jnp.int32)
        onehot = episode_shard[:, :1] == lanes[None, :]
        local_counts = jnp.sum(onehot.astype(jnp.float32), axis=0).astype(jnp.bfloat16)
        count_tile = jnp.pad(local_counts[None, :], ((0, 15), (0, block - shard_total)))
        count_tile, _ = lax.optimization_barrier(
            (count_tile, tuple(r[k] for r in rounds[:2] for k in range(2)))
        )
        pieces = pl.pallas_call(
            pieces_kernel,
            out_shape=jax.ShapeDtypeStruct((2, shard_total, strip + 16, block), jnp.bfloat16),
            in_specs=[smem] + [pl.BlockSpec(memory_space=pl.ANY)] * 2 + [vmem],
            out_specs=vmem,
            scratch_shapes=[
                pltpu.VMEM((2, strip, side), jnp.bfloat16),
                pltpu.SemaphoreType.DMA((2,)),
            ],
            compiler_params=pltpu.CompilerParams(vmem_limit_bytes=4 << 20),
            cost_estimate=pl.CostEstimate(
                flops=0, transcendentals=0, bytes_accessed=8 * strip * side
            ),
            name="pieces",
        )(where, normed_own, normed_got, count_tile)
        pieces = lax.all_to_all(
            pieces.reshape(2 * shard_total, strip + 16, block), ("grp", "fsdp"), 0, 0, tiled=True
        ).reshape(2, shard_total, strip + 16, block)
        counts = jnp.sum(pieces[0, :, strip, :shard_total].astype(jnp.float32), axis=0)
        pieces = pieces[:, :, :strip]
        after = lax.ppermute(pieces, "tp", x_from(1))
        before = lax.ppermute(pieces, "tp", x_from(3))
        far_a = lax.ppermute(after[0], "tp", x_from(1))
        far_b = lax.ppermute(before[1], "tp", x_from(3))
        columns = pl.pallas_call(
            columns_kernel,
            out_shape=jax.ShapeDtypeStruct((2 * block, shard_total * half), jnp.bfloat16),
            in_specs=[smem] + [vmem] * 5,
            out_specs=vmem,
            scratch_shapes=[pltpu.VMEM((half, 2 * block), jnp.bfloat16)],
            compiler_params=pltpu.CompilerParams(vmem_limit_bytes=8 << 20),
            cost_estimate=pl.CostEstimate(
                flops=0, transcendentals=0, bytes_accessed=8 * shard_total * half * block
            ),
            name="columns",
        )(where, pieces, after, before, far_a, far_b)

    with jax.named_scope("counts"):
        inverse = float(rows_block) / counts
        row_weight = jnp.sum(jnp.where(onehot, inverse[None, :], 0.0), axis=1)
        row_weight = lax.dynamic_slice_in_dim(row_weight, own_rows, half, 0)

    choose_mask = (action_rows[:, None] == jnp.arange(ACTIONS, dtype=jnp.int32)[None, :]).astype(
        jnp.bfloat16
    )
    picked = jnp.dot(choose_mask, value_weight, preferred_element_type=jnp.float32)
    cosine = jnp.cos(
        jnp.pi * jnp.arange(COSINES, dtype=jnp.float32)[None, :] * table[:, None]
    ).astype(jnp.bfloat16)
    embedding = jax.nn.relu(
        jnp.dot(cosine, embed_weight, preferred_element_type=jnp.float32)
    ).astype(jnp.bfloat16)
    ids = jnp.arange(FRACS, dtype=jnp.int32)
    online_fractions = fraction_rows[:, half:]
    online_select = online_fractions[:, None, :] == ids[None, :, None]
    levels = jnp.sum(jnp.where(online_select, table[None, :, None], 0.0), axis=1)
    reward_rows = lax.dynamic_slice_in_dim(rewards, own_rows, half, 0).astype(jnp.float32)

    part_shape = jax.ShapeDtypeStruct((rows_block, features), jnp.float32)
    keep, send = pl.pallas_call(
        preact_kernel,
        out_shape=(part_shape, part_shape),
        in_specs=[smem] + [pl.BlockSpec(memory_space=pl.ANY)] * (2 + Y * Z),
        out_specs=(vmem, vmem),
        scratch_shapes=[
            pltpu.VMEM((2 * rows_block, features), jnp.float32),
            pltpu.VMEM((Y * Z, 2 * rows_block, block), jnp.bfloat16),
            pltpu.VMEM((Y * Z, block, features), jnp.bfloat16),
            pltpu.SemaphoreType.DMA((3, Y * Z)),
        ],
        compiler_params=pltpu.CompilerParams(vmem_limit_bytes=14 << 20),
        cost_estimate=pl.CostEstimate(
            flops=4 * rows_block * side * features,
            transcendentals=0,
            bytes_accessed=2 * side * features + 4 * side * rows_block + 8 * rows_block * features,
        ),
        name="preact",
    )(where, normed_own, normed_got, *chunks)
    preact = keep + lax.ppermute(send, "grp", SWAP)
    weighted = (jax.nn.silu(preact) * picked).astype(jnp.bfloat16)
    table_values = lax.dot_general(
        embedding, weighted, (((1,), (1,)), ((), ())), preferred_element_type=jnp.float32
    )
    partial_quant = jnp.sum(
        jnp.where(
            fraction_rows[:, None, :] == ids[None, :, None], table_values[None, :, :], 0.0
        ),
        axis=1,
    )
    partial_quant, _ = lax.optimization_barrier((partial_quant, pieces))
    with jax.named_scope("quant_sum"):
        tp_total = lax.axis_size("tp")
        quant = jnp.sum(
            lax.all_to_all(
                jnp.broadcast_to(partial_quant[None], (tp_total,) + partial_quant.shape),
                "tp",
                0,
                0,
                tiled=True,
            ),
            axis=0,
        )
    quant, _ = lax.optimization_barrier((quant, (after, before)))
    target_quant = quant[:, :half]
    online_quant = quant[:, half:]
    target_value = reward_rows[None, :] + 0.99 * target_quant
    errors = target_value[None, :, :] - online_quant[:, None, :]
    weight = jnp.abs(levels[:, None, :] - (errors < 0).astype(jnp.float32))
    grad_quant = -row_weight[None, :] * jnp.sum(weight * jnp.clip(errors, -1.0, 1.0), axis=1)
    grad_table = jnp.sum(jnp.where(online_select, grad_quant[:, None, :], 0.0), axis=0)
    grad_feature = lax.dot_general(
        grad_table,
        embedding.astype(jnp.float32),
        (((0,), (0,)), ((), ())),
        precision=lax.Precision.HIGHEST,
    )
    online_preact = preact[half:]
    gate_value = jax.nn.sigmoid(online_preact)
    grad_preact = (
        grad_feature
        * picked[half:]
        * gate_value
        * (1.0 + online_preact * (1.0 - gate_value))
    ).astype(jnp.bfloat16)

    with jax.named_scope("grad_gather"):
        b0 = lax.ppermute(grad_preact, "fsdp", y_from(1))
        a0 = lax.ppermute(grad_preact, "fsdp", y_from(3))
        pieces_z = tuple(lax.ppermute(grad_preact, "fsdp", z_from(k)) for k in range(1, Z))
        pieces_z, _ = lax.optimization_barrier((pieces_z, (b0, a0)))
        line = jnp.concatenate(pieces_z, 0)
        f0 = lax.ppermute(a0, "fsdp", y_from(3))
        a1 = lax.ppermute(line, "fsdp", y_from(3))
        b1 = lax.ppermute(line, "fsdp", y_from(1))
        f1 = lax.ppermute(a1[:half], "fsdp", y_from(3))
        f2 = lax.ppermute(b1[half:], "fsdp", y_from(1))

    near = pl.pallas_call(
        near_kernel,
        out_shape=jax.ShapeDtypeStruct((2 * block, features), jnp.float32),
        in_specs=[vmem] * 7,
        out_specs=vmem,
        compiler_params=pltpu.CompilerParams(vmem_limit_bytes=12 << 20),
        cost_estimate=pl.CostEstimate(
            flops=12 * Z * half * 2 * block * features // 2,
            transcendentals=0,
            bytes_accessed=6 * Z * half * (2 * block + features),
        ),
        name="near",
    )(columns, grad_preact, line, b0, b1, a0, a1)
    final_shape = jax.ShapeDtypeStruct((block, features), jnp.float32)
    mine, theirs = pl.pallas_call(
        far_kernel,
        out_shape=(final_shape, final_shape),
        in_specs=[vmem] * 5,
        out_specs=(vmem, vmem),
        compiler_params=pltpu.CompilerParams(vmem_limit_bytes=12 << 20),
        cost_estimate=pl.CostEstimate(
            flops=4 * Z * half * block * features,
            transcendentals=0,
            bytes_accessed=2 * Z * half * (2 * block + features) + 16 * block * features,
        ),
        name="far",
    )(columns, near, f0, f1, f2)
    torso_grad = mine + lax.ppermute(theirs, "grp", SWAP)
    updated = (torso_weight.astype(jnp.float32) - 0.01 * torso_grad).astype(jnp.bfloat16)
    refreshed_weight = lax.all_to_all(updated, "tp", split_axis=0, concat_axis=1, tiled=True)
    return (torso_grad, refreshed_weight)


def solution(mesh):
    placed = (
        P("grp", "fsdp", None),
        P("fsdp"),
        P("grp", "fsdp"),
        P("grp", "fsdp", None),
        P("fsdp", None),
        P(),
        P(),
        P(("grp", "fsdp"), "tp"),
        P(None, "tp"),
        P(None, "tp"),
    )
    return jax.shard_map(
        shards,
        mesh=mesh,
        in_specs=placed,
        out_specs=(P(("grp", "fsdp"), "tp"), P(("grp", "fsdp", "tp"), None)),
        check_vma=False,
    )
```

```python
import jax
import jax.numpy as jnp
from jax import lax
from jax.experimental import pallas as pl
from jax.experimental.pallas import tpu as pltpu
from jax.sharding import PartitionSpec as P

ACTIONS = 18
COSINES = 64
FRACS = 64
X = 4
Y = 4
Z = 4


SWAP = [(0, 1), (1, 0)]


def z_from(step):
    return [(f, (f // Z) * Z + (f % Z - step) % Z) for f in range(Y * Z)]


def y_from(step):
    return [(f, (f - step * Z) % (Y * Z)) for f in range(Y * Z)]


def x_from(step):
    return [(t, (t - step * 2) % (X * 2)) for t in range(X * 2)]


def round_y(block, upward):
    below = lax.ppermute(block, "fsdp", y_from(1))
    above = lax.ppermute(block, "fsdp", y_from(3))
    if upward:
        return below, above, lax.ppermute(above, "fsdp", y_from(3))
    return below, above, lax.ppermute(below, "fsdp", y_from(1))


def preact_kernel(where_ref, own_ref, got_ref, *refs):
    weights = refs[: Y * Z]
    keep_ref, send_ref, total, rows_held, held, sems = refs[Y * Z :]
    group, y, z = where_ref[0], where_ref[1], where_ref[2]
    rows = own_ref.shape[0]
    block = weights[0].shape[0]
    order = [(0, k) for k in range(Z)] + [(j, k) for k in range(Z) for j in (1, 3)]
    order += [(2, k) for k in range(Z)]
    copies = []
    for step, (step_y, step_z) in enumerate(order):
        place = lax.rem(y + step_y, Y) * Z + lax.rem(z + step_z, Z)
        cols = pl.ds(pl.multiple_of(place * block, block), block)
        source = weights[step_y * Z + step_z]
        copies.append(
            (
                pltpu.make_async_copy(
                    own_ref.at[:, cols], rows_held.at[step, pl.ds(0, rows)], sems.at[0, step]
                ),
                pltpu.make_async_copy(
                    got_ref.at[:, cols], rows_held.at[step, pl.ds(rows, rows)], sems.at[1, step]
                ),
                pltpu.make_async_copy(source, held.at[step], sems.at[2, step]),
            )
        )
        for copy in copies[-1]:
            copy.start()
    for step in range(len(order)):
        for copy in copies[step]:
            copy.wait()
        term = jnp.dot(rows_held[step], held[step], preferred_element_type=jnp.float32)
        if step == 0:
            total[...] = term
        else:
            total[...] += term
    half = rows // 2
    other = 1 - group
    for base, part in ((0, group), (rows, other)):
        out = pl.ds(pl.multiple_of(part * half, half), half)
        keep_ref[out, :] = total[pl.ds(pl.multiple_of(base + group * half, half), half), :]
        send_ref[out, :] = total[pl.ds(pl.multiple_of(base + other * half, half), half), :]


def norm_kernel(where_ref, rows_ref, gain_ref, own_ref, send_ref):
    side = own_ref.shape[1]
    wide = rows_ref[...].astype(jnp.float32)
    scale = lax.rsqrt(jnp.mean(wide * wide, axis=-1, keepdims=True) + 1e-05)
    for part, out_ref in ((where_ref[0], own_ref), (1 - where_ref[0], send_ref)):
        cols = pl.ds(pl.multiple_of(part * side, side), side)
        values = rows_ref[:, cols].astype(jnp.float32)
        out_ref[...] = (values * scale * gain_ref[:, cols]).astype(jnp.bfloat16)


def pieces_kernel(where_ref, own_ref, got_ref, count_ref, out_ref, held, sems):
    places, _, block = out_ref.shape[1:]
    strip = held.shape[1]
    half = own_ref.shape[0] // 2

    def fetch(source):
        copies = []
        for k in range(2):
            row = pl.multiple_of(k * half + where_ref[3] * strip, strip)
            copies.append(
                pltpu.make_async_copy(source.at[pl.ds(row, strip), :], held.at[k], sems.at[k])
            )
            copies[-1].start()
        for copy in copies:
            copy.wait()

    @pl.when(where_ref[0] == 1)
    def _():
        fetch(own_ref)

    @pl.when(where_ref[0] == 0)
    def _():
        fetch(got_ref)

    for k in range(2):
        for place in range(places):
            out_ref[k, place, :strip] = held[k, :, place * block : (place + 1) * block]
            out_ref[k, place, strip:] = count_ref[...]


def columns_kernel(where_ref, own_ref, after_ref, before_ref, far_a_ref, far_b_ref, out_ref, held):
    group, y, z, x = where_ref[0], where_ref[1], where_ref[2], where_ref[3]
    other = 1 - group
    strip, block = own_ref.shape[2], own_ref.shape[3]
    span = strip * X

    def body(step, carry):
        place = lax.rem(y + step // Z, Y) * Z + lax.rem(z + lax.rem(step, Z), Z)
        for shift, ref in ((0, own_ref), (1, after_ref), (3, before_ref)):
            rows = pl.ds(pl.multiple_of(lax.rem(x + shift, X) * strip, strip), strip)
            held[rows, :block] = ref[group, place]
            held[rows, block:] = ref[other, place]
        rows = pl.ds(pl.multiple_of(lax.rem(x + 2, X) * strip, strip), strip)
        held[rows, pl.ds(pl.multiple_of(group * block, block), block)] = far_a_ref[place]
        held[rows, pl.ds(pl.multiple_of(other * block, block), block)] = far_b_ref[place]
        out_ref[:, pl.ds(pl.multiple_of(step * span, span), span)] = held[...].T
        return carry

    lax.fori_loop(0, Y * Z, body, 0)


def near_kernel(cols_ref, own_ref, line_ref, b0_ref, b1_ref, a0_ref, a1_ref, out_ref):
    half = own_ref.shape[0]
    span = Z * half
    total = None
    for base, first, rest in (
        (0, own_ref, line_ref),
        (span, b0_ref, b1_ref),
        (3 * span, a0_ref, a1_ref),
    ):
        grads = jnp.concatenate([first[...], rest[...]], 0)
        term = jnp.dot(
            cols_ref[:, base : base + span], grads, preferred_element_type=jnp.float32
        )
        total = term if total is None else total + term
    out_ref[...] = total


def far_kernel(cols_ref, near_ref, f0_ref, f1_ref, f2_ref, own_ref, other_ref):
    grads = jnp.concatenate([f0_ref[...], f1_ref[...], f2_ref[...]], 0)
    span = grads.shape[0]
    block = own_ref.shape[0]
    cols = cols_ref[:, 2 * span : 3 * span]
    total = near_ref[...] + jnp.dot(cols, grads, preferred_element_type=jnp.float32)
    own_ref[...] = total[:block]
    other_ref[...] = total[block:]


def shards(
    frames,
    rewards,
    actions,
    fractions,
    episode_shard,
    table,
    norm_gain,
    torso_weight,
    embed_weight,
    value_weight,
):
    group = lax.axis_index("grp")
    place = lax.axis_index("fsdp")
    x_place = lax.axis_index("tp") // 2
    shard_total = lax.axis_size("fsdp")
    where = jnp.stack([group, place // Z, place % Z, x_place]).astype(jnp.int32)
    rows_block = frames.shape[1]
    width = frames.shape[2]
    features = torso_weight.shape[1]
    half = rows_block // 2
    side = width // 2
    block = side // shard_total
    strip = half // X
    own_rows = group * half
    other_rows = (1 - group) * half
    smem = pl.BlockSpec(memory_space=pltpu.SMEM)
    vmem = pl.BlockSpec(memory_space=pltpu.VMEM)

    with jax.named_scope("weight_gather"):
        lines = [torso_weight] + [
            lax.ppermute(torso_weight, "fsdp", z_from(k)) for k in range(1, Z)
        ]
        rounds = [round_y(line, k < 2) for k, line in enumerate(lines)]
        chunks = lines + [rounds[k][j] for j in (0, 2, 1) for k in range(Z)]

    with jax.named_scope("rows_swap"):
        values, _ = lax.optimization_barrier((frames[0], (lines[1:], rounds[0][:2], rounds[1][:2])))
        tile = 32
        normed_own, normed_send = pl.pallas_call(
            norm_kernel,
            grid=(rows_block // tile,),
            out_shape=(jax.ShapeDtypeStruct((rows_block, side), jnp.bfloat16),) * 2,
            in_specs=[
                smem,
                pl.BlockSpec((tile, width), lambda i: (i, 0)),
                pl.BlockSpec((1, width), lambda i: (0, 0)),
            ],
            out_specs=(pl.BlockSpec((tile, side), lambda i: (i, 0)),) * 2,
            compiler_params=pltpu.CompilerParams(vmem_limit_bytes=12 << 20),
            cost_estimate=pl.CostEstimate(
                flops=6 * rows_block * width,
                transcendentals=0,
                bytes_accessed=4 * rows_block * width,
            ),
            name="norm",
        )(where, values, norm_gain[None, :])
    with jax.named_scope("rows_swap"):
        normed_got = lax.ppermute(normed_send, "grp", SWAP)
        ints = jnp.concatenate([fractions[0].T, actions[0][None, :]], 0)
        kept = lax.dynamic_slice_in_dim(ints, own_rows, half, 1)
        got = lax.ppermute(lax.dynamic_slice_in_dim(ints, other_rows, half, 1), "grp", SWAP)
        target_ints = jnp.where(group == 0, kept, got)
        online_ints = jnp.where(group == 0, got, kept)
        ints_all = jnp.concatenate([target_ints, online_ints], 1)
        fraction_rows = ints_all[:-1]
        action_rows = ints_all[-1]

    with jax.named_scope("columns_exchange"):

        lanes = jnp.arange(shard_total, dtype=jnp.int32)
        onehot = episode_shard[:, :1] == lanes[None, :]
        local_counts = jnp.sum(onehot.astype(jnp.float32), axis=0).astype(jnp.bfloat16)
        count_tile = jnp.pad(local_counts[None, :], ((0, 15), (0, block - shard_total)))
        count_tile, _ = lax.optimization_barrier(
            (count_tile, tuple(r[k] for r in rounds for k in range(2)))
        )
        pieces = pl.pallas_call(
            pieces_kernel,
            out_shape=jax.ShapeDtypeStruct((2, shard_total, strip + 16, block), jnp.bfloat16),
            in_specs=[smem] + [pl.BlockSpec(memory_space=pl.ANY)] * 2 + [vmem],
            out_specs=vmem,
            scratch_shapes=[
                pltpu.VMEM((2, strip, side), jnp.bfloat16),
                pltpu.SemaphoreType.DMA((2,)),
            ],
            compiler_params=pltpu.CompilerParams(vmem_limit_bytes=4 << 20),
            cost_estimate=pl.CostEstimate(
                flops=0, transcendentals=0, bytes_accessed=8 * strip * side
            ),
            name="pieces",
        )(where, normed_own, normed_got, count_tile)
        pieces = lax.all_to_all(
            pieces.reshape(2 * shard_total, strip + 16, block), ("grp", "fsdp"), 0, 0, tiled=True
        ).reshape(2, shard_total, strip + 16, block)
        counts = jnp.sum(pieces[0, :, strip, :shard_total].astype(jnp.float32), axis=0)
        pieces = pieces[:, :, :strip]

    with jax.named_scope("counts"):
        inverse = float(rows_block) / counts
        row_weight = jnp.sum(jnp.where(onehot, inverse[None, :], 0.0), axis=1)
        row_weight = lax.dynamic_slice_in_dim(row_weight, own_rows, half, 0)

    choose_mask = (action_rows[:, None] == jnp.arange(ACTIONS, dtype=jnp.int32)[None, :]).astype(
        jnp.bfloat16
    )
    picked = jnp.dot(choose_mask, value_weight, preferred_element_type=jnp.float32)
    cosine = jnp.cos(
        jnp.pi * jnp.arange(COSINES, dtype=jnp.float32)[None, :] * table[:, None]
    ).astype(jnp.bfloat16)
    embedding = jax.nn.relu(
        jnp.dot(cosine, embed_weight, preferred_element_type=jnp.float32)
    ).astype(jnp.bfloat16)
    ids = jnp.arange(FRACS, dtype=jnp.int32)
    online_fractions = fraction_rows[:, half:]
    online_select = online_fractions[:, None, :] == ids[None, :, None]
    levels = jnp.sum(jnp.where(online_select, table[None, :, None], 0.0), axis=1)
    reward_rows = lax.dynamic_slice_in_dim(rewards, own_rows, half, 0).astype(jnp.float32)

    part_shape = jax.ShapeDtypeStruct((rows_block, features), jnp.float32)
    keep, send = pl.pallas_call(
        preact_kernel,
        out_shape=(part_shape, part_shape),
        in_specs=[smem] + [pl.BlockSpec(memory_space=pl.ANY)] * (2 + Y * Z),
        out_specs=(vmem, vmem),
        scratch_shapes=[
            pltpu.VMEM((2 * rows_block, features), jnp.float32),
            pltpu.VMEM((Y * Z, 2 * rows_block, block), jnp.bfloat16),
            pltpu.VMEM((Y * Z, block, features), jnp.bfloat16),
            pltpu.SemaphoreType.DMA((3, Y * Z)),
        ],
        compiler_params=pltpu.CompilerParams(vmem_limit_bytes=14 << 20),
        cost_estimate=pl.CostEstimate(
            flops=4 * rows_block * side * features,
            transcendentals=0,
            bytes_accessed=2 * side * features + 4 * side * rows_block + 8 * rows_block * features,
        ),
        name="preact",
    )(where, normed_own, normed_got, *chunks)
    preact = keep + lax.ppermute(send, "grp", SWAP)
    weighted = (jax.nn.silu(preact) * picked).astype(jnp.bfloat16)
    table_values = lax.dot_general(
        embedding, weighted, (((1,), (1,)), ((), ())), preferred_element_type=jnp.float32
    )
    partial_quant = jnp.sum(
        jnp.where(
            fraction_rows[:, None, :] == ids[None, :, None], table_values[None, :, :], 0.0
        ),
        axis=1,
    )
    with jax.named_scope("quant_sum"):
        quant = partial_quant
        for flip in (2, 4):
            quant = quant + lax.ppermute(quant, "tp", [(t, t ^ flip) for t in range(2 * X)])
        quant = quant + lax.ppermute(quant, "tp", [(t, t ^ 1) for t in range(2 * X)])
    quant, pieces = lax.optimization_barrier((quant, pieces))
    target_quant = quant[:, :half]
    online_quant = quant[:, half:]
    target_value = reward_rows[None, :] + 0.99 * target_quant
    errors = target_value[None, :, :] - online_quant[:, None, :]
    weight = jnp.abs(levels[:, None, :] - (errors < 0).astype(jnp.float32))
    grad_quant = -row_weight[None, :] * jnp.sum(weight * jnp.clip(errors, -1.0, 1.0), axis=1)
    grad_table = jnp.sum(jnp.where(online_select, grad_quant[:, None, :], 0.0), axis=0)
    grad_feature = lax.dot_general(
        grad_table,
        embedding.astype(jnp.float32),
        (((0,), (0,)), ((), ())),
        precision=lax.Precision.HIGHEST,
    )
    online_preact = preact[half:]
    gate_value = jax.nn.sigmoid(online_preact)
    grad_preact = (
        grad_feature
        * picked[half:]
        * gate_value
        * (1.0 + online_preact * (1.0 - gate_value))
    ).astype(jnp.bfloat16)

    grad_preact, pieces = lax.optimization_barrier((grad_preact, pieces))
    with jax.named_scope("columns_round_x"):
        after = lax.ppermute(pieces, "tp", x_from(1))
        before = lax.ppermute(pieces, "tp", x_from(3))
        far_a = lax.ppermute(after[0], "tp", x_from(1))
        far_b = lax.ppermute(before[1], "tp", x_from(3))
        columns = pl.pallas_call(
            columns_kernel,
            out_shape=jax.ShapeDtypeStruct((2 * block, shard_total * half), jnp.bfloat16),
            in_specs=[smem] + [vmem] * 5,
            out_specs=vmem,
            scratch_shapes=[pltpu.VMEM((half, 2 * block), jnp.bfloat16)],
            compiler_params=pltpu.CompilerParams(vmem_limit_bytes=8 << 20),
            cost_estimate=pl.CostEstimate(
                flops=0, transcendentals=0, bytes_accessed=8 * shard_total * half * block
            ),
            name="columns",
        )(where, pieces, after, before, far_a, far_b)

    with jax.named_scope("grad_gather"):
        b0 = lax.ppermute(grad_preact, "fsdp", y_from(1))
        a0 = lax.ppermute(grad_preact, "fsdp", y_from(3))
        pieces_z = tuple(lax.ppermute(grad_preact, "fsdp", z_from(k)) for k in range(1, Z))
        pieces_z, _ = lax.optimization_barrier((pieces_z, (b0, a0, after, before)))
        line = jnp.concatenate(pieces_z, 0)
        f0 = lax.ppermute(a0, "fsdp", y_from(3))
        a1 = lax.ppermute(line, "fsdp", y_from(3))
        b1 = lax.ppermute(line, "fsdp", y_from(1))
        f1 = lax.ppermute(a1[:half], "fsdp", y_from(3))
        f2 = lax.ppermute(b1[half:], "fsdp", y_from(1))

    near = pl.pallas_call(
        near_kernel,
        out_shape=jax.ShapeDtypeStruct((2 * block, features), jnp.float32),
        in_specs=[vmem] * 7,
        out_specs=vmem,
        compiler_params=pltpu.CompilerParams(vmem_limit_bytes=12 << 20),
        cost_estimate=pl.CostEstimate(
            flops=12 * Z * half * 2 * block * features // 2,
            transcendentals=0,
            bytes_accessed=6 * Z * half * (2 * block + features),
        ),
        name="near",
    )(columns, grad_preact, line, b0, b1, a0, a1)
    final_shape = jax.ShapeDtypeStruct((block, features), jnp.float32)
    mine, theirs = pl.pallas_call(
        far_kernel,
        out_shape=(final_shape, final_shape),
        in_specs=[vmem] * 5,
        out_specs=(vmem, vmem),
        compiler_params=pltpu.CompilerParams(vmem_limit_bytes=12 << 20),
        cost_estimate=pl.CostEstimate(
            flops=4 * Z * half * block * features,
            transcendentals=0,
            bytes_accessed=2 * Z * half * (2 * block + features) + 16 * block * features,
        ),
        name="far",
    )(columns, near, f0, f1, f2)
    torso_grad = mine + lax.ppermute(theirs, "grp", SWAP)
    updated = (torso_weight.astype(jnp.float32) - 0.01 * torso_grad).astype(jnp.bfloat16)
    refreshed_weight = lax.all_to_all(updated, "tp", split_axis=0, concat_axis=1, tiled=True)
    return (torso_grad, refreshed_weight)


def solution(mesh):
    placed = (
        P("grp", "fsdp", None),
        P("fsdp"),
        P("grp", "fsdp"),
        P("grp", "fsdp", None),
        P("fsdp", None),
        P(),
        P(),
        P(("grp", "fsdp"), "tp"),
        P(None, "tp"),
        P(None, "tp"),
    )
    return jax.shard_map(
        shards,
        mesh=mesh,
        in_specs=placed,
        out_specs=(P(("grp", "fsdp"), "tp"), P(("grp", "fsdp", "tp"), None)),
        check_vma=False,
    )
```

```python
import jax
import jax.numpy as jnp
from jax import lax
from jax.experimental import pallas as pl
from jax.experimental.pallas import tpu as pltpu
from jax.sharding import PartitionSpec as P

ACTIONS = 18
COSINES = 64
FRACS = 64
X = 4
Y = 4
Z = 4


SWAP = [(0, 1), (1, 0)]


def z_from(step):
    return [(f, (f // Z) * Z + (f % Z - step) % Z) for f in range(Y * Z)]


def y_from(step):
    return [(f, (f - step * Z) % (Y * Z)) for f in range(Y * Z)]


def x_from(step):
    return [(t, (t - step * 2) % (X * 2)) for t in range(X * 2)]


def round_y(block, upward):
    below = lax.ppermute(block, "fsdp", y_from(1))
    above = lax.ppermute(block, "fsdp", y_from(3))
    if upward:
        return below, above, lax.ppermute(above, "fsdp", y_from(3))
    return below, above, lax.ppermute(below, "fsdp", y_from(1))


def in_hbm(*arrays):
    return [pltpu.with_memory_space_constraint(array, pltpu.HBM) for array in arrays]


def preact_kernel(where_ref, own_ref, got_ref, *refs):
    weights = refs[: Y * Z]
    keep_ref, send_ref, total, rows_held, held, sems = refs[Y * Z :]
    group, y, z = where_ref[0], where_ref[1], where_ref[2]
    rows = own_ref.shape[0]
    block = weights[0].shape[0]
    order = [(0, k) for k in range(Z)] + [(j, k) for k in range(Z) for j in (1, 3)]
    order += [(2, k) for k in range(Z)]
    copies = []
    for step, (step_y, step_z) in enumerate(order):
        place = lax.rem(y + step_y, Y) * Z + lax.rem(z + step_z, Z)
        cols = pl.ds(pl.multiple_of(place * block, block), block)
        source = weights[step_y * Z + step_z]
        copies.append(
            (
                pltpu.make_async_copy(
                    own_ref.at[:, cols], rows_held.at[step, pl.ds(0, rows)], sems.at[0, step]
                ),
                pltpu.make_async_copy(
                    got_ref.at[:, cols], rows_held.at[step, pl.ds(rows, rows)], sems.at[1, step]
                ),
                pltpu.make_async_copy(source, held.at[step], sems.at[2, step]),
            )
        )
        for copy in copies[-1]:
            copy.start()
    for step in range(len(order)):
        for copy in copies[step]:
            copy.wait()
        term = jnp.dot(rows_held[step], held[step], preferred_element_type=jnp.float32)
        if step == 0:
            total[...] = term
        else:
            total[...] += term
    half = rows // 2
    other = 1 - group
    for base, part in ((0, group), (rows, other)):
        out = pl.ds(pl.multiple_of(part * half, half), half)
        keep_ref[out, :] = total[pl.ds(pl.multiple_of(base + group * half, half), half), :]
        send_ref[out, :] = total[pl.ds(pl.multiple_of(base + other * half, half), half), :]


def norm_kernel(where_ref, rows_ref, gain_ref, own_ref, send_ref):
    side = own_ref.shape[1]
    wide = rows_ref[...].astype(jnp.float32)
    scale = lax.rsqrt(jnp.mean(wide * wide, axis=-1, keepdims=True) + 1e-05)
    for part, out_ref in ((where_ref[0], own_ref), (1 - where_ref[0], send_ref)):
        cols = pl.ds(pl.multiple_of(part * side, side), side)
        values = rows_ref[:, cols].astype(jnp.float32)
        out_ref[...] = (values * scale * gain_ref[:, cols]).astype(jnp.bfloat16)


def pieces_kernel(where_ref, own_ref, got_ref, count_ref, out_ref, held, sems):
    places, _, block = out_ref.shape[1:]
    strip = held.shape[1]
    half = own_ref.shape[0] // 2

    def fetch(source):
        copies = []
        for k in range(2):
            row = pl.multiple_of(k * half + where_ref[3] * strip, strip)
            copies.append(
                pltpu.make_async_copy(source.at[pl.ds(row, strip), :], held.at[k], sems.at[k])
            )
            copies[-1].start()
        for copy in copies:
            copy.wait()

    @pl.when(where_ref[0] == 1)
    def _():
        fetch(own_ref)

    @pl.when(where_ref[0] == 0)
    def _():
        fetch(got_ref)

    for k in range(2):
        for place in range(places):
            out_ref[k, place, :strip] = held[k, :, place * block : (place + 1) * block]
            out_ref[k, place, strip:] = count_ref[...]


def columns_kernel(where_ref, own_ref, after_ref, before_ref, far_a_ref, far_b_ref, out_ref, held):
    group, y, z, x = where_ref[0], where_ref[1], where_ref[2], where_ref[3]
    other = 1 - group
    strip, block = own_ref.shape[2], own_ref.shape[3]
    span = strip * X

    def body(step, carry):
        place = lax.rem(y + step // Z, Y) * Z + lax.rem(z + lax.rem(step, Z), Z)
        for shift, ref in ((0, own_ref), (1, after_ref), (3, before_ref)):
            rows = pl.ds(pl.multiple_of(lax.rem(x + shift, X) * strip, strip), strip)
            held[rows, :block] = ref[group, place]
            held[rows, block:] = ref[other, place]
        rows = pl.ds(pl.multiple_of(lax.rem(x + 2, X) * strip, strip), strip)
        held[rows, pl.ds(pl.multiple_of(group * block, block), block)] = far_a_ref[place]
        held[rows, pl.ds(pl.multiple_of(other * block, block), block)] = far_b_ref[place]
        out_ref[:, pl.ds(pl.multiple_of(step * span, span), span)] = held[...].T
        return carry

    lax.fori_loop(0, Y * Z, body, 0)


def near_kernel(cols_ref, own_ref, line_ref, b0_ref, b1_ref, a0_ref, a1_ref, out_ref):
    half = own_ref.shape[0]
    span = Z * half
    total = None
    for base, first, rest in (
        (0, own_ref, line_ref),
        (span, b0_ref, b1_ref),
        (3 * span, a0_ref, a1_ref),
    ):
        grads = jnp.concatenate([first[...], rest[...]], 0)
        term = jnp.dot(
            cols_ref[:, base : base + span], grads, preferred_element_type=jnp.float32
        )
        total = term if total is None else total + term
    out_ref[...] = total


def far_kernel(cols_ref, near_ref, f0_ref, f1_ref, f2_ref, own_ref, other_ref):
    grads = jnp.concatenate([f0_ref[...], f1_ref[...], f2_ref[...]], 0)
    span = grads.shape[0]
    block = own_ref.shape[0]
    cols = cols_ref[:, 2 * span : 3 * span]
    total = near_ref[...] + jnp.dot(cols, grads, preferred_element_type=jnp.float32)
    own_ref[...] = total[:block]
    other_ref[...] = total[block:]


def shards(
    frames,
    rewards,
    actions,
    fractions,
    episode_shard,
    table,
    norm_gain,
    torso_weight,
    embed_weight,
    value_weight,
):
    group = lax.axis_index("grp")
    place = lax.axis_index("fsdp")
    x_place = lax.axis_index("tp") // 2
    shard_total = lax.axis_size("fsdp")
    where = jnp.stack([group, place // Z, place % Z, x_place]).astype(jnp.int32)
    rows_block = frames.shape[1]
    width = frames.shape[2]
    features = torso_weight.shape[1]
    half = rows_block // 2
    side = width // 2
    block = side // shard_total
    strip = half // X
    own_rows = group * half
    other_rows = (1 - group) * half
    smem = pl.BlockSpec(memory_space=pltpu.SMEM)
    vmem = pl.BlockSpec(memory_space=pltpu.VMEM)

    with jax.named_scope("weight_gather"):
        lines = [torso_weight] + [
            lax.ppermute(torso_weight, "fsdp", z_from(k)) for k in range(1, Z)
        ]
        rounds = [round_y(line, k < 2) for k, line in enumerate(lines)]
        chunks = lines + [rounds[k][j] for j in (0, 2, 1) for k in range(Z)]

    with jax.named_scope("rows_swap"):
        values = frames[0]
        tile = 64
        normed_own, normed_send = pl.pallas_call(
            norm_kernel,
            grid=(rows_block // tile,),
            out_shape=(jax.ShapeDtypeStruct((rows_block, side), jnp.bfloat16),) * 2,
            in_specs=[
                smem,
                pl.BlockSpec((tile, width), lambda i: (i, 0)),
                pl.BlockSpec((1, width), lambda i: (0, 0)),
            ],
            out_specs=(pl.BlockSpec((tile, side), lambda i: (i, 0)),) * 2,
            compiler_params=pltpu.CompilerParams(vmem_limit_bytes=12 << 20),
            cost_estimate=pl.CostEstimate(
                flops=6 * rows_block * width,
                transcendentals=0,
                bytes_accessed=4 * rows_block * width,
            ),
            name="norm",
        )(where, *in_hbm(values, norm_gain[None, :]))
    with jax.named_scope("rows_swap"):
        normed_got = lax.ppermute(normed_send, "grp", SWAP)
        ints = jnp.concatenate([fractions[0].T, actions[0][None, :]], 0)
        kept = lax.dynamic_slice_in_dim(ints, own_rows, half, 1)
        got = lax.ppermute(lax.dynamic_slice_in_dim(ints, other_rows, half, 1), "grp", SWAP)
        target_ints = jnp.where(group == 0, kept, got)
        online_ints = jnp.where(group == 0, got, kept)
        ints_all = jnp.concatenate([target_ints, online_ints], 1)
        fraction_rows = ints_all[:-1]
        action_rows = ints_all[-1]

    with jax.named_scope("columns_exchange"):

        lanes = jnp.arange(shard_total, dtype=jnp.int32)
        onehot = episode_shard[:, :1] == lanes[None, :]
        local_counts = jnp.sum(onehot.astype(jnp.float32), axis=0).astype(jnp.bfloat16)
        count_tile = jnp.pad(local_counts[None, :], ((0, 15), (0, block - shard_total)))
        count_tile, _ = lax.optimization_barrier(
            (count_tile, tuple(r[k] for r in rounds for k in range(2)))
        )
        pieces = pl.pallas_call(
            pieces_kernel,
            out_shape=jax.ShapeDtypeStruct((2, shard_total, strip + 16, block), jnp.bfloat16),
            in_specs=[smem] + [pl.BlockSpec(memory_space=pl.ANY)] * 2 + [vmem],
            out_specs=vmem,
            scratch_shapes=[
                pltpu.VMEM((2, strip, side), jnp.bfloat16),
                pltpu.SemaphoreType.DMA((2,)),
            ],
            compiler_params=pltpu.CompilerParams(vmem_limit_bytes=4 << 20),
            cost_estimate=pl.CostEstimate(
                flops=0, transcendentals=0, bytes_accessed=8 * strip * side
            ),
            name="pieces",
        )(where, normed_own, normed_got, count_tile)
        pieces = lax.all_to_all(
            pieces.reshape(2 * shard_total, strip + 16, block), ("grp", "fsdp"), 0, 0, tiled=True
        ).reshape(2, shard_total, strip + 16, block)
        counts = jnp.sum(pieces[0, :, strip, :shard_total].astype(jnp.float32), axis=0)
        pieces = pieces[:, :, :strip]

    with jax.named_scope("counts"):
        inverse = float(rows_block) / counts
        row_weight = jnp.sum(jnp.where(onehot, inverse[None, :], 0.0), axis=1)
        row_weight = lax.dynamic_slice_in_dim(row_weight, own_rows, half, 0)

    choose_mask = (action_rows[:, None] == jnp.arange(ACTIONS, dtype=jnp.int32)[None, :]).astype(
        jnp.bfloat16
    )
    picked = jnp.dot(choose_mask, value_weight, preferred_element_type=jnp.float32)
    cosine = jnp.cos(
        jnp.pi * jnp.arange(COSINES, dtype=jnp.float32)[None, :] * table[:, None]
    ).astype(jnp.bfloat16)
    embedding = jax.nn.relu(
        jnp.dot(cosine, embed_weight, preferred_element_type=jnp.float32)
    ).astype(jnp.bfloat16)
    ids = jnp.arange(FRACS, dtype=jnp.int32)
    online_fractions = fraction_rows[:, half:]
    online_select = online_fractions[:, None, :] == ids[None, :, None]
    levels = jnp.sum(jnp.where(online_select, table[None, :, None], 0.0), axis=1)
    reward_rows = lax.dynamic_slice_in_dim(rewards, own_rows, half, 0).astype(jnp.float32)

    part_shape = jax.ShapeDtypeStruct((rows_block, features), jnp.float32)
    keep, send = pl.pallas_call(
        preact_kernel,
        out_shape=(part_shape, part_shape),
        in_specs=[smem] + [pl.BlockSpec(memory_space=pl.ANY)] * (2 + Y * Z),
        out_specs=(vmem, vmem),
        scratch_shapes=[
            pltpu.VMEM((2 * rows_block, features), jnp.float32),
            pltpu.VMEM((Y * Z, 2 * rows_block, block), jnp.bfloat16),
            pltpu.VMEM((Y * Z, block, features), jnp.bfloat16),
            pltpu.SemaphoreType.DMA((3, Y * Z)),
        ],
        compiler_params=pltpu.CompilerParams(vmem_limit_bytes=14 << 20),
        cost_estimate=pl.CostEstimate(
            flops=4 * rows_block * side * features,
            transcendentals=0,
            bytes_accessed=2 * side * features + 4 * side * rows_block + 8 * rows_block * features,
        ),
        name="preact",
    )(where, *in_hbm(normed_own, normed_got, *chunks))
    preact = keep + lax.ppermute(send, "grp", SWAP)
    weighted = (jax.nn.silu(preact) * picked).astype(jnp.bfloat16)
    table_values = lax.dot_general(
        embedding, weighted, (((1,), (1,)), ((), ())), preferred_element_type=jnp.float32
    )
    partial_quant = jnp.sum(
        jnp.where(
            fraction_rows[:, None, :] == ids[None, :, None], table_values[None, :, :], 0.0
        ),
        axis=1,
    )
    with jax.named_scope("quant_sum"):
        quant = partial_quant
        for flip in (2, 4):
            quant = quant + lax.ppermute(quant, "tp", [(t, t ^ flip) for t in range(2 * X)])
        quant = quant + lax.ppermute(quant, "tp", [(t, t ^ 1) for t in range(2 * X)])
    quant, pieces = lax.optimization_barrier((quant, pieces))
    target_quant = quant[:, :half]
    online_quant = quant[:, half:]
    target_value = reward_rows[None, :] + 0.99 * target_quant
    errors = target_value[None, :, :] - online_quant[:, None, :]
    weight = jnp.abs(levels[:, None, :] - (errors < 0).astype(jnp.float32))
    grad_quant = -row_weight[None, :] * jnp.sum(weight * jnp.clip(errors, -1.0, 1.0), axis=1)
    grad_table = jnp.sum(jnp.where(online_select, grad_quant[:, None, :], 0.0), axis=0)
    grad_feature = lax.dot_general(
        grad_table,
        embedding.astype(jnp.float32),
        (((0,), (0,)), ((), ())),
        precision=lax.Precision.HIGHEST,
    )
    online_preact = preact[half:]
    gate_value = jax.nn.sigmoid(online_preact)
    grad_preact = (
        grad_feature
        * picked[half:]
        * gate_value
        * (1.0 + online_preact * (1.0 - gate_value))
    ).astype(jnp.bfloat16)

    with jax.named_scope("grad_gather"):
        b0 = lax.ppermute(grad_preact, "fsdp", y_from(1))
        a0 = lax.ppermute(grad_preact, "fsdp", y_from(3))
        pieces_z = tuple(lax.ppermute(grad_preact, "fsdp", z_from(k)) for k in range(1, Z))
        pieces_z, _ = lax.optimization_barrier((pieces_z, (b0, a0)))
        line = jnp.concatenate(pieces_z, 0)
        f0 = lax.ppermute(a0, "fsdp", y_from(3))
        a1 = lax.ppermute(line, "fsdp", y_from(3))
        b1 = lax.ppermute(line, "fsdp", y_from(1))
        f1 = lax.ppermute(a1[:half], "fsdp", y_from(3))
        f2 = lax.ppermute(b1[half:], "fsdp", y_from(1))

    pieces, _ = lax.optimization_barrier((pieces, (b0, a0, pieces_z[0])))
    with jax.named_scope("columns_round_x"):
        after = lax.ppermute(pieces, "tp", x_from(1))
        before = lax.ppermute(pieces, "tp", x_from(3))
        far_a = lax.ppermute(after[0], "tp", x_from(1))
        far_b = lax.ppermute(before[1], "tp", x_from(3))
        columns = pl.pallas_call(
            columns_kernel,
            out_shape=jax.ShapeDtypeStruct((2 * block, shard_total * half), jnp.bfloat16),
            in_specs=[smem] + [vmem] * 5,
            out_specs=vmem,
            scratch_shapes=[pltpu.VMEM((half, 2 * block), jnp.bfloat16)],
            compiler_params=pltpu.CompilerParams(vmem_limit_bytes=8 << 20),
            cost_estimate=pl.CostEstimate(
                flops=0, transcendentals=0, bytes_accessed=8 * shard_total * half * block
            ),
            name="columns",
        )(where, pieces, after, before, far_a, far_b)

    near = pl.pallas_call(
        near_kernel,
        out_shape=jax.ShapeDtypeStruct((2 * block, features), jnp.float32),
        in_specs=[vmem] * 7,
        out_specs=vmem,
        compiler_params=pltpu.CompilerParams(vmem_limit_bytes=12 << 20),
        cost_estimate=pl.CostEstimate(
            flops=12 * Z * half * 2 * block * features // 2,
            transcendentals=0,
            bytes_accessed=6 * Z * half * (2 * block + features),
        ),
        name="near",
    )(columns, grad_preact, line, b0, b1, a0, a1)
    final_shape = jax.ShapeDtypeStruct((block, features), jnp.float32)
    mine, theirs = pl.pallas_call(
        far_kernel,
        out_shape=(final_shape, final_shape),
        in_specs=[vmem] * 5,
        out_specs=(vmem, vmem),
        compiler_params=pltpu.CompilerParams(vmem_limit_bytes=12 << 20),
        cost_estimate=pl.CostEstimate(
            flops=4 * Z * half * block * features,
            transcendentals=0,
            bytes_accessed=2 * Z * half * (2 * block + features) + 16 * block * features,
        ),
        name="far",
    )(columns, near, f0, f1, f2)
    torso_grad = mine + lax.ppermute(theirs, "grp", SWAP)
    updated = (torso_weight.astype(jnp.float32) - 0.01 * torso_grad).astype(jnp.bfloat16)
    refreshed_weight = lax.all_to_all(updated, "tp", split_axis=0, concat_axis=1, tiled=True)
    return (torso_grad, refreshed_weight)


def solution(mesh):
    placed = (
        P("grp", "fsdp", None),
        P("fsdp"),
        P("grp", "fsdp"),
        P("grp", "fsdp", None),
        P("fsdp", None),
        P(),
        P(),
        P(("grp", "fsdp"), "tp"),
        P(None, "tp"),
        P(None, "tp"),
    )
    return jax.shard_map(
        shards,
        mesh=mesh,
        in_specs=placed,
        out_specs=(P(("grp", "fsdp"), "tp"), P(("grp", "fsdp", "tp"), None)),
        check_vma=False,
    )
```

```python
import jax
import jax.numpy as jnp
from jax import lax
from jax.experimental import pallas as pl
from jax.experimental.pallas import tpu as pltpu
from jax.sharding import PartitionSpec as P

ACTIONS = 18
COSINES = 64
FRACS = 64
X = 4
Y = 4
Z = 4


SWAP = [(0, 1), (1, 0)]


def z_from(step):
    return [(f, (f // Z) * Z + (f % Z - step) % Z) for f in range(Y * Z)]


def y_from(step):
    return [(f, (f - step * Z) % (Y * Z)) for f in range(Y * Z)]


def x_from(step):
    return [(t, (t - step * 2) % (X * 2)) for t in range(X * 2)]


def in_hbm(*arrays):
    return [pltpu.with_memory_space_constraint(array, pltpu.HBM) for array in arrays]


def preact_kernel(where_ref, own_ref, got_ref, *refs):
    weights = refs[: Y * Z]
    keep_ref, send_ref, total, rows_held, held, sems = refs[Y * Z :]
    group, y, z = where_ref[0], where_ref[1], where_ref[2]
    rows = own_ref.shape[0]
    block = weights[0].shape[0]
    order = [(0, k) for k in range(Z)] + [(j, k) for k in range(Z) for j in (1, 3)]
    order += [(2, k) for k in range(Z)]
    copies = []
    for step, (step_y, step_z) in enumerate(order):
        place = lax.rem(y + step_y, Y) * Z + lax.rem(z + step_z, Z)
        cols = pl.ds(pl.multiple_of(place * block, block), block)
        source = weights[step_y * Z + step_z]
        copies.append(
            (
                pltpu.make_async_copy(
                    own_ref.at[:, cols], rows_held.at[step, pl.ds(0, rows)], sems.at[0, step]
                ),
                pltpu.make_async_copy(
                    got_ref.at[:, cols], rows_held.at[step, pl.ds(rows, rows)], sems.at[1, step]
                ),
                pltpu.make_async_copy(source, held.at[step], sems.at[2, step]),
            )
        )
        for copy in copies[-1]:
            copy.start()
    for step in range(len(order)):
        for copy in copies[step]:
            copy.wait()
        term = jnp.dot(rows_held[step], held[step], preferred_element_type=jnp.float32)
        if step == 0:
            total[...] = term
        else:
            total[...] += term
    half = rows // 2
    other = 1 - group
    for base, part in ((0, group), (rows, other)):
        out = pl.ds(pl.multiple_of(part * half, half), half)
        keep_ref[out, :] = total[pl.ds(pl.multiple_of(base + group * half, half), half), :]
        send_ref[out, :] = total[pl.ds(pl.multiple_of(base + other * half, half), half), :]


def norm_kernel(where_ref, rows_ref, gain_ref, own_ref, send_ref):
    side = own_ref.shape[1]
    wide = rows_ref[...].astype(jnp.float32)
    scale = lax.rsqrt(jnp.mean(wide * wide, axis=-1, keepdims=True) + 1e-05)
    for part, out_ref in ((where_ref[0], own_ref), (1 - where_ref[0], send_ref)):
        cols = pl.ds(pl.multiple_of(part * side, side), side)
        values = rows_ref[:, cols].astype(jnp.float32)
        out_ref[...] = (values * scale * gain_ref[:, cols]).astype(jnp.bfloat16)


def pieces_kernel(where_ref, own_ref, got_ref, count_ref, out_ref, held, sems):
    places, _, block = out_ref.shape[1:]
    strip = held.shape[1]
    half = own_ref.shape[0] // 2

    def fetch(source):
        copies = []
        for k in range(2):
            row = pl.multiple_of(k * half + where_ref[3] * strip, strip)
            copies.append(
                pltpu.make_async_copy(source.at[pl.ds(row, strip), :], held.at[k], sems.at[k])
            )
            copies[-1].start()
        for copy in copies:
            copy.wait()

    @pl.when(where_ref[0] == 1)
    def _():
        fetch(own_ref)

    @pl.when(where_ref[0] == 0)
    def _():
        fetch(got_ref)

    for k in range(2):
        for place in range(places):
            out_ref[k, place, :strip] = held[k, :, place * block : (place + 1) * block]
            out_ref[k, place, strip:] = count_ref[...]


def columns_kernel(where_ref, own_ref, after_ref, before_ref, far_a_ref, far_b_ref, out_ref, held):
    group, y, z, x = where_ref[0], where_ref[1], where_ref[2], where_ref[3]
    other = 1 - group
    block = own_ref.shape[3]
    span = held.shape[0]
    strip = span // X

    def body(step, carry):
        place = lax.rem(y + step // Z, Y) * Z + lax.rem(z + lax.rem(step, Z), Z)
        for shift, ref in ((0, own_ref), (1, after_ref), (3, before_ref)):
            rows = pl.ds(pl.multiple_of(lax.rem(x + shift, X) * strip, strip), strip)
            held[rows, :block] = ref[group, place, :strip]
            held[rows, block:] = ref[other, place, :strip]
        rows = pl.ds(pl.multiple_of(lax.rem(x + 2, X) * strip, strip), strip)
        held[rows, pl.ds(pl.multiple_of(group * block, block), block)] = far_a_ref[place, :strip]
        held[rows, pl.ds(pl.multiple_of(other * block, block), block)] = far_b_ref[place, :strip]
        out_ref[:, pl.ds(pl.multiple_of(step * span, span), span)] = held[...].T
        return carry

    lax.fori_loop(0, Y * Z, body, 0)


def near_kernel(cols_ref, own_ref, line_ref, b0_ref, b1_ref, a0_ref, a1_ref, out_ref):
    half = own_ref.shape[0]
    span = Z * half
    total = None
    for base, first, rest in (
        (0, own_ref, line_ref),
        (span, b0_ref, b1_ref),
        (3 * span, a0_ref, a1_ref),
    ):
        grads = jnp.concatenate([first[...], rest[...]], 0)
        term = jnp.dot(
            cols_ref[:, base : base + span], grads, preferred_element_type=jnp.float32
        )
        total = term if total is None else total + term
    out_ref[...] = total


def far_kernel(cols_ref, near_ref, f0_ref, f1_ref, f2_ref, own_ref, other_ref):
    grads = jnp.concatenate([f0_ref[...], f1_ref[...], f2_ref[...]], 0)
    span = grads.shape[0]
    block = own_ref.shape[0]
    cols = cols_ref[:, 2 * span : 3 * span]
    total = near_ref[...] + jnp.dot(cols, grads, preferred_element_type=jnp.float32)
    own_ref[...] = total[:block]
    other_ref[...] = total[block:]


def shards(
    frames,
    rewards,
    actions,
    fractions,
    episode_shard,
    table,
    norm_gain,
    torso_weight,
    embed_weight,
    value_weight,
):
    group = lax.axis_index("grp")
    place = lax.axis_index("fsdp")
    x_place = lax.axis_index("tp") // 2
    shard_total = lax.axis_size("fsdp")
    where = jnp.stack([group, place // Z, place % Z, x_place]).astype(jnp.int32)
    rows_block = frames.shape[1]
    width = frames.shape[2]
    features = torso_weight.shape[1]
    half = rows_block // 2
    side = width // 2
    block = side // shard_total
    strip = half // X
    own_rows = group * half
    other_rows = (1 - group) * half
    smem = pl.BlockSpec(memory_space=pltpu.SMEM)
    vmem = pl.BlockSpec(memory_space=pltpu.VMEM)

    with jax.named_scope("weight_gather"):
        lines = [torso_weight] + [
            lax.ppermute(torso_weight, "fsdp", z_from(k)) for k in range(1, Z)
        ]
        near = [
            (lax.ppermute(line, "fsdp", y_from(1)), lax.ppermute(line, "fsdp", y_from(3)))
            for line in lines
        ]
        near = lax.optimization_barrier(near)
        far = [
            lax.ppermute(above, "fsdp", y_from(3)) if k < 2 else lax.ppermute(below, "fsdp", y_from(1))
            for k, (below, above) in enumerate(near)
        ]
        rounds = [(below, above, last) for (below, above), last in zip(near, far)]
        chunks = lines + [rounds[k][j] for j in (0, 2, 1) for k in range(Z)]

    with jax.named_scope("rows_swap"):
        values = frames[0]
        tile = 64
        normed_own, normed_send = pl.pallas_call(
            norm_kernel,
            grid=(rows_block // tile,),
            out_shape=(jax.ShapeDtypeStruct((rows_block, side), jnp.bfloat16),) * 2,
            in_specs=[
                smem,
                pl.BlockSpec((tile, width), lambda i: (i, 0)),
                pl.BlockSpec((1, width), lambda i: (0, 0)),
            ],
            out_specs=(pl.BlockSpec((tile, side), lambda i: (i, 0)),) * 2,
            compiler_params=pltpu.CompilerParams(vmem_limit_bytes=12 << 20),
            cost_estimate=pl.CostEstimate(
                flops=6 * rows_block * width,
                transcendentals=0,
                bytes_accessed=4 * rows_block * width,
            ),
            name="norm",
        )(where, *in_hbm(values, norm_gain[None, :]))
    with jax.named_scope("rows_swap"):
        normed_send, _ = lax.optimization_barrier((normed_send, near[0]))
        normed_got = lax.ppermute(normed_send, "grp", SWAP)
        ints = jnp.concatenate([fractions[0].T, actions[0][None, :]], 0)
        kept = lax.dynamic_slice_in_dim(ints, own_rows, half, 1)
        got = lax.ppermute(lax.dynamic_slice_in_dim(ints, other_rows, half, 1), "grp", SWAP)
        target_ints = jnp.where(group == 0, kept, got)
        online_ints = jnp.where(group == 0, got, kept)
        ints_all = jnp.concatenate([target_ints, online_ints], 1)
        fraction_rows = ints_all[:-1]
        action_rows = ints_all[-1]

    with jax.named_scope("columns_exchange"):

        lanes = jnp.arange(shard_total, dtype=jnp.int32)
        onehot = episode_shard[:, :1] == lanes[None, :]
        local_counts = jnp.sum(onehot.astype(jnp.float32), axis=0).astype(jnp.bfloat16)
        count_tile = jnp.pad(local_counts[None, :], ((0, 15), (0, block - shard_total)))
        count_tile, _ = lax.optimization_barrier(
            (count_tile, tuple(r[k] for r in rounds for k in range(2)))
        )
        pieces = pl.pallas_call(
            pieces_kernel,
            out_shape=jax.ShapeDtypeStruct((2, shard_total, strip + 16, block), jnp.bfloat16),
            in_specs=[smem] + [pl.BlockSpec(memory_space=pl.ANY)] * 2 + [vmem],
            out_specs=vmem,
            scratch_shapes=[
                pltpu.VMEM((2, strip, side), jnp.bfloat16),
                pltpu.SemaphoreType.DMA((2,)),
            ],
            compiler_params=pltpu.CompilerParams(vmem_limit_bytes=4 << 20),
            cost_estimate=pl.CostEstimate(
                flops=0, transcendentals=0, bytes_accessed=8 * strip * side
            ),
            name="pieces",
        )(where, normed_own, normed_got, count_tile)
        pieces = lax.all_to_all(
            pieces.reshape(2 * shard_total, strip + 16, block), ("grp", "fsdp"), 0, 0, tiled=True
        ).reshape(2, shard_total, strip + 16, block)
        counts = jnp.sum(pieces[0, :, strip, :shard_total].astype(jnp.float32), axis=0)

    with jax.named_scope("counts"):
        inverse = float(rows_block) / counts
        row_weight = jnp.sum(jnp.where(onehot, inverse[None, :], 0.0), axis=1)
        row_weight = lax.dynamic_slice_in_dim(row_weight, own_rows, half, 0)

    choose_mask = (action_rows[:, None] == jnp.arange(ACTIONS, dtype=jnp.int32)[None, :]).astype(
        jnp.bfloat16
    )
    picked = jnp.dot(choose_mask, value_weight, preferred_element_type=jnp.float32)
    cosine = jnp.cos(
        jnp.pi * jnp.arange(COSINES, dtype=jnp.float32)[None, :] * table[:, None]
    ).astype(jnp.bfloat16)
    embedding = jax.nn.relu(
        jnp.dot(cosine, embed_weight, preferred_element_type=jnp.float32)
    ).astype(jnp.bfloat16)
    ids = jnp.arange(FRACS, dtype=jnp.int32)
    online_fractions = fraction_rows[:, half:]
    online_select = online_fractions[:, None, :] == ids[None, :, None]
    levels = jnp.sum(jnp.where(online_select, table[None, :, None], 0.0), axis=1)
    reward_rows = lax.dynamic_slice_in_dim(rewards, own_rows, half, 0).astype(jnp.float32)

    part_shape = jax.ShapeDtypeStruct((rows_block, features), jnp.float32)
    keep, send = pl.pallas_call(
        preact_kernel,
        out_shape=(part_shape, part_shape),
        in_specs=[smem] + [pl.BlockSpec(memory_space=pl.ANY)] * (2 + Y * Z),
        out_specs=(vmem, vmem),
        scratch_shapes=[
            pltpu.VMEM((2 * rows_block, features), jnp.float32),
            pltpu.VMEM((Y * Z, 2 * rows_block, block), jnp.bfloat16),
            pltpu.VMEM((Y * Z, block, features), jnp.bfloat16),
            pltpu.SemaphoreType.DMA((3, Y * Z)),
        ],
        compiler_params=pltpu.CompilerParams(vmem_limit_bytes=14 << 20),
        cost_estimate=pl.CostEstimate(
            flops=4 * rows_block * side * features,
            transcendentals=0,
            bytes_accessed=2 * side * features + 4 * side * rows_block + 8 * rows_block * features,
        ),
        name="preact",
    )(where, *in_hbm(normed_own, normed_got, *chunks[:8]), *chunks[8:12], *in_hbm(*chunks[12:]))
    preact = keep + lax.ppermute(send, "grp", SWAP)
    weighted = (jax.nn.silu(preact) * picked).astype(jnp.bfloat16)
    table_values = lax.dot_general(
        embedding, weighted, (((1,), (1,)), ((), ())), preferred_element_type=jnp.float32
    )
    partial_quant = jnp.sum(
        jnp.where(
            fraction_rows[:, None, :] == ids[None, :, None], table_values[None, :, :], 0.0
        ),
        axis=1,
    )
    with jax.named_scope("quant_sum"):
        quant = partial_quant
        for flip in (2, 4):
            quant = quant + lax.ppermute(quant, "tp", [(t, t ^ flip) for t in range(2 * X)])
        quant = quant + lax.ppermute(quant, "tp", [(t, t ^ 1) for t in range(2 * X)])
    quant, pieces = lax.optimization_barrier((quant, pieces))
    target_quant = quant[:, :half]
    online_quant = quant[:, half:]
    target_value = reward_rows[None, :] + 0.99 * target_quant
    errors = target_value[None, :, :] - online_quant[:, None, :]
    weight = jnp.abs(levels[:, None, :] - (errors < 0).astype(jnp.float32))
    grad_quant = -row_weight[None, :] * jnp.sum(weight * jnp.clip(errors, -1.0, 1.0), axis=1)
    grad_table = jnp.sum(jnp.where(online_select, grad_quant[:, None, :], 0.0), axis=0)
    grad_feature = lax.dot_general(
        grad_table,
        embedding.astype(jnp.float32),
        (((0,), (0,)), ((), ())),
        precision=lax.Precision.HIGHEST,
    )
    online_preact = preact[half:]
    gate_value = jax.nn.sigmoid(online_preact)
    grad_preact = (
        grad_feature
        * picked[half:]
        * gate_value
        * (1.0 + online_preact * (1.0 - gate_value))
    ).astype(jnp.bfloat16)

    with jax.named_scope("grad_gather"):
        b0 = lax.ppermute(grad_preact, "fsdp", y_from(1))
        a0 = lax.ppermute(grad_preact, "fsdp", y_from(3))
        pieces_z = tuple(lax.ppermute(grad_preact, "fsdp", z_from(k)) for k in range(1, Z))
        pieces_z, _ = lax.optimization_barrier((pieces_z, (b0, a0)))
        line = jnp.concatenate(pieces_z, 0)
        f0 = lax.ppermute(a0, "fsdp", y_from(3))
        a1 = lax.ppermute(line, "fsdp", y_from(3))
        b1 = lax.ppermute(line, "fsdp", y_from(1))
        f1 = lax.ppermute(a1[:half], "fsdp", y_from(3))
        f2 = lax.ppermute(b1[half:], "fsdp", y_from(1))

    pieces, _ = lax.optimization_barrier((pieces, grad_preact))
    with jax.named_scope("columns_round_x"):
        after = lax.ppermute(pieces, "tp", x_from(1))
        before = lax.ppermute(pieces, "tp", x_from(3))
        far_a = lax.ppermute(after[0], "tp", x_from(1))
        far_b = lax.ppermute(before[1], "tp", x_from(3))
        columns = pl.pallas_call(
            columns_kernel,
            out_shape=jax.ShapeDtypeStruct((2 * block, shard_total * half), jnp.bfloat16),
            in_specs=[smem] + [vmem] * 5,
            out_specs=vmem,
            scratch_shapes=[pltpu.VMEM((half, 2 * block), jnp.bfloat16)],
            compiler_params=pltpu.CompilerParams(vmem_limit_bytes=8 << 20),
            cost_estimate=pl.CostEstimate(
                flops=0, transcendentals=0, bytes_accessed=8 * shard_total * half * block
            ),
            name="columns",
        )(where, pieces, after, before, far_a, far_b)

    near = pl.pallas_call(
        near_kernel,
        out_shape=jax.ShapeDtypeStruct((2 * block, features), jnp.float32),
        in_specs=[vmem] * 7,
        out_specs=vmem,
        compiler_params=pltpu.CompilerParams(vmem_limit_bytes=12 << 20),
        cost_estimate=pl.CostEstimate(
            flops=12 * Z * half * 2 * block * features // 2,
            transcendentals=0,
            bytes_accessed=6 * Z * half * (2 * block + features),
        ),
        name="near",
    )(columns, grad_preact, line, b0, b1, a0, a1)
    final_shape = jax.ShapeDtypeStruct((block, features), jnp.float32)
    mine, theirs = pl.pallas_call(
        far_kernel,
        out_shape=(final_shape, final_shape),
        in_specs=[vmem] * 5,
        out_specs=(vmem, vmem),
        compiler_params=pltpu.CompilerParams(vmem_limit_bytes=12 << 20),
        cost_estimate=pl.CostEstimate(
            flops=4 * Z * half * block * features,
            transcendentals=0,
            bytes_accessed=2 * Z * half * (2 * block + features) + 16 * block * features,
        ),
        name="far",
    )(columns, near, f0, f1, f2)
    torso_grad = mine + lax.ppermute(theirs, "grp", SWAP)
    updated = (torso_weight.astype(jnp.float32) - 0.01 * torso_grad).astype(jnp.bfloat16)
    refreshed_weight = lax.all_to_all(updated, "tp", split_axis=0, concat_axis=1, tiled=True)
    return (torso_grad, refreshed_weight)


def solution(mesh):
    placed = (
        P("grp", "fsdp", None),
        P("fsdp"),
        P("grp", "fsdp"),
        P("grp", "fsdp", None),
        P("fsdp", None),
        P(),
        P(),
        P(("grp", "fsdp"), "tp"),
        P(None, "tp"),
        P(None, "tp"),
    )
    return jax.shard_map(
        shards,
        mesh=mesh,
        in_specs=placed,
        out_specs=(P(("grp", "fsdp"), "tp"), P(("grp", "fsdp", "tp"), None)),
        check_vma=False,
    )
```

```python
import jax
import jax.numpy as jnp
from jax import lax
from jax.experimental import pallas as pl
from jax.experimental.pallas import tpu as pltpu
from jax.sharding import PartitionSpec as P

ACTIONS = 18
COSINES = 64
FRACS = 64
X = 4
Y = 4
Z = 4


SWAP = [(0, 1), (1, 0)]


def z_from(step):
    return [(f, (f // Z) * Z + (f % Z - step) % Z) for f in range(Y * Z)]


def y_from(step):
    return [(f, (f - step * Z) % (Y * Z)) for f in range(Y * Z)]


def x_from(step):
    return [(t, (t - step * 2) % (X * 2)) for t in range(X * 2)]


def in_hbm(*arrays):
    return [pltpu.with_memory_space_constraint(array, pltpu.HBM) for array in arrays]


def multiply_chunks(where_ref, own_ref, got_ref, order, sources, total, rows_held, held, sems):
    y, z = where_ref[1], where_ref[2]
    rows = own_ref.shape[0]
    block = sources[0].shape[0]
    copies = []
    for step, (step_y, step_z) in enumerate(order):
        place = lax.rem(y + step_y, Y) * Z + lax.rem(z + step_z, Z)
        cols = pl.ds(pl.multiple_of(place * block, block), block)
        copies.append(
            (
                pltpu.make_async_copy(
                    own_ref.at[:, cols], rows_held.at[step, pl.ds(0, rows)], sems.at[0, step]
                ),
                pltpu.make_async_copy(
                    got_ref.at[:, cols], rows_held.at[step, pl.ds(rows, rows)], sems.at[1, step]
                ),
                pltpu.make_async_copy(sources[step], held.at[step], sems.at[2, step]),
            )
        )
        for copy in copies[-1]:
            copy.start()
    for step in range(len(order)):
        for copy in copies[step]:
            copy.wait()
        term = jnp.dot(rows_held[step], held[step], preferred_element_type=jnp.float32)
        if step == 0:
            total[...] = term
        else:
            total[...] += term


def early_kernel(where_ref, own_ref, got_ref, *refs):
    order = [(j, k) for j in (0, 1, 3) for k in range(Z)]
    multiply_chunks(where_ref, own_ref, got_ref, order, refs[: len(order)], *refs[len(order) :])


def late_kernel(where_ref, own_ref, got_ref, early_ref, *refs):
    order = [(2, k) for k in range(Z)]
    keep_ref, send_ref, total = refs[Z : Z + 3]
    multiply_chunks(where_ref, own_ref, got_ref, order, refs[:Z], total, *refs[Z + 3 :])
    group = where_ref[0]
    rows = own_ref.shape[0]
    half = rows // 2
    other = 1 - group
    for base, part in ((0, group), (rows, other)):
        out = pl.ds(pl.multiple_of(part * half, half), half)
        for half_of, out_ref in ((group, keep_ref), (other, send_ref)):
            source = pl.ds(pl.multiple_of(base + half_of * half, half), half)
            out_ref[out, :] = early_ref[source, :] + total[source, :]


def norm_kernel(where_ref, rows_ref, gain_ref, own_ref, send_ref):
    side = own_ref.shape[1]
    wide = rows_ref[...].astype(jnp.float32)
    scale = lax.rsqrt(jnp.mean(wide * wide, axis=-1, keepdims=True) + 1e-05)
    for part, out_ref in ((where_ref[0], own_ref), (1 - where_ref[0], send_ref)):
        cols = pl.ds(pl.multiple_of(part * side, side), side)
        values = rows_ref[:, cols].astype(jnp.float32)
        out_ref[...] = (values * scale * gain_ref[:, cols]).astype(jnp.bfloat16)


def pieces_kernel(where_ref, own_ref, got_ref, count_ref, out_ref, held, sems):
    places, _, block = out_ref.shape[1:]
    strip = held.shape[1]
    half = own_ref.shape[0] // 2

    def fetch(source):
        copies = []
        for k in range(2):
            row = pl.multiple_of(k * half + where_ref[3] * strip, strip)
            copies.append(
                pltpu.make_async_copy(source.at[pl.ds(row, strip), :], held.at[k], sems.at[k])
            )
            copies[-1].start()
        for copy in copies:
            copy.wait()

    @pl.when(where_ref[0] == 1)
    def _():
        fetch(own_ref)

    @pl.when(where_ref[0] == 0)
    def _():
        fetch(got_ref)

    for k in range(2):
        for place in range(places):
            out_ref[k, place, :strip] = held[k, :, place * block : (place + 1) * block]
            out_ref[k, place, strip:] = count_ref[...]


def columns_kernel(where_ref, own_ref, after_ref, before_ref, far_a_ref, far_b_ref, out_ref, held):
    group, y, z, x = where_ref[0], where_ref[1], where_ref[2], where_ref[3]
    other = 1 - group
    block = own_ref.shape[3]
    span = held.shape[0]
    strip = span // X

    def body(step, carry):
        place = lax.rem(y + step // Z, Y) * Z + lax.rem(z + lax.rem(step, Z), Z)
        for shift, ref in ((0, own_ref), (1, after_ref), (3, before_ref)):
            rows = pl.ds(pl.multiple_of(lax.rem(x + shift, X) * strip, strip), strip)
            held[rows, :block] = ref[group, place, :strip]
            held[rows, block:] = ref[other, place, :strip]
        rows = pl.ds(pl.multiple_of(lax.rem(x + 2, X) * strip, strip), strip)
        held[rows, pl.ds(pl.multiple_of(group * block, block), block)] = far_a_ref[place, :strip]
        held[rows, pl.ds(pl.multiple_of(other * block, block), block)] = far_b_ref[place, :strip]
        out_ref[:, pl.ds(pl.multiple_of(step * span, span), span)] = held[...].T
        return carry

    lax.fori_loop(0, Y * Z, body, 0)


def near_kernel(cols_ref, own_ref, line_ref, b0_ref, b1_ref, a0_ref, a1_ref, out_ref):
    half = own_ref.shape[0]
    span = Z * half
    total = None
    for base, first, rest in (
        (0, own_ref, line_ref),
        (span, b0_ref, b1_ref),
        (3 * span, a0_ref, a1_ref),
    ):
        grads = jnp.concatenate([first[...], rest[...]], 0)
        term = jnp.dot(
            cols_ref[:, base : base + span], grads, preferred_element_type=jnp.float32
        )
        total = term if total is None else total + term
    out_ref[...] = total


def far_kernel(cols_ref, near_ref, f0_ref, f1_ref, f2_ref, own_ref, other_ref):
    grads = jnp.concatenate([f0_ref[...], f1_ref[...], f2_ref[...]], 0)
    span = grads.shape[0]
    block = own_ref.shape[0]
    cols = cols_ref[:, 2 * span : 3 * span]
    total = near_ref[...] + jnp.dot(cols, grads, preferred_element_type=jnp.float32)
    own_ref[...] = total[:block]
    other_ref[...] = total[block:]


def shards(
    frames,
    rewards,
    actions,
    fractions,
    episode_shard,
    table,
    norm_gain,
    torso_weight,
    embed_weight,
    value_weight,
):
    group = lax.axis_index("grp")
    place = lax.axis_index("fsdp")
    x_place = lax.axis_index("tp") // 2
    shard_total = lax.axis_size("fsdp")
    where = jnp.stack([group, place // Z, place % Z, x_place]).astype(jnp.int32)
    rows_block = frames.shape[1]
    width = frames.shape[2]
    features = torso_weight.shape[1]
    half = rows_block // 2
    side = width // 2
    block = side // shard_total
    strip = half // X
    own_rows = group * half
    other_rows = (1 - group) * half
    smem = pl.BlockSpec(memory_space=pltpu.SMEM)
    vmem = pl.BlockSpec(memory_space=pltpu.VMEM)

    with jax.named_scope("rows_swap"):
        values = frames[0]
        tile = 64
        normed_own, normed_send = pl.pallas_call(
            norm_kernel,
            grid=(rows_block // tile,),
            out_shape=(jax.ShapeDtypeStruct((rows_block, side), jnp.bfloat16),) * 2,
            in_specs=[
                smem,
                pl.BlockSpec((tile, width), lambda i: (i, 0)),
                pl.BlockSpec((1, width), lambda i: (0, 0)),
            ],
            out_specs=(pl.BlockSpec((tile, side), lambda i: (i, 0)),) * 2,
            compiler_params=pltpu.CompilerParams(vmem_limit_bytes=12 << 20),
            cost_estimate=pl.CostEstimate(
                flops=6 * rows_block * width,
                transcendentals=0,
                bytes_accessed=4 * rows_block * width,
            ),
            name="norm",
        )(where, *in_hbm(values, norm_gain[None, :]))
    with jax.named_scope("weight_gather"):
        after_z = lax.ppermute(torso_weight, "fsdp", z_from(1))
        before_z = lax.ppermute(torso_weight, "fsdp", z_from(3))
        after_z, normed_send = lax.optimization_barrier((after_z, normed_send))
        lines = [torso_weight, after_z, lax.ppermute(after_z, "fsdp", z_from(1)), before_z]
        near = [
            (lax.ppermute(line, "fsdp", y_from(1)), lax.ppermute(line, "fsdp", y_from(3)))
            for line in lines
        ]
        near = lax.optimization_barrier(near)
        far = [
            lax.ppermute(above, "fsdp", y_from(3)) if k < 2 else lax.ppermute(below, "fsdp", y_from(1))
            for k, (below, above) in enumerate(near)
        ]

    with jax.named_scope("rows_swap"):
        normed_send, _ = lax.optimization_barrier((normed_send, near[0]))
        normed_got = lax.ppermute(normed_send, "grp", SWAP)
        ints = jnp.concatenate([fractions[0].T, actions[0][None, :]], 0)
        kept = lax.dynamic_slice_in_dim(ints, own_rows, half, 1)
        got = lax.ppermute(lax.dynamic_slice_in_dim(ints, other_rows, half, 1), "grp", SWAP)
        target_ints = jnp.where(group == 0, kept, got)
        online_ints = jnp.where(group == 0, got, kept)
        ints_all = jnp.concatenate([target_ints, online_ints], 1)
        fraction_rows = ints_all[:-1]
        action_rows = ints_all[-1]

    with jax.named_scope("columns_exchange"):

        lanes = jnp.arange(shard_total, dtype=jnp.int32)
        onehot = episode_shard[:, :1] == lanes[None, :]
        local_counts = jnp.sum(onehot.astype(jnp.float32), axis=0).astype(jnp.bfloat16)
        count_tile = jnp.pad(local_counts[None, :], ((0, 15), (0, block - shard_total)))
        count_tile, _ = lax.optimization_barrier(
            (count_tile, near)
        )
        pieces = pl.pallas_call(
            pieces_kernel,
            out_shape=jax.ShapeDtypeStruct((2, shard_total, strip + 16, block), jnp.bfloat16),
            in_specs=[smem] + [pl.BlockSpec(memory_space=pl.ANY)] * 2 + [vmem],
            out_specs=vmem,
            scratch_shapes=[
                pltpu.VMEM((2, strip, side), jnp.bfloat16),
                pltpu.SemaphoreType.DMA((2,)),
            ],
            compiler_params=pltpu.CompilerParams(vmem_limit_bytes=4 << 20),
            cost_estimate=pl.CostEstimate(
                flops=0, transcendentals=0, bytes_accessed=8 * strip * side
            ),
            name="pieces",
        )(where, normed_own, normed_got, count_tile)
        pieces = lax.all_to_all(
            pieces.reshape(2 * shard_total, strip + 16, block), ("grp", "fsdp"), 0, 0, tiled=True
        ).reshape(2, shard_total, strip + 16, block)
        counts = jnp.sum(pieces[0, :, strip, :shard_total].astype(jnp.float32), axis=0)

    with jax.named_scope("counts"):
        inverse = float(rows_block) / counts
        row_weight = jnp.sum(jnp.where(onehot, inverse[None, :], 0.0), axis=1)
        row_weight = lax.dynamic_slice_in_dim(row_weight, own_rows, half, 0)

    choose_mask = (action_rows[:, None] == jnp.arange(ACTIONS, dtype=jnp.int32)[None, :]).astype(
        jnp.bfloat16
    )
    picked = jnp.dot(choose_mask, value_weight, preferred_element_type=jnp.float32)
    cosine = jnp.cos(
        jnp.pi * jnp.arange(COSINES, dtype=jnp.float32)[None, :] * table[:, None]
    ).astype(jnp.bfloat16)
    embedding = jax.nn.relu(
        jnp.dot(cosine, embed_weight, preferred_element_type=jnp.float32)
    ).astype(jnp.bfloat16)
    ids = jnp.arange(FRACS, dtype=jnp.int32)
    online_fractions = fraction_rows[:, half:]
    online_select = online_fractions[:, None, :] == ids[None, :, None]
    levels = jnp.sum(jnp.where(online_select, table[None, :, None], 0.0), axis=1)
    reward_rows = lax.dynamic_slice_in_dim(rewards, own_rows, half, 0).astype(jnp.float32)

    any_space = pl.BlockSpec(memory_space=pl.ANY)

    def held(count):
        return [
            pltpu.VMEM((count, 2 * rows_block, block), jnp.bfloat16),
            pltpu.VMEM((count, block, features), jnp.bfloat16),
            pltpu.SemaphoreType.DMA((3, count)),
        ]

    def work(count):
        return pl.CostEstimate(
            flops=4 * count * rows_block * block * features,
            transcendentals=0,
            bytes_accessed=2 * count * block * (features + 2 * rows_block)
            + 8 * rows_block * features,
        )

    total_shape = jax.ShapeDtypeStruct((2 * rows_block, features), jnp.float32)
    part_shape = jax.ShapeDtypeStruct((rows_block, features), jnp.float32)
    near_chunks = lines + [pair[0] for pair in near] + [pair[1] for pair in near]
    early = pl.pallas_call(
        early_kernel,
        out_shape=total_shape,
        in_specs=[smem] + [any_space] * (2 + 3 * Z),
        out_specs=vmem,
        scratch_shapes=held(3 * Z),
        compiler_params=pltpu.CompilerParams(vmem_limit_bytes=12 << 20),
        cost_estimate=work(3 * Z),
        name="early",
    )(where, *in_hbm(normed_own, normed_got, *near_chunks))
    keep, send = pl.pallas_call(
        late_kernel,
        out_shape=(part_shape, part_shape),
        in_specs=[smem] + [any_space] * 2 + [vmem] + [any_space] * Z,
        out_specs=(vmem, vmem),
        scratch_shapes=[pltpu.VMEM((2 * rows_block, features), jnp.float32)] + held(Z),
        compiler_params=pltpu.CompilerParams(vmem_limit_bytes=8 << 20),
        cost_estimate=work(Z),
        name="late",
    )(where, *in_hbm(normed_own, normed_got), early, *far)
    preact = keep + lax.ppermute(send, "grp", SWAP)
    weighted = (jax.nn.silu(preact) * picked).astype(jnp.bfloat16)
    table_values = lax.dot_general(
        embedding, weighted, (((1,), (1,)), ((), ())), preferred_element_type=jnp.float32
    )
    partial_quant = jnp.sum(
        jnp.where(
            fraction_rows[:, None, :] == ids[None, :, None], table_values[None, :, :], 0.0
        ),
        axis=1,
    )
    with jax.named_scope("quant_sum"):
        quant = partial_quant
        for flip in (2, 4):
            quant = quant + lax.ppermute(quant, "tp", [(t, t ^ flip) for t in range(2 * X)])
        quant, pieces = lax.optimization_barrier((quant, pieces))
        quant = quant + lax.ppermute(quant, "tp", [(t, t ^ 1) for t in range(2 * X)])
    with jax.named_scope("columns_round_x"):
        after = lax.ppermute(pieces, "tp", x_from(1))
        before = lax.ppermute(pieces, "tp", x_from(3))
        far_a = lax.ppermute(after[0], "tp", x_from(1))
        far_b = lax.ppermute(before[1], "tp", x_from(3))
        columns = pl.pallas_call(
            columns_kernel,
            out_shape=jax.ShapeDtypeStruct((2 * block, shard_total * half), jnp.bfloat16),
            in_specs=[smem] + [vmem] * 5,
            out_specs=vmem,
            scratch_shapes=[pltpu.VMEM((half, 2 * block), jnp.bfloat16)],
            compiler_params=pltpu.CompilerParams(vmem_limit_bytes=8 << 20),
            cost_estimate=pl.CostEstimate(
                flops=0, transcendentals=0, bytes_accessed=8 * shard_total * half * block
            ),
            name="columns",
        )(where, pieces, after, before, far_a, far_b)
    target_quant = quant[:, :half]
    online_quant = quant[:, half:]
    target_value = reward_rows[None, :] + 0.99 * target_quant
    errors = target_value[None, :, :] - online_quant[:, None, :]
    weight = jnp.abs(levels[:, None, :] - (errors < 0).astype(jnp.float32))
    grad_quant = -row_weight[None, :] * jnp.sum(weight * jnp.clip(errors, -1.0, 1.0), axis=1)
    grad_table = jnp.sum(jnp.where(online_select, grad_quant[:, None, :], 0.0), axis=0)
    grad_feature = lax.dot_general(
        grad_table,
        embedding.astype(jnp.float32),
        (((0,), (0,)), ((), ())),
        precision=lax.Precision.HIGHEST,
    )
    online_preact = preact[half:]
    gate_value = jax.nn.sigmoid(online_preact)
    grad_preact = (
        grad_feature
        * picked[half:]
        * gate_value
        * (1.0 + online_preact * (1.0 - gate_value))
    ).astype(jnp.bfloat16)

    with jax.named_scope("grad_gather"):
        b0 = lax.ppermute(grad_preact, "fsdp", y_from(1))
        a0 = lax.ppermute(grad_preact, "fsdp", y_from(3))
        pieces_z = tuple(lax.ppermute(grad_preact, "fsdp", z_from(k)) for k in range(1, Z))
        pieces_z, _ = lax.optimization_barrier((pieces_z, (b0, a0)))
        line = jnp.concatenate(pieces_z, 0)
        f0 = lax.ppermute(a0, "fsdp", y_from(3))
        a1 = lax.ppermute(line, "fsdp", y_from(3))
        b1 = lax.ppermute(line, "fsdp", y_from(1))
        f1 = lax.ppermute(a1[:half], "fsdp", y_from(3))
        f2 = lax.ppermute(b1[half:], "fsdp", y_from(1))

    near = pl.pallas_call(
        near_kernel,
        out_shape=jax.ShapeDtypeStruct((2 * block, features), jnp.float32),
        in_specs=[vmem] * 7,
        out_specs=vmem,
        compiler_params=pltpu.CompilerParams(vmem_limit_bytes=12 << 20),
        cost_estimate=pl.CostEstimate(
            flops=12 * Z * half * 2 * block * features // 2,
            transcendentals=0,
            bytes_accessed=6 * Z * half * (2 * block + features),
        ),
        name="near",
    )(columns, grad_preact, line, b0, b1, a0, a1)
    final_shape = jax.ShapeDtypeStruct((block, features), jnp.float32)
    mine, theirs = pl.pallas_call(
        far_kernel,
        out_shape=(final_shape, final_shape),
        in_specs=[vmem] * 5,
        out_specs=(vmem, vmem),
        compiler_params=pltpu.CompilerParams(vmem_limit_bytes=12 << 20),
        cost_estimate=pl.CostEstimate(
            flops=4 * Z * half * block * features,
            transcendentals=0,
            bytes_accessed=2 * Z * half * (2 * block + features) + 16 * block * features,
        ),
        name="far",
    )(columns, near, f0, f1, f2)
    torso_grad = mine + lax.ppermute(theirs, "grp", SWAP)
    updated = (torso_weight.astype(jnp.float32) - 0.01 * torso_grad).astype(jnp.bfloat16)
    refreshed_weight = lax.all_to_all(updated, "tp", split_axis=0, concat_axis=1, tiled=True)
    return (torso_grad, refreshed_weight)


def solution(mesh):
    placed = (
        P("grp", "fsdp", None),
        P("fsdp"),
        P("grp", "fsdp"),
        P("grp", "fsdp", None),
        P("fsdp", None),
        P(),
        P(),
        P(("grp", "fsdp"), "tp"),
        P(None, "tp"),
        P(None, "tp"),
    )
    return jax.shard_map(
        shards,
        mesh=mesh,
        in_specs=placed,
        out_specs=(P(("grp", "fsdp"), "tp"), P(("grp", "fsdp", "tp"), None)),
        check_vma=False,
    )
```

```python
import jax
import jax.numpy as jnp
from jax import lax
from jax.experimental import pallas as pl
from jax.experimental.pallas import tpu as pltpu
from jax.sharding import PartitionSpec as P

ACTIONS = 18
COSINES = 64
FRACS = 64
X = 4
Y = 4
Z = 4


SWAP = [(0, 1), (1, 0)]


def z_from(step):
    return [(f, (f // Z) * Z + (f % Z - step) % Z) for f in range(Y * Z)]


def y_from(step):
    return [(f, (f - step * Z) % (Y * Z)) for f in range(Y * Z)]


def x_from(step):
    return [(t, (t - step * 2) % (X * 2)) for t in range(X * 2)]


def in_hbm(*arrays):
    return [pltpu.with_memory_space_constraint(array, pltpu.HBM) for array in arrays]


def multiply_chunks(where_ref, own_ref, got_ref, order, sources, total, rows_held, held, sems):
    y, z = where_ref[1], where_ref[2]
    rows = own_ref.shape[0]
    block = sources[0].shape[0]
    copies = []
    for step, (step_y, step_z) in enumerate(order):
        place = lax.rem(y + step_y, Y) * Z + lax.rem(z + step_z, Z)
        cols = pl.ds(pl.multiple_of(place * block, block), block)
        copies.append(
            (
                pltpu.make_async_copy(
                    own_ref.at[:, cols], rows_held.at[step, pl.ds(0, rows)], sems.at[0, step]
                ),
                pltpu.make_async_copy(
                    got_ref.at[:, cols], rows_held.at[step, pl.ds(rows, rows)], sems.at[1, step]
                ),
                pltpu.make_async_copy(sources[step], held.at[step], sems.at[2, step]),
            )
        )
        for copy in copies[-1]:
            copy.start()
    for step in range(len(order)):
        for copy in copies[step]:
            copy.wait()
        term = jnp.dot(rows_held[step], held[step], preferred_element_type=jnp.float32)
        if step == 0:
            total[...] = term
        else:
            total[...] += term


def early_kernel(where_ref, own_ref, got_ref, *refs):
    order = [(j, k) for j in (0, 1, 3) for k in range(Z)]
    multiply_chunks(where_ref, own_ref, got_ref, order, refs[: len(order)], *refs[len(order) :])


def late_kernel(where_ref, own_ref, got_ref, early_ref, *refs):
    order = [(2, k) for k in range(Z)]
    keep_ref, send_ref, total = refs[Z : Z + 3]
    multiply_chunks(where_ref, own_ref, got_ref, order, refs[:Z], total, *refs[Z + 3 :])
    group = where_ref[0]
    rows = own_ref.shape[0]
    half = rows // 2
    other = 1 - group
    for base, part in ((0, group), (rows, other)):
        out = pl.ds(pl.multiple_of(part * half, half), half)
        for half_of, out_ref in ((group, keep_ref), (other, send_ref)):
            source = pl.ds(pl.multiple_of(base + half_of * half, half), half)
            out_ref[out, :] = early_ref[source, :] + total[source, :]


def norm_kernel(where_ref, rows_ref, gain_ref, own_ref, send_ref):
    side = own_ref.shape[1]
    wide = rows_ref[...].astype(jnp.float32)
    scale = lax.rsqrt(jnp.mean(wide * wide, axis=-1, keepdims=True) + 1e-05)
    for part, out_ref in ((where_ref[0], own_ref), (1 - where_ref[0], send_ref)):
        cols = pl.ds(pl.multiple_of(part * side, side), side)
        values = rows_ref[:, cols].astype(jnp.float32)
        out_ref[...] = (values * scale * gain_ref[:, cols]).astype(jnp.bfloat16)


def pieces_kernel(where_ref, own_ref, got_ref, count_ref, out_ref, held, sems):
    places, _, block = out_ref.shape[1:]
    strip = held.shape[1]
    half = own_ref.shape[0] // 2

    def fetch(source):
        copies = []
        for k in range(2):
            row = pl.multiple_of(k * half + where_ref[3] * strip, strip)
            copies.append(
                pltpu.make_async_copy(source.at[pl.ds(row, strip), :], held.at[k], sems.at[k])
            )
            copies[-1].start()
        for copy in copies:
            copy.wait()

    @pl.when(where_ref[0] == 1)
    def _():
        fetch(own_ref)

    @pl.when(where_ref[0] == 0)
    def _():
        fetch(got_ref)

    for k in range(2):
        for place in range(places):
            out_ref[k, place, :strip] = held[k, :, place * block : (place + 1) * block]
            out_ref[k, place, strip:] = count_ref[...]


def columns_kernel(where_ref, own_ref, after_ref, before_ref, far_a_ref, far_b_ref, out_ref, held):
    group, y, z, x = where_ref[0], where_ref[1], where_ref[2], where_ref[3]
    other = 1 - group
    block = own_ref.shape[3]
    span = held.shape[0]
    strip = span // X

    def body(step, carry):
        place = lax.rem(y + step // Z, Y) * Z + lax.rem(z + lax.rem(step, Z), Z)
        for shift, ref in ((0, own_ref), (1, after_ref), (3, before_ref)):
            rows = pl.ds(pl.multiple_of(lax.rem(x + shift, X) * strip, strip), strip)
            held[rows, :block] = ref[group, place, :strip]
            held[rows, block:] = ref[other, place, :strip]
        rows = pl.ds(pl.multiple_of(lax.rem(x + 2, X) * strip, strip), strip)
        held[rows, pl.ds(pl.multiple_of(group * block, block), block)] = far_a_ref[place, :strip]
        held[rows, pl.ds(pl.multiple_of(other * block, block), block)] = far_b_ref[place, :strip]
        out_ref[:, pl.ds(pl.multiple_of(step * span, span), span)] = held[...].T
        return carry

    lax.fori_loop(0, Y * Z, body, 0)


def near_kernel(cols_ref, own_ref, line_ref, b0_ref, b1_ref, a0_ref, a1_ref, out_ref):
    half = own_ref.shape[0]
    span = Z * half
    total = None
    for base, first, rest in (
        (0, own_ref, line_ref),
        (span, b0_ref, b1_ref),
        (3 * span, a0_ref, a1_ref),
    ):
        grads = jnp.concatenate([first[...], rest[...]], 0)
        term = jnp.dot(
            cols_ref[:, base : base + span], grads, preferred_element_type=jnp.float32
        )
        total = term if total is None else total + term
    out_ref[...] = total


def far_kernel(cols_ref, near_ref, f0_ref, f1_ref, f2_ref, own_ref, other_ref):
    grads = jnp.concatenate([f0_ref[...], f1_ref[...], f2_ref[...]], 0)
    span = grads.shape[0]
    block = own_ref.shape[0]
    cols = cols_ref[:, 2 * span : 3 * span]
    total = near_ref[...] + jnp.dot(cols, grads, preferred_element_type=jnp.float32)
    own_ref[...] = total[:block]
    other_ref[...] = total[block:]


def shards(
    frames,
    rewards,
    actions,
    fractions,
    episode_shard,
    table,
    norm_gain,
    torso_weight,
    embed_weight,
    value_weight,
):
    group = lax.axis_index("grp")
    place = lax.axis_index("fsdp")
    x_place = lax.axis_index("tp") // 2
    shard_total = lax.axis_size("fsdp")
    where = jnp.stack([group, place // Z, place % Z, x_place]).astype(jnp.int32)
    rows_block = frames.shape[1]
    width = frames.shape[2]
    features = torso_weight.shape[1]
    half = rows_block // 2
    side = width // 2
    block = side // shard_total
    strip = half // X
    own_rows = group * half
    other_rows = (1 - group) * half
    smem = pl.BlockSpec(memory_space=pltpu.SMEM)
    vmem = pl.BlockSpec(memory_space=pltpu.VMEM)

    with jax.named_scope("rows_swap"):
        values = frames[0]
        tile = 64
        normed_own, normed_send = pl.pallas_call(
            norm_kernel,
            grid=(rows_block // tile,),
            out_shape=(jax.ShapeDtypeStruct((rows_block, side), jnp.bfloat16),) * 2,
            in_specs=[
                smem,
                pl.BlockSpec((tile, width), lambda i: (i, 0)),
                pl.BlockSpec((1, width), lambda i: (0, 0)),
            ],
            out_specs=(pl.BlockSpec((tile, side), lambda i: (i, 0)),) * 2,
            compiler_params=pltpu.CompilerParams(vmem_limit_bytes=12 << 20),
            cost_estimate=pl.CostEstimate(
                flops=6 * rows_block * width,
                transcendentals=0,
                bytes_accessed=4 * rows_block * width,
            ),
            name="norm",
        )(where, *in_hbm(values, norm_gain[None, :]))
    with jax.named_scope("weight_gather"):
        first = (
            lax.ppermute(torso_weight, "fsdp", z_from(1)),
            lax.ppermute(torso_weight, "fsdp", z_from(3)),
            lax.ppermute(torso_weight, "fsdp", y_from(1)),
            lax.ppermute(torso_weight, "fsdp", y_from(3)),
        )
        first, normed_send = lax.optimization_barrier((first, normed_send))
        after_z, before_z = first[:2]
        normed_got = lax.ppermute(normed_send, "grp", SWAP)
        twice_z = lax.ppermute(after_z, "fsdp", z_from(1))
        lines = [torso_weight, after_z, twice_z, before_z]
        near = [first[2:]] + [
            (lax.ppermute(line, "fsdp", y_from(1)), lax.ppermute(line, "fsdp", y_from(3)))
            for line in lines[1:]
        ]
        sent = list(near)
        near[2:], normed_got = lax.optimization_barrier((near[2:], normed_got))
        far = [
            lax.ppermute(above, "fsdp", y_from(3)) if k % 2 == 0 else lax.ppermute(below, "fsdp", y_from(1))
            for k, (below, above) in enumerate(near)
        ]

    with jax.named_scope("rows_swap"):
        ints = jnp.concatenate([fractions[0].T, actions[0][None, :]], 0)
        ints, _ = lax.optimization_barrier((ints, sent))
        kept = lax.dynamic_slice_in_dim(ints, own_rows, half, 1)
        got = lax.ppermute(lax.dynamic_slice_in_dim(ints, other_rows, half, 1), "grp", SWAP)
        target_ints = jnp.where(group == 0, kept, got)
        online_ints = jnp.where(group == 0, got, kept)
        ints_all = jnp.concatenate([target_ints, online_ints], 1)
        fraction_rows = ints_all[:-1]
        action_rows = ints_all[-1]

    with jax.named_scope("columns_exchange"):

        lanes = jnp.arange(shard_total, dtype=jnp.int32)
        onehot = episode_shard[:, :1] == lanes[None, :]
        local_counts = jnp.sum(onehot.astype(jnp.float32), axis=0).astype(jnp.bfloat16)
        count_tile = jnp.pad(local_counts[None, :], ((0, 15), (0, block - shard_total)))
        count_tile, _ = lax.optimization_barrier(
            (count_tile, got)
        )
        pieces = pl.pallas_call(
            pieces_kernel,
            out_shape=jax.ShapeDtypeStruct((2, shard_total, strip + 16, block), jnp.bfloat16),
            in_specs=[smem] + [pl.BlockSpec(memory_space=pl.ANY)] * 2 + [vmem],
            out_specs=vmem,
            scratch_shapes=[
                pltpu.VMEM((2, strip, side), jnp.bfloat16),
                pltpu.SemaphoreType.DMA((2,)),
            ],
            compiler_params=pltpu.CompilerParams(vmem_limit_bytes=4 << 20),
            cost_estimate=pl.CostEstimate(
                flops=0, transcendentals=0, bytes_accessed=8 * strip * side
            ),
            name="pieces",
        )(where, normed_own, normed_got, count_tile)
        pieces = lax.all_to_all(
            pieces.reshape(2 * shard_total, strip + 16, block), ("grp", "fsdp"), 0, 0, tiled=True
        ).reshape(2, shard_total, strip + 16, block)
        counts = jnp.sum(pieces[0, :, strip, :shard_total].astype(jnp.float32), axis=0)
        pieces = pieces[:, :, :strip]

    with jax.named_scope("counts"):
        inverse = float(rows_block) / counts
        row_weight = jnp.sum(jnp.where(onehot, inverse[None, :], 0.0), axis=1)
        row_weight = lax.dynamic_slice_in_dim(row_weight, own_rows, half, 0)

    choose_mask = (action_rows[:, None] == jnp.arange(ACTIONS, dtype=jnp.int32)[None, :]).astype(
        jnp.bfloat16
    )
    picked = jnp.dot(choose_mask, value_weight, preferred_element_type=jnp.float32)
    cosine = jnp.cos(
        jnp.pi * jnp.arange(COSINES, dtype=jnp.float32)[None, :] * table[:, None]
    ).astype(jnp.bfloat16)
    embedding = jax.nn.relu(
        jnp.dot(cosine, embed_weight, preferred_element_type=jnp.float32)
    ).astype(jnp.bfloat16)
    ids = jnp.arange(FRACS, dtype=jnp.int32)
    online_fractions = fraction_rows[:, half:]
    online_select = online_fractions[:, None, :] == ids[None, :, None]
    levels = jnp.sum(jnp.where(online_select, table[None, :, None], 0.0), axis=1)
    reward_rows = lax.dynamic_slice_in_dim(rewards, own_rows, half, 0).astype(jnp.float32)

    any_space = pl.BlockSpec(memory_space=pl.ANY)

    def held(count):
        return [
            pltpu.VMEM((count, 2 * rows_block, block), jnp.bfloat16),
            pltpu.VMEM((count, block, features), jnp.bfloat16),
            pltpu.SemaphoreType.DMA((3, count)),
        ]

    def work(count):
        return pl.CostEstimate(
            flops=4 * count * rows_block * block * features,
            transcendentals=0,
            bytes_accessed=2 * count * block * (features + 2 * rows_block)
            + 8 * rows_block * features,
        )

    total_shape = jax.ShapeDtypeStruct((2 * rows_block, features), jnp.float32)
    part_shape = jax.ShapeDtypeStruct((rows_block, features), jnp.float32)
    near_chunks = lines + [pair[0] for pair in near] + [pair[1] for pair in near]
    early = pl.pallas_call(
        early_kernel,
        out_shape=total_shape,
        in_specs=[smem] + [any_space] * (2 + 3 * Z),
        out_specs=vmem,
        scratch_shapes=held(3 * Z),
        compiler_params=pltpu.CompilerParams(vmem_limit_bytes=12 << 20),
        cost_estimate=work(3 * Z),
        name="early",
    )(where, *in_hbm(normed_own, normed_got, *near_chunks))
    early, pieces = lax.optimization_barrier((early, pieces))
    keep, send = pl.pallas_call(
        late_kernel,
        out_shape=(part_shape, part_shape),
        in_specs=[smem] + [any_space] * 2 + [vmem] + [any_space] * Z,
        out_specs=(vmem, vmem),
        scratch_shapes=[pltpu.VMEM((2 * rows_block, features), jnp.float32)] + held(Z),
        compiler_params=pltpu.CompilerParams(vmem_limit_bytes=8 << 20),
        cost_estimate=work(Z),
        name="late",
    )(where, *in_hbm(normed_own, normed_got), early, *far)
    preact = keep + lax.ppermute(send, "grp", SWAP)
    weighted = (jax.nn.silu(preact) * picked).astype(jnp.bfloat16)
    table_values = lax.dot_general(
        embedding, weighted, (((1,), (1,)), ((), ())), preferred_element_type=jnp.float32
    )
    partial_quant = jnp.sum(
        jnp.where(
            fraction_rows[:, None, :] == ids[None, :, None], table_values[None, :, :], 0.0
        ),
        axis=1,
    )
    with jax.named_scope("columns_round_x"):
        after = lax.ppermute(pieces, "tp", x_from(1))
        before = lax.ppermute(pieces, "tp", x_from(3))
        far_a = lax.ppermute(after[0], "tp", x_from(1))
        far_b = lax.ppermute(before[1], "tp", x_from(3))
        columns = pl.pallas_call(
            columns_kernel,
            out_shape=jax.ShapeDtypeStruct((2 * block, shard_total * half), jnp.bfloat16),
            in_specs=[smem] + [vmem] * 5,
            out_specs=vmem,
            scratch_shapes=[pltpu.VMEM((half, 2 * block), jnp.bfloat16)],
            compiler_params=pltpu.CompilerParams(vmem_limit_bytes=8 << 20),
            cost_estimate=pl.CostEstimate(
                flops=0, transcendentals=0, bytes_accessed=8 * shard_total * half * block
            ),
            name="columns",
        )(where, pieces, after, before, far_a, far_b)
    with jax.named_scope("quant_sum"):
        quant = partial_quant
        for flip in (1, 2, 4):
            quant = quant + lax.ppermute(quant, "tp", [(t, t ^ flip) for t in range(2 * X)])
    quant, _ = lax.optimization_barrier((quant, (far_a, far_b)))
    target_quant = quant[:, :half]
    online_quant = quant[:, half:]
    target_value = reward_rows[None, :] + 0.99 * target_quant
    errors = target_value[None, :, :] - online_quant[:, None, :]
    weight = jnp.abs(levels[:, None, :] - (errors < 0).astype(jnp.float32))
    grad_quant = -row_weight[None, :] * jnp.sum(weight * jnp.clip(errors, -1.0, 1.0), axis=1)
    grad_table = jnp.sum(jnp.where(online_select, grad_quant[:, None, :], 0.0), axis=0)
    grad_feature = lax.dot_general(
        grad_table,
        embedding.astype(jnp.float32),
        (((0,), (0,)), ((), ())),
        precision=lax.Precision.HIGHEST,
    )
    online_preact = preact[half:]
    gate_value = jax.nn.sigmoid(online_preact)
    grad_preact = (
        grad_feature
        * picked[half:]
        * gate_value
        * (1.0 + online_preact * (1.0 - gate_value))
    ).astype(jnp.bfloat16)

    with jax.named_scope("grad_gather"):
        b0 = lax.ppermute(grad_preact, "fsdp", y_from(1))
        a0 = lax.ppermute(grad_preact, "fsdp", y_from(3))
        pieces_z = tuple(lax.ppermute(grad_preact, "fsdp", z_from(k)) for k in range(1, Z))
        pieces_z, _ = lax.optimization_barrier((pieces_z, (b0, a0)))
        line = jnp.concatenate(pieces_z, 0)
        f0 = lax.ppermute(a0, "fsdp", y_from(3))
        a1 = lax.ppermute(line, "fsdp", y_from(3))
        b1 = lax.ppermute(line, "fsdp", y_from(1))
        f1 = lax.ppermute(a1[:half], "fsdp", y_from(3))
        f2 = lax.ppermute(b1[half:], "fsdp", y_from(1))

    near = pl.pallas_call(
        near_kernel,
        out_shape=jax.ShapeDtypeStruct((2 * block, features), jnp.float32),
        in_specs=[vmem] * 7,
        out_specs=vmem,
        compiler_params=pltpu.CompilerParams(vmem_limit_bytes=12 << 20),
        cost_estimate=pl.CostEstimate(
            flops=12 * Z * half * 2 * block * features // 2,
            transcendentals=0,
            bytes_accessed=6 * Z * half * (2 * block + features),
        ),
        name="near",
    )(columns, grad_preact, line, b0, b1, a0, a1)
    final_shape = jax.ShapeDtypeStruct((block, features), jnp.float32)
    mine, theirs = pl.pallas_call(
        far_kernel,
        out_shape=(final_shape, final_shape),
        in_specs=[vmem] * 5,
        out_specs=(vmem, vmem),
        compiler_params=pltpu.CompilerParams(vmem_limit_bytes=12 << 20),
        cost_estimate=pl.CostEstimate(
            flops=4 * Z * half * block * features,
            transcendentals=0,
            bytes_accessed=2 * Z * half * (2 * block + features) + 16 * block * features,
        ),
        name="far",
    )(columns, near, f0, f1, f2)
    torso_grad = mine + lax.ppermute(theirs, "grp", SWAP)
    updated = (torso_weight.astype(jnp.float32) - 0.01 * torso_grad).astype(jnp.bfloat16)
    refreshed_weight = lax.all_to_all(updated, "tp", split_axis=0, concat_axis=1, tiled=True)
    return (torso_grad, refreshed_weight)


def solution(mesh):
    placed = (
        P("grp", "fsdp", None),
        P("fsdp"),
        P("grp", "fsdp"),
        P("grp", "fsdp", None),
        P("fsdp", None),
        P(),
        P(),
        P(("grp", "fsdp"), "tp"),
        P(None, "tp"),
        P(None, "tp"),
    )
    return jax.shard_map(
        shards,
        mesh=mesh,
        in_specs=placed,
        out_specs=(P(("grp", "fsdp"), "tp"), P(("grp", "fsdp", "tp"), None)),
        check_vma=False,
    )
```

```python
import jax
import jax.numpy as jnp
from jax import lax
from jax.experimental import pallas as pl
from jax.experimental.pallas import tpu as pltpu
from jax.sharding import PartitionSpec as P

ACTIONS = 18
COSINES = 64
FRACS = 64
X = 4
Y = 4
Z = 4


SWAP = [(0, 1), (1, 0)]


def z_from(step):
    return [(f, (f // Z) * Z + (f % Z - step) % Z) for f in range(Y * Z)]


def y_from(step):
    return [(f, (f - step * Z) % (Y * Z)) for f in range(Y * Z)]


def x_from(step):
    return [(t, (t - step * 2) % (X * 2)) for t in range(X * 2)]


def in_hbm(*arrays):
    return [pltpu.with_memory_space_constraint(array, pltpu.HBM) for array in arrays]


def multiply_chunks(where_ref, own_ref, got_ref, order, sources, total, rows_held, held, sems):
    y, z = where_ref[1], where_ref[2]
    rows = own_ref.shape[0]
    block = sources[0].shape[0]
    copies = []
    for step, (step_y, step_z) in enumerate(order):
        place = lax.rem(y + step_y, Y) * Z + lax.rem(z + step_z, Z)
        cols = pl.ds(pl.multiple_of(place * block, block), block)
        copies.append(
            (
                pltpu.make_async_copy(
                    own_ref.at[:, cols], rows_held.at[step, pl.ds(0, rows)], sems.at[0, step]
                ),
                pltpu.make_async_copy(
                    got_ref.at[:, cols], rows_held.at[step, pl.ds(rows, rows)], sems.at[1, step]
                ),
                pltpu.make_async_copy(sources[step], held.at[step], sems.at[2, step]),
            )
        )
        for copy in copies[-1]:
            copy.start()
    for step in range(len(order)):
        for copy in copies[step]:
            copy.wait()
        term = jnp.dot(rows_held[step], held[step], preferred_element_type=jnp.float32)
        if step == 0:
            total[...] = term
        else:
            total[...] += term


def early_kernel(where_ref, own_ref, got_ref, *refs):
    order = [(j, k) for j in (0, 1, 3) for k in range(Z)]
    multiply_chunks(where_ref, own_ref, got_ref, order, refs[: len(order)], *refs[len(order) :])


def late_kernel(where_ref, own_ref, got_ref, early_ref, *refs):
    order = [(2, k) for k in range(Z)]
    keep_ref, send_ref, total = refs[Z : Z + 3]
    multiply_chunks(where_ref, own_ref, got_ref, order, refs[:Z], total, *refs[Z + 3 :])
    group = where_ref[0]
    rows = own_ref.shape[0]
    half = rows // 2
    other = 1 - group
    for base, part in ((0, group), (rows, other)):
        out = pl.ds(pl.multiple_of(part * half, half), half)
        for half_of, out_ref in ((group, keep_ref), (other, send_ref)):
            source = pl.ds(pl.multiple_of(base + half_of * half, half), half)
            out_ref[out, :] = early_ref[source, :] + total[source, :]


def norm_kernel(where_ref, rows_ref, gain_ref, own_ref, send_ref):
    side = own_ref.shape[1]
    wide = rows_ref[...].astype(jnp.float32)
    scale = lax.rsqrt(jnp.mean(wide * wide, axis=-1, keepdims=True) + 1e-05)
    for part, out_ref in ((where_ref[0], own_ref), (1 - where_ref[0], send_ref)):
        cols = pl.ds(pl.multiple_of(part * side, side), side)
        values = rows_ref[:, cols].astype(jnp.float32)
        out_ref[...] = (values * scale * gain_ref[:, cols]).astype(jnp.bfloat16)


def pieces_kernel(where_ref, own_ref, got_ref, count_ref, out_ref, held, sems):
    places, _, block = out_ref.shape[1:]
    strip = held.shape[1]
    half = own_ref.shape[0] // 2

    def fetch(source):
        copies = []
        for k in range(2):
            row = pl.multiple_of(k * half + where_ref[3] * strip, strip)
            copies.append(
                pltpu.make_async_copy(source.at[pl.ds(row, strip), :], held.at[k], sems.at[k])
            )
            copies[-1].start()
        for copy in copies:
            copy.wait()

    @pl.when(where_ref[0] == 1)
    def _():
        fetch(own_ref)

    @pl.when(where_ref[0] == 0)
    def _():
        fetch(got_ref)

    for k in range(2):
        for place in range(places):
            out_ref[k, place, :strip] = held[k, :, place * block : (place + 1) * block]
            out_ref[k, place, strip:] = count_ref[...]


def columns_kernel(where_ref, own_ref, after_ref, before_ref, far_a_ref, far_b_ref, out_ref, held):
    group, y, z, x = where_ref[0], where_ref[1], where_ref[2], where_ref[3]
    other = 1 - group
    block = own_ref.shape[3]
    span = held.shape[0]
    strip = span // X

    def body(step, carry):
        place = lax.rem(y + step // Z, Y) * Z + lax.rem(z + lax.rem(step, Z), Z)
        for shift, ref in ((0, own_ref), (1, after_ref), (3, before_ref)):
            rows = pl.ds(pl.multiple_of(lax.rem(x + shift, X) * strip, strip), strip)
            held[rows, :block] = ref[group, place, :strip]
            held[rows, block:] = ref[other, place, :strip]
        rows = pl.ds(pl.multiple_of(lax.rem(x + 2, X) * strip, strip), strip)
        held[rows, pl.ds(pl.multiple_of(group * block, block), block)] = far_a_ref[place, :strip]
        held[rows, pl.ds(pl.multiple_of(other * block, block), block)] = far_b_ref[place, :strip]
        out_ref[:, pl.ds(pl.multiple_of(step * span, span), span)] = held[...].T
        return carry

    lax.fori_loop(0, Y * Z, body, 0)


def near_kernel(cols_ref, own_ref, line_ref, b0_ref, b1_ref, a0_ref, a1_ref, out_ref):
    half = own_ref.shape[0]
    span = Z * half
    total = None
    for base, first, rest in (
        (0, own_ref, line_ref),
        (span, b0_ref, b1_ref),
        (3 * span, a0_ref, a1_ref),
    ):
        grads = jnp.concatenate([first[...], rest[...]], 0)
        term = jnp.dot(
            cols_ref[:, base : base + span], grads, preferred_element_type=jnp.float32
        )
        total = term if total is None else total + term
    out_ref[...] = total


def far_kernel(cols_ref, near_ref, f0_ref, f1_ref, f2_ref, own_ref, other_ref):
    grads = jnp.concatenate([f0_ref[...], f1_ref[...], f2_ref[...]], 0)
    span = grads.shape[0]
    block = own_ref.shape[0]
    cols = cols_ref[:, 2 * span : 3 * span]
    total = near_ref[...] + jnp.dot(cols, grads, preferred_element_type=jnp.float32)
    own_ref[...] = total[:block]
    other_ref[...] = total[block:]


def shards(
    frames,
    rewards,
    actions,
    fractions,
    episode_shard,
    table,
    norm_gain,
    torso_weight,
    embed_weight,
    value_weight,
):
    group = lax.axis_index("grp")
    place = lax.axis_index("fsdp")
    x_place = lax.axis_index("tp") // 2
    shard_total = lax.axis_size("fsdp")
    where = jnp.stack([group, place // Z, place % Z, x_place]).astype(jnp.int32)
    rows_block = frames.shape[1]
    width = frames.shape[2]
    features = torso_weight.shape[1]
    half = rows_block // 2
    side = width // 2
    block = side // shard_total
    strip = half // X
    own_rows = group * half
    other_rows = (1 - group) * half
    smem = pl.BlockSpec(memory_space=pltpu.SMEM)
    vmem = pl.BlockSpec(memory_space=pltpu.VMEM)

    with jax.named_scope("rows_swap"):
        values = frames[0]
        tile = 64
        normed_own, normed_send = pl.pallas_call(
            norm_kernel,
            grid=(rows_block // tile,),
            out_shape=(jax.ShapeDtypeStruct((rows_block, side), jnp.bfloat16),) * 2,
            in_specs=[
                smem,
                pl.BlockSpec((tile, width), lambda i: (i, 0)),
                pl.BlockSpec((1, width), lambda i: (0, 0)),
            ],
            out_specs=(pl.BlockSpec((tile, side), lambda i: (i, 0)),) * 2,
            compiler_params=pltpu.CompilerParams(vmem_limit_bytes=12 << 20),
            cost_estimate=pl.CostEstimate(
                flops=6 * rows_block * width,
                transcendentals=0,
                bytes_accessed=4 * rows_block * width,
            ),
            name="norm",
        )(where, *in_hbm(values, norm_gain[None, :]))
    with jax.named_scope("weight_gather"):
        after_z = lax.ppermute(torso_weight, "fsdp", z_from(1))
        before_z = lax.ppermute(torso_weight, "fsdp", z_from(3))
        after_z, normed_send = lax.optimization_barrier((after_z, normed_send))
        lines = [torso_weight, after_z, lax.ppermute(after_z, "fsdp", z_from(1)), before_z]
        near = [
            (lax.ppermute(line, "fsdp", y_from(1)), lax.ppermute(line, "fsdp", y_from(3)))
            for line in lines
        ]
        near = lax.optimization_barrier(near)
        far = [
            lax.ppermute(above, "fsdp", y_from(3)) if k < 2 else lax.ppermute(below, "fsdp", y_from(1))
            for k, (below, above) in enumerate(near)
        ]

    with jax.named_scope("rows_swap"):
        normed_send, _ = lax.optimization_barrier((normed_send, near[0]))
        normed_got = lax.ppermute(normed_send, "grp", SWAP)
        ints = jnp.concatenate([fractions[0].T, actions[0][None, :]], 0)
        kept = lax.dynamic_slice_in_dim(ints, own_rows, half, 1)
        got = lax.ppermute(lax.dynamic_slice_in_dim(ints, other_rows, half, 1), "grp", SWAP)
        target_ints = jnp.where(group == 0, kept, got)
        online_ints = jnp.where(group == 0, got, kept)
        ints_all = jnp.concatenate([target_ints, online_ints], 1)
        fraction_rows = ints_all[:-1]
        action_rows = ints_all[-1]

    with jax.named_scope("columns_exchange"):

        lanes = jnp.arange(shard_total, dtype=jnp.int32)
        onehot = episode_shard[:, :1] == lanes[None, :]
        local_counts = jnp.sum(onehot.astype(jnp.float32), axis=0).astype(jnp.bfloat16)
        count_tile = jnp.pad(local_counts[None, :], ((0, 15), (0, block - shard_total)))
        count_tile, _ = lax.optimization_barrier(
            (count_tile, near)
        )
        pieces = pl.pallas_call(
            pieces_kernel,
            out_shape=jax.ShapeDtypeStruct((2, shard_total, strip + 16, block), jnp.bfloat16),
            in_specs=[smem] + [pl.BlockSpec(memory_space=pl.ANY)] * 2 + [vmem],
            out_specs=vmem,
            scratch_shapes=[
                pltpu.VMEM((2, strip, side), jnp.bfloat16),
                pltpu.SemaphoreType.DMA((2,)),
            ],
            compiler_params=pltpu.CompilerParams(vmem_limit_bytes=4 << 20),
            cost_estimate=pl.CostEstimate(
                flops=0, transcendentals=0, bytes_accessed=8 * strip * side
            ),
            name="pieces",
        )(where, normed_own, normed_got, count_tile)
        pieces = lax.all_to_all(
            pieces.reshape(2 * shard_total, strip + 16, block), ("grp", "fsdp"), 0, 0, tiled=True
        ).reshape(2, shard_total, strip + 16, block)
        counts = jnp.sum(pieces[0, :, strip, :shard_total].astype(jnp.float32), axis=0)

    with jax.named_scope("counts"):
        inverse = float(rows_block) / counts
        row_weight = jnp.sum(jnp.where(onehot, inverse[None, :], 0.0), axis=1)
        row_weight = lax.dynamic_slice_in_dim(row_weight, own_rows, half, 0)

    choose_mask = (action_rows[:, None] == jnp.arange(ACTIONS, dtype=jnp.int32)[None, :]).astype(
        jnp.bfloat16
    )
    picked = jnp.dot(choose_mask, value_weight, preferred_element_type=jnp.float32)
    cosine = jnp.cos(
        jnp.pi * jnp.arange(COSINES, dtype=jnp.float32)[None, :] * table[:, None]
    ).astype(jnp.bfloat16)
    embedding = jax.nn.relu(
        jnp.dot(cosine, embed_weight, preferred_element_type=jnp.float32)
    ).astype(jnp.bfloat16)
    ids = jnp.arange(FRACS, dtype=jnp.int32)
    online_fractions = fraction_rows[:, half:]
    online_select = online_fractions[:, None, :] == ids[None, :, None]
    levels = jnp.sum(jnp.where(online_select, table[None, :, None], 0.0), axis=1)
    reward_rows = lax.dynamic_slice_in_dim(rewards, own_rows, half, 0).astype(jnp.float32)

    any_space = pl.BlockSpec(memory_space=pl.ANY)

    def held(count):
        return [
            pltpu.VMEM((count, 2 * rows_block, block), jnp.bfloat16),
            pltpu.VMEM((count, block, features), jnp.bfloat16),
            pltpu.SemaphoreType.DMA((3, count)),
        ]

    def work(count):
        return pl.CostEstimate(
            flops=4 * count * rows_block * block * features,
            transcendentals=0,
            bytes_accessed=2 * count * block * (features + 2 * rows_block)
            + 8 * rows_block * features,
        )

    total_shape = jax.ShapeDtypeStruct((2 * rows_block, features), jnp.float32)
    part_shape = jax.ShapeDtypeStruct((rows_block, features), jnp.float32)
    near_chunks = lines + [pair[0] for pair in near] + [pair[1] for pair in near]
    early = pl.pallas_call(
        early_kernel,
        out_shape=total_shape,
        in_specs=[smem] + [any_space] * (2 + 3 * Z),
        out_specs=vmem,
        scratch_shapes=held(3 * Z),
        compiler_params=pltpu.CompilerParams(vmem_limit_bytes=12 << 20),
        cost_estimate=work(3 * Z),
        name="early",
    )(where, *in_hbm(normed_own, normed_got, *near_chunks))
    keep, send = pl.pallas_call(
        late_kernel,
        out_shape=(part_shape, part_shape),
        in_specs=[smem] + [any_space] * 2 + [vmem] + [any_space] * Z,
        out_specs=(vmem, vmem),
        scratch_shapes=[pltpu.VMEM((2 * rows_block, features), jnp.float32)] + held(Z),
        compiler_params=pltpu.CompilerParams(vmem_limit_bytes=8 << 20),
        cost_estimate=work(Z),
        name="late",
    )(where, *in_hbm(normed_own, normed_got), early, *far)
    preact = keep + lax.ppermute(send, "grp", SWAP)
    weighted = (jax.nn.silu(preact) * picked).astype(jnp.bfloat16)
    table_values = lax.dot_general(
        embedding, weighted, (((1,), (1,)), ((), ())), preferred_element_type=jnp.float32
    )
    partial_quant = jnp.sum(
        jnp.where(
            fraction_rows[:, None, :] == ids[None, :, None], table_values[None, :, :], 0.0
        ),
        axis=1,
    )
    with jax.named_scope("quant_sum"):
        quant = partial_quant
        for flip in (2, 4):
            quant = quant + lax.ppermute(quant, "tp", [(t, t ^ flip) for t in range(2 * X)])
        quant, pieces = lax.optimization_barrier((quant, pieces))
        quant = quant + lax.ppermute(quant, "tp", [(t, t ^ 1) for t in range(2 * X)])
    with jax.named_scope("columns_round_x"):
        after = lax.ppermute(pieces, "tp", x_from(1))
        before = lax.ppermute(pieces, "tp", x_from(3))
        far_a = lax.ppermute(after[0], "tp", x_from(1))
        far_b = lax.ppermute(before[1], "tp", x_from(3))
        columns = pl.pallas_call(
            columns_kernel,
            out_shape=jax.ShapeDtypeStruct((2 * block, shard_total * half), jnp.bfloat16),
            in_specs=[smem] + [vmem] * 5,
            out_specs=vmem,
            scratch_shapes=[pltpu.VMEM((half, 2 * block), jnp.bfloat16)],
            compiler_params=pltpu.CompilerParams(vmem_limit_bytes=8 << 20),
            cost_estimate=pl.CostEstimate(
                flops=0, transcendentals=0, bytes_accessed=8 * shard_total * half * block
            ),
            name="columns",
        )(where, pieces, after, before, far_a, far_b)
    target_quant = quant[:, :half]
    online_quant = quant[:, half:]
    target_value = reward_rows[None, :] + 0.99 * target_quant
    errors = target_value[None, :, :] - online_quant[:, None, :]
    weight = jnp.abs(levels[:, None, :] - (errors < 0).astype(jnp.float32))
    grad_quant = -row_weight[None, :] * jnp.sum(weight * jnp.clip(errors, -1.0, 1.0), axis=1)
    grad_table = jnp.sum(jnp.where(online_select, grad_quant[:, None, :], 0.0), axis=0)
    grad_feature = lax.dot_general(
        grad_table,
        embedding.astype(jnp.float32),
        (((0,), (0,)), ((), ())),
        precision=lax.Precision.HIGHEST,
    )
    online_preact = preact[half:]
    gate_value = jax.nn.sigmoid(online_preact)
    grad_preact = (
        grad_feature
        * picked[half:]
        * gate_value
        * (1.0 + online_preact * (1.0 - gate_value))
    ).astype(jnp.bfloat16)

    with jax.named_scope("grad_gather"):
        b0 = lax.ppermute(grad_preact, "fsdp", y_from(1))
        a0 = lax.ppermute(grad_preact, "fsdp", y_from(3))
        pieces_z = tuple(lax.ppermute(grad_preact, "fsdp", z_from(k)) for k in range(1, Z))
        pieces_z, _ = lax.optimization_barrier((pieces_z, b0))
        line = jnp.concatenate(pieces_z, 0)
        f0 = lax.ppermute(a0, "fsdp", y_from(3))
        a1 = lax.ppermute(line, "fsdp", y_from(3))
        b1 = lax.ppermute(line, "fsdp", y_from(1))
        f1 = lax.ppermute(a1[:half], "fsdp", y_from(3))
        f2 = lax.ppermute(b1[half:], "fsdp", y_from(1))

    near = pl.pallas_call(
        near_kernel,
        out_shape=jax.ShapeDtypeStruct((2 * block, features), jnp.float32),
        in_specs=[vmem] * 7,
        out_specs=vmem,
        compiler_params=pltpu.CompilerParams(vmem_limit_bytes=12 << 20),
        cost_estimate=pl.CostEstimate(
            flops=12 * Z * half * 2 * block * features // 2,
            transcendentals=0,
            bytes_accessed=6 * Z * half * (2 * block + features),
        ),
        name="near",
    )(columns, grad_preact, line, b0, b1, a0, a1)
    final_shape = jax.ShapeDtypeStruct((block, features), jnp.float32)
    mine, theirs = pl.pallas_call(
        far_kernel,
        out_shape=(final_shape, final_shape),
        in_specs=[vmem] * 5,
        out_specs=(vmem, vmem),
        compiler_params=pltpu.CompilerParams(vmem_limit_bytes=12 << 20),
        cost_estimate=pl.CostEstimate(
            flops=4 * Z * half * block * features,
            transcendentals=0,
            bytes_accessed=2 * Z * half * (2 * block + features) + 16 * block * features,
        ),
        name="far",
    )(columns, near, f0, f1, f2)
    torso_grad = mine + lax.ppermute(theirs, "grp", SWAP)
    updated = (torso_weight.astype(jnp.float32) - 0.01 * torso_grad).astype(jnp.bfloat16)
    refreshed_weight = lax.all_to_all(updated, "tp", split_axis=0, concat_axis=1, tiled=True)
    return (torso_grad, refreshed_weight)


def solution(mesh):
    placed = (
        P("grp", "fsdp", None),
        P("fsdp"),
        P("grp", "fsdp"),
        P("grp", "fsdp", None),
        P("fsdp", None),
        P(),
        P(),
        P(("grp", "fsdp"), "tp"),
        P(None, "tp"),
        P(None, "tp"),
    )
    return jax.shard_map(
        shards,
        mesh=mesh,
        in_specs=placed,
        out_specs=(P(("grp", "fsdp"), "tp"), P(("grp", "fsdp", "tp"), None)),
        check_vma=False,
    )
```

```python
import jax
import jax.numpy as jnp
from jax import lax
from jax.experimental import pallas as pl
from jax.experimental.pallas import tpu as pltpu
from jax.sharding import PartitionSpec as P

ACTIONS = 18
COSINES = 64
FRACS = 64
X = 4
Y = 4
Z = 4


SWAP = [(0, 1), (1, 0)]


def z_from(step):
    return [(f, (f // Z) * Z + (f % Z - step) % Z) for f in range(Y * Z)]


def y_from(step):
    return [(f, (f - step * Z) % (Y * Z)) for f in range(Y * Z)]


def x_from(step):
    return [(t, (t - step * 2) % (X * 2)) for t in range(X * 2)]


def in_hbm(*arrays):
    return [pltpu.with_memory_space_constraint(array, pltpu.HBM) for array in arrays]


def multiply_chunks(where_ref, own_ref, got_ref, order, sources, total, rows_held, held, sems):
    y, z = where_ref[1], where_ref[2]
    rows = own_ref.shape[0]
    block = sources[0].shape[0]
    copies = []
    for step, (step_y, step_z) in enumerate(order):
        place = lax.rem(y + step_y, Y) * Z + lax.rem(z + step_z, Z)
        cols = pl.ds(pl.multiple_of(place * block, block), block)
        copies.append(
            (
                pltpu.make_async_copy(
                    own_ref.at[:, cols], rows_held.at[step, pl.ds(0, rows)], sems.at[0, step]
                ),
                pltpu.make_async_copy(
                    got_ref.at[:, cols], rows_held.at[step, pl.ds(rows, rows)], sems.at[1, step]
                ),
                pltpu.make_async_copy(sources[step], held.at[step], sems.at[2, step]),
            )
        )
        for copy in copies[-1]:
            copy.start()
    for step in range(len(order)):
        for copy in copies[step]:
            copy.wait()
        term = jnp.dot(rows_held[step], held[step], preferred_element_type=jnp.float32)
        if step == 0:
            total[...] = term
        else:
            total[...] += term


def early_kernel(where_ref, own_ref, got_ref, *refs):
    order = [(j, k) for j in (0, 1, 3) for k in range(Z)]
    multiply_chunks(where_ref, own_ref, got_ref, order, refs[: len(order)], *refs[len(order) :])


def late_kernel(where_ref, own_ref, got_ref, early_ref, *refs):
    order = [(2, k) for k in range(Z)]
    keep_ref, send_ref, total = refs[Z : Z + 3]
    multiply_chunks(where_ref, own_ref, got_ref, order, refs[:Z], total, *refs[Z + 3 :])
    group = where_ref[0]
    rows = own_ref.shape[0]
    half = rows // 2
    other = 1 - group
    for base, part in ((0, group), (rows, other)):
        out = pl.ds(pl.multiple_of(part * half, half), half)
        for half_of, out_ref in ((group, keep_ref), (other, send_ref)):
            source = pl.ds(pl.multiple_of(base + half_of * half, half), half)
            out_ref[out, :] = early_ref[source, :] + total[source, :]


def norm_kernel(where_ref, rows_ref, gain_ref, own_ref, send_ref):
    side = own_ref.shape[1]
    wide = rows_ref[...].astype(jnp.float32)
    scale = lax.rsqrt(jnp.mean(wide * wide, axis=-1, keepdims=True) + 1e-05)
    for part, out_ref in ((where_ref[0], own_ref), (1 - where_ref[0], send_ref)):
        cols = pl.ds(pl.multiple_of(part * side, side), side)
        values = rows_ref[:, cols].astype(jnp.float32)
        out_ref[...] = (values * scale * gain_ref[:, cols]).astype(jnp.bfloat16)


def pieces_kernel(where_ref, own_ref, got_ref, count_ref, out_ref, held, sems):
    places, _, block = out_ref.shape[1:]
    strip = held.shape[1]
    half = own_ref.shape[0] // 2

    def fetch(source):
        copies = []
        for k in range(2):
            row = pl.multiple_of(k * half + where_ref[3] * strip, strip)
            copies.append(
                pltpu.make_async_copy(source.at[pl.ds(row, strip), :], held.at[k], sems.at[k])
            )
            copies[-1].start()
        for copy in copies:
            copy.wait()

    @pl.when(where_ref[0] == 1)
    def _():
        fetch(own_ref)

    @pl.when(where_ref[0] == 0)
    def _():
        fetch(got_ref)

    for k in range(2):
        for place in range(places):
            out_ref[k, place, :strip] = held[k, :, place * block : (place + 1) * block]
            out_ref[k, place, strip:] = count_ref[...]


def columns_kernel(where_ref, own_ref, after_ref, before_ref, far_a_ref, far_b_ref, out_ref, held):
    group, y, z, x = where_ref[0], where_ref[1], where_ref[2], where_ref[3]
    other = 1 - group
    block = own_ref.shape[3]
    span = held.shape[0]
    strip = span // X

    def body(step, carry):
        place = lax.rem(y + step // Z, Y) * Z + lax.rem(z + lax.rem(step, Z), Z)
        for shift, ref in ((0, own_ref), (1, after_ref), (3, before_ref)):
            rows = pl.ds(pl.multiple_of(lax.rem(x + shift, X) * strip, strip), strip)
            held[rows, :block] = ref[group, place, :strip]
            held[rows, block:] = ref[other, place, :strip]
        rows = pl.ds(pl.multiple_of(lax.rem(x + 2, X) * strip, strip), strip)
        held[rows, pl.ds(pl.multiple_of(group * block, block), block)] = far_a_ref[place, :strip]
        held[rows, pl.ds(pl.multiple_of(other * block, block), block)] = far_b_ref[place, :strip]
        out_ref[:, pl.ds(pl.multiple_of(step * span, span), span)] = held[...].T
        return carry

    lax.fori_loop(0, Y * Z, body, 0)


def near_kernel(cols_ref, own_ref, line_ref, b0_ref, b1_ref, a0_ref, a1_ref, out_ref):
    half = own_ref.shape[0]
    span = Z * half
    total = None
    for base, first, rest in (
        (0, own_ref, line_ref),
        (span, b0_ref, b1_ref),
        (3 * span, a0_ref, a1_ref),
    ):
        grads = jnp.concatenate([first[...], rest[...]], 0)
        term = jnp.dot(
            cols_ref[:, base : base + span], grads, preferred_element_type=jnp.float32
        )
        total = term if total is None else total + term
    out_ref[...] = total


def far_kernel(cols_ref, near_ref, f0_ref, f1_ref, f2_ref, own_ref, other_ref):
    grads = jnp.concatenate([f0_ref[...], f1_ref[...], f2_ref[...]], 0)
    span = grads.shape[0]
    block = own_ref.shape[0]
    cols = cols_ref[:, 2 * span : 3 * span]
    total = near_ref[...] + jnp.dot(cols, grads, preferred_element_type=jnp.float32)
    own_ref[...] = total[:block]
    other_ref[...] = total[block:]


def shards(
    frames,
    rewards,
    actions,
    fractions,
    episode_shard,
    table,
    norm_gain,
    torso_weight,
    embed_weight,
    value_weight,
):
    group = lax.axis_index("grp")
    place = lax.axis_index("fsdp")
    x_place = lax.axis_index("tp") // 2
    shard_total = lax.axis_size("fsdp")
    where = jnp.stack([group, place // Z, place % Z, x_place]).astype(jnp.int32)
    rows_block = frames.shape[1]
    width = frames.shape[2]
    features = torso_weight.shape[1]
    half = rows_block // 2
    side = width // 2
    block = side // shard_total
    strip = half // X
    own_rows = group * half
    other_rows = (1 - group) * half
    smem = pl.BlockSpec(memory_space=pltpu.SMEM)
    vmem = pl.BlockSpec(memory_space=pltpu.VMEM)

    with jax.named_scope("rows_swap"):
        values = frames[0]
        tile = 64
        normed_own, normed_send = pl.pallas_call(
            norm_kernel,
            grid=(rows_block // tile,),
            out_shape=(jax.ShapeDtypeStruct((rows_block, side), jnp.bfloat16),) * 2,
            in_specs=[
                smem,
                pl.BlockSpec((tile, width), lambda i: (i, 0)),
                pl.BlockSpec((1, width), lambda i: (0, 0)),
            ],
            out_specs=(pl.BlockSpec((tile, side), lambda i: (i, 0)),) * 2,
            compiler_params=pltpu.CompilerParams(vmem_limit_bytes=12 << 20),
            cost_estimate=pl.CostEstimate(
                flops=6 * rows_block * width,
                transcendentals=0,
                bytes_accessed=4 * rows_block * width,
            ),
            name="norm",
        )(where, *in_hbm(values, norm_gain[None, :]))
    with jax.named_scope("weight_gather"):
        after_z = lax.ppermute(torso_weight, "fsdp", z_from(1))
        before_z = lax.ppermute(torso_weight, "fsdp", z_from(3))
        after_z, normed_send = lax.optimization_barrier((after_z, normed_send))
        lines = [torso_weight, after_z, lax.ppermute(after_z, "fsdp", z_from(1)), before_z]
        near = [
            (lax.ppermute(line, "fsdp", y_from(1)), lax.ppermute(line, "fsdp", y_from(3)))
            for line in lines
        ]
        near = lax.optimization_barrier(near)
        far = [
            lax.ppermute(above, "fsdp", y_from(3)) if k < 2 else lax.ppermute(below, "fsdp", y_from(1))
            for k, (below, above) in enumerate(near)
        ]

    with jax.named_scope("rows_swap"):
        normed_send, _ = lax.optimization_barrier((normed_send, near[0]))
        normed_got = lax.ppermute(normed_send, "grp", SWAP)
        ints = jnp.concatenate([fractions[0].T, actions[0][None, :]], 0)
        kept = lax.dynamic_slice_in_dim(ints, own_rows, half, 1)
        got = lax.ppermute(lax.dynamic_slice_in_dim(ints, other_rows, half, 1), "grp", SWAP)
        target_ints = jnp.where(group == 0, kept, got)
        online_ints = jnp.where(group == 0, got, kept)
        ints_all = jnp.concatenate([target_ints, online_ints], 1)
        fraction_rows = ints_all[:-1]
        action_rows = ints_all[-1]

    with jax.named_scope("columns_exchange"):

        lanes = jnp.arange(shard_total, dtype=jnp.int32)
        onehot = episode_shard[:, :1] == lanes[None, :]
        local_counts = jnp.sum(onehot.astype(jnp.float32), axis=0).astype(jnp.bfloat16)
        count_tile = jnp.pad(local_counts[None, :], ((0, 15), (0, block - shard_total)))
        count_tile, _ = lax.optimization_barrier(
            (count_tile, near)
        )
        pieces = pl.pallas_call(
            pieces_kernel,
            out_shape=jax.ShapeDtypeStruct((2, shard_total, strip + 16, block), jnp.bfloat16),
            in_specs=[smem] + [pl.BlockSpec(memory_space=pl.ANY)] * 2 + [vmem],
            out_specs=vmem,
            scratch_shapes=[
                pltpu.VMEM((2, strip, side), jnp.bfloat16),
                pltpu.SemaphoreType.DMA((2,)),
            ],
            compiler_params=pltpu.CompilerParams(vmem_limit_bytes=4 << 20),
            cost_estimate=pl.CostEstimate(
                flops=0, transcendentals=0, bytes_accessed=8 * strip * side
            ),
            name="pieces",
        )(where, normed_own, normed_got, count_tile)
        pieces = lax.all_to_all(
            pieces.reshape(2 * shard_total, strip + 16, block), ("grp", "fsdp"), 0, 0, tiled=True
        ).reshape(2, shard_total, strip + 16, block)
        counts = jnp.sum(pieces[0, :, strip, :shard_total].astype(jnp.float32), axis=0)

    with jax.named_scope("counts"):
        inverse = float(rows_block) / counts
        row_weight = jnp.sum(jnp.where(onehot, inverse[None, :], 0.0), axis=1)
        row_weight = lax.dynamic_slice_in_dim(row_weight, own_rows, half, 0)

    choose_mask = (action_rows[:, None] == jnp.arange(ACTIONS, dtype=jnp.int32)[None, :]).astype(
        jnp.bfloat16
    )
    picked = jnp.dot(choose_mask, value_weight, preferred_element_type=jnp.float32)
    cosine = jnp.cos(
        jnp.pi * jnp.arange(COSINES, dtype=jnp.float32)[None, :] * table[:, None]
    ).astype(jnp.bfloat16)
    embedding = jax.nn.relu(
        jnp.dot(cosine, embed_weight, preferred_element_type=jnp.float32)
    ).astype(jnp.bfloat16)
    ids = jnp.arange(FRACS, dtype=jnp.int32)
    online_fractions = fraction_rows[:, half:]
    online_select = online_fractions[:, None, :] == ids[None, :, None]
    levels = jnp.sum(jnp.where(online_select, table[None, :, None], 0.0), axis=1)
    reward_rows = lax.dynamic_slice_in_dim(rewards, own_rows, half, 0).astype(jnp.float32)

    any_space = pl.BlockSpec(memory_space=pl.ANY)

    def held(count):
        return [
            pltpu.VMEM((count, 2 * rows_block, block), jnp.bfloat16),
            pltpu.VMEM((count, block, features), jnp.bfloat16),
            pltpu.SemaphoreType.DMA((3, count)),
        ]

    def work(count):
        return pl.CostEstimate(
            flops=4 * count * rows_block * block * features,
            transcendentals=0,
            bytes_accessed=2 * count * block * (features + 2 * rows_block)
            + 8 * rows_block * features,
        )

    total_shape = jax.ShapeDtypeStruct((2 * rows_block, features), jnp.float32)
    part_shape = jax.ShapeDtypeStruct((rows_block, features), jnp.float32)
    near_chunks = lines + [pair[0] for pair in near] + [pair[1] for pair in near]
    early = pl.pallas_call(
        early_kernel,
        out_shape=total_shape,
        in_specs=[smem] + [any_space] * (2 + 3 * Z),
        out_specs=vmem,
        scratch_shapes=held(3 * Z),
        compiler_params=pltpu.CompilerParams(vmem_limit_bytes=12 << 20),
        cost_estimate=work(3 * Z),
        name="early",
    )(where, *in_hbm(normed_own, normed_got, *near_chunks))
    keep, send = pl.pallas_call(
        late_kernel,
        out_shape=(part_shape, part_shape),
        in_specs=[smem] + [any_space] * 2 + [vmem] + [any_space] * Z,
        out_specs=(vmem, vmem),
        scratch_shapes=[pltpu.VMEM((2 * rows_block, features), jnp.float32)] + held(Z),
        compiler_params=pltpu.CompilerParams(vmem_limit_bytes=8 << 20),
        cost_estimate=work(Z),
        name="late",
    )(where, *in_hbm(normed_own, normed_got), early, *far)
    preact = keep + lax.ppermute(send, "grp", SWAP)
    weighted = (jax.nn.silu(preact) * picked).astype(jnp.bfloat16)
    table_values = lax.dot_general(
        embedding, weighted, (((1,), (1,)), ((), ())), preferred_element_type=jnp.float32
    )
    partial_quant = jnp.sum(
        jnp.where(
            fraction_rows[:, None, :] == ids[None, :, None], table_values[None, :, :], 0.0
        ),
        axis=1,
    )
    with jax.named_scope("quant_sum"):
        quant = partial_quant
        for flip in (2, 4):
            quant = quant + lax.ppermute(quant, "tp", [(t, t ^ flip) for t in range(2 * X)])
        quant, pieces = lax.optimization_barrier((quant, pieces))
        quant = quant + lax.ppermute(quant, "tp", [(t, t ^ 1) for t in range(2 * X)])
    with jax.named_scope("columns_round_x"):
        after = lax.ppermute(pieces, "tp", x_from(1))
        before = lax.ppermute(pieces, "tp", x_from(3))
        far_a = lax.ppermute(after[0], "tp", x_from(1))
        far_b = lax.ppermute(before[1], "tp", x_from(3))
        columns = pl.pallas_call(
            columns_kernel,
            out_shape=jax.ShapeDtypeStruct((2 * block, shard_total * half), jnp.bfloat16),
            in_specs=[smem] + [vmem] * 5,
            out_specs=vmem,
            scratch_shapes=[pltpu.VMEM((half, 2 * block), jnp.bfloat16)],
            compiler_params=pltpu.CompilerParams(vmem_limit_bytes=8 << 20),
            cost_estimate=pl.CostEstimate(
                flops=0, transcendentals=0, bytes_accessed=8 * shard_total * half * block
            ),
            name="columns",
        )(where, pieces, after, before, far_a, far_b)
    target_quant = quant[:, :half]
    online_quant = quant[:, half:]
    target_value = reward_rows[None, :] + 0.99 * target_quant
    errors = target_value[None, :, :] - online_quant[:, None, :]
    weight = jnp.abs(levels[:, None, :] - (errors < 0).astype(jnp.float32))
    grad_quant = -row_weight[None, :] * jnp.sum(weight * jnp.clip(errors, -1.0, 1.0), axis=1)
    grad_table = jnp.sum(jnp.where(online_select, grad_quant[:, None, :], 0.0), axis=0)
    grad_feature = lax.dot_general(
        grad_table,
        embedding.astype(jnp.float32),
        (((0,), (0,)), ((), ())),
        precision=lax.Precision.HIGHEST,
    )
    online_preact = preact[half:]
    gate_value = jax.nn.sigmoid(online_preact)
    grad_preact = (
        grad_feature
        * picked[half:]
        * gate_value
        * (1.0 + online_preact * (1.0 - gate_value))
    ).astype(jnp.bfloat16)

    with jax.named_scope("grad_gather"):
        b0 = lax.ppermute(grad_preact, "fsdp", y_from(1))
        a0 = lax.ppermute(grad_preact, "fsdp", y_from(3))
        after_g = lax.ppermute(grad_preact, "fsdp", z_from(1))
        before_g = lax.ppermute(grad_preact, "fsdp", z_from(3))
        pieces_z = (after_g, lax.ppermute(after_g, "fsdp", z_from(1)), before_g)
        pieces_z, _ = lax.optimization_barrier((pieces_z, (b0, a0)))
        line = jnp.concatenate(pieces_z, 0)
        f0 = lax.ppermute(a0, "fsdp", y_from(3))
        a1 = lax.ppermute(line, "fsdp", y_from(3))
        b1 = lax.ppermute(line, "fsdp", y_from(1))
        f1 = lax.ppermute(a1[:half], "fsdp", y_from(3))
        f2 = lax.ppermute(b1[half:], "fsdp", y_from(1))

    near = pl.pallas_call(
        near_kernel,
        out_shape=jax.ShapeDtypeStruct((2 * block, features), jnp.float32),
        in_specs=[vmem] * 7,
        out_specs=vmem,
        compiler_params=pltpu.CompilerParams(vmem_limit_bytes=12 << 20),
        cost_estimate=pl.CostEstimate(
            flops=12 * Z * half * 2 * block * features // 2,
            transcendentals=0,
            bytes_accessed=6 * Z * half * (2 * block + features),
        ),
        name="near",
    )(columns, grad_preact, line, b0, b1, a0, a1)
    final_shape = jax.ShapeDtypeStruct((block, features), jnp.float32)
    mine, theirs = pl.pallas_call(
        far_kernel,
        out_shape=(final_shape, final_shape),
        in_specs=[vmem] * 5,
        out_specs=(vmem, vmem),
        compiler_params=pltpu.CompilerParams(vmem_limit_bytes=12 << 20),
        cost_estimate=pl.CostEstimate(
            flops=4 * Z * half * block * features,
            transcendentals=0,
            bytes_accessed=2 * Z * half * (2 * block + features) + 16 * block * features,
        ),
        name="far",
    )(columns, near, f0, f1, f2)
    torso_grad = mine + lax.ppermute(theirs, "grp", SWAP)
    updated = (torso_weight.astype(jnp.float32) - 0.01 * torso_grad).astype(jnp.bfloat16)
    refreshed_weight = lax.all_to_all(updated, "tp", split_axis=0, concat_axis=1, tiled=True)
    return (torso_grad, refreshed_weight)


def solution(mesh):
    placed = (
        P("grp", "fsdp", None),
        P("fsdp"),
        P("grp", "fsdp"),
        P("grp", "fsdp", None),
        P("fsdp", None),
        P(),
        P(),
        P(("grp", "fsdp"), "tp"),
        P(None, "tp"),
        P(None, "tp"),
    )
    return jax.shard_map(
        shards,
        mesh=mesh,
        in_specs=placed,
        out_specs=(P(("grp", "fsdp"), "tp"), P(("grp", "fsdp", "tp"), None)),
        check_vma=False,
    )
```
